32 devices in a mesh: groups: 2 (over y), blk: 4 (over z), oct: 2 (over x), sub: 2 (over core).
Axes of the slice: x: 2, y: 2, z: 4, core: 2. Of those that a mesh axis runs over, the one named last changes fastest.
Arguments:
- positions: float32 [3, 65536], P(None, ('groups', 'blk', 'oct', 'sub')), parts along dimension 1, may hold values from 0 to 320
- polarizability: float32 [65536], P(('groups', 'blk', 'oct', 'sub')), parts along dimension 0, may hold values from 0.5 to 1.5
- permanent_field: float32 [3, 65536], P(None, ('groups', 'blk', 'oct', 'sub')), parts along dimension 1, may hold values from -40 to 40
- group_id: int32 [65536], P(('groups', 'blk', 'oct', 'sub')), parts along dimension 0, may hold values from 0 to 10921, never falling along the last dimension, each value on 1 to 6 neighbouring positions
- pair_mask: int32 [512, 9], P(('groups', 'blk', 'oct', 'sub')), parts along dimension 0, may hold values from 0 to 1, as said below
Outputs:
- dipoles: float32 [3, 65536], P(None, ('groups', 'blk', 'oct', 'sub')), parts along dimension 1
- residual: float32 [3, 65536], P(None, ('groups', 'blk', 'oct', 'sub')), parts along dimension 1
The draws below stay inside these ranges and needn't reach their ends.
There are 2 independent parts, one for each index of `groups`. The reference program is written for one: setup_inputs(seed, part) draws one part's arguments, and reference() takes and returns one part's arrays. A program takes and returns all parts, laid end to end along the dimension named above; each array names one. Nothing has to cross between parts.
Inputs may be any that keep to these rules, and one draw needn't show every extreme that they name: `group_id`: never falls from one atom to the next; each value names 1 to 6 consecutive atoms. pair_mask[b, 4] = 1, and pair_mask[b, 4 + o] = pair_mask[(b + o) mod 256, 4 - o].
All inputs are finite; a program needn't handle non-finite values.
Results may differ from the reference program's by a relative error of at most 0.0003.
Values sent between devices are 32-bit elements; how exact they have to be, the bound alone decides.
No kernel may reach another device: no remote copies, remote signals or barrier semaphores. Data moves between devices by JAX's collectives and lax.ppermute only.
A program may use at most 64 MiB of HBM per device.

```python
import math
import jax
import jax.numpy as jnp
import numpy as np
from jax import lax

ATOM_DEV = 2048
BOXES_DEV = 2
BLOCK = 128
REACH = 4
ORDER = 5
NODE_PAD = 128
ITERS = 2
ATOMS = 32768
BLOCKS = 256
BOXES = 32


def draw_positions(key, part):
    index = jnp.arange(ATOMS, dtype=jnp.int32)
    layer = (index // 256).astype(jnp.float32)
    column = (index % 16).astype(jnp.float32)
    row = (index // 16 % 16).astype(jnp.float32)
    jitter = jax.random.uniform(key, (3, ATOMS), jnp.float32, -0.35, 0.35)
    return jnp.stack([2.0 * (column + 0.5 + jitter[0]), 2.0 * (row + 0.5 + jitter[1]), 2.5 * (layer + 0.5 + jitter[2])])


def draw_permanent_field(key, part):
    first, second = jax.random.split(key)
    fraction = jnp.arange(ATOMS, dtype=jnp.float32) / (ATOMS - 1)
    spread = jnp.exp(jax.random.uniform(first, (ATOMS,), jnp.float32, math.log(0.5), math.log(2.0)))
    lean = jnp.array([0.0, 0.0, 1.0], jnp.float32)[:, None]
    base = jnp.clip(jax.random.normal(second, (3, ATOMS), jnp.float32), -4.0, 4.0)
    return 3.0 ** fraction * spread * (base + 0.5 * lean)


def draw_pair_mask(key, part):
    ahead = (jax.random.randint(key, (BLOCKS, REACH), 0, 4) > 0).astype(jnp.int32)
    blocks = jnp.arange(BLOCKS, dtype=jnp.int32)
    farthest = jnp.where(blocks % 4 == 0, 1, ahead[:, REACH - 1])
    ahead = jnp.concatenate([ahead[:, :REACH - 1], farthest[:, None]], axis=1)
    behind = [jnp.roll(ahead[:, offset - 1], offset) for offset in range(REACH, 0, -1)]
    forward = [ahead[:, offset - 1] for offset in range(1, REACH + 1)]
    columns = behind + [jnp.ones((BLOCKS,), jnp.int32)] + forward
    return jnp.stack(columns, axis=1).astype(jnp.int32)


def block_levels(key, extent, cuts, low, high):
    def one(axis_at, parts):
        steps = jax.random.uniform(jax.random.fold_in(jax.random.fold_in(key, 6), axis_at), (parts,), jnp.float32, low / len(cuts), high / len(cuts))
        return jnp.repeat(jnp.exp(steps), extent[axis_at] // parts).reshape((-1,) + (1,) * (len(extent) - axis_at - 1))

    factor_of = one(*cuts[0])
    for cut in cuts[1:]:
        factor_of = factor_of * one(*cut)
    return factor_of


def profile(amount, total, most, skew):
    loads = [(1 << 20) // math.isqrt(standing ** skew) + 1 for standing in range(2, amount + 1)]
    surplus, given = total - most - (amount - 1), [1] * (amount - 1)
    while surplus > 0:
        movable = [i for i in range(amount - 1) if given[i] < most]
        whole, remaining = sum([loads[i] for i in movable]), surplus
        for i in movable:
            extra = min(most - given[i], max(1, remaining * loads[i] // whole), surplus)
            given[i] = given[i] + extra
            surplus = surplus - extra
    return np.array([most] + given)


def ragged_sizes(stream_key, count, total, most, skew):
    if count == 2:
        one = jax.random.randint(stream_key, (), max(1, total - most), min(most, total - 1) + 1)
        return jnp.stack([one, total - one])
    sizes = jnp.asarray(profile(count, total, most, skew), jnp.int32)
    pairs = (count - 1) // 2
    source_of, receiver = sizes[1:1 + 2 * pairs:2], sizes[2:2 + 2 * pairs:2]
    room = jnp.minimum(source_of - 1, most - receiver)
    moved = jax.random.randint(jax.random.fold_in(stream_key, 1), (pairs,), 0, 1 << 20) % (room + 1)
    sizes = sizes.at[1:1 + 2 * pairs:2].set(source_of - moved).at[2:2 + 2 * pairs:2].set(receiver + moved)
    return sizes[jax.random.permutation(jax.random.fold_in(stream_key, 2), count)]


def setup_inputs(seed: int = 0, part: int = 0) -> dict:
    key_of = jax.random.split(jax.random.key(seed), 6)
    part_keys = jax.random.split(jax.random.fold_in(key_of[5], part), 6)
    positions = draw_positions(jax.random.fold_in(jax.random.fold_in(key_of[5], part), 71), part)
    polarizability = jnp.clip(jnp.exp(math.log(1.5) - 1.0986123 * jax.random.uniform(part_keys[1], (ATOMS,), jnp.float32) ** block_levels(part_keys[1], (ATOMS,), ((0, 16),), -0.2, 0.2)), 0.5, 1.5)
    permanent_field = draw_permanent_field(jax.random.fold_in(jax.random.fold_in(key_of[5], part), 71), part)
    group_id = jnp.searchsorted(jnp.cumsum(ragged_sizes(part_keys[3], ATOMS // 3, ATOMS, 6, 0)), jnp.arange(ATOMS), side="right").astype(jnp.int32)
    pair_mask = draw_pair_mask(jax.random.fold_in(jax.random.fold_in(key_of[5], part), 71), part)
    return dict(positions=positions, polarizability=polarizability, permanent_field=permanent_field, group_id=group_id, pair_mask=pair_mask)


side_length = 32.0
layer_gap = 2.5
thole_damp = 0.39
highest = lax.Precision.HIGHEST

def wrap_image(delta, period):
    return delta - period * jnp.floor(delta / period + 0.5)

def near_tiles(target, source, moments, keep_tile, length_z):
    delta_x = wrap_image(target[0][:, :, None] - source[0][:, None, :], side_length)
    delta_y = wrap_image(target[1][:, :, None] - source[1][:, None, :], side_length)
    delta_z = wrap_image(target[2][:, :, None] - source[2][:, None, :], length_z)
    keep = (keep_tile[:, None, None] > 0.5) & (target[4][:, :, None] != source[4][:, None, :])
    dist_sq = jnp.where(keep, delta_x * delta_x + delta_y * delta_y + delta_z * delta_z, 1.0)
    inv_three = lax.rsqrt(dist_sq) / dist_sq
    scaled = thole_damp * dist_sq * jnp.sqrt(dist_sq) * lax.rsqrt(target[3][:, :, None] * source[3][:, None, :])
    lam_three = -jnp.expm1(-scaled)
    lam_five = lam_three - scaled * jnp.exp(-scaled)
    coef_five = jnp.where(keep, 3.0 * lam_five * inv_three / dist_sq, 0.0)
    coef_three = jnp.where(keep, lam_three * inv_three, 0.0)
    along = delta_x * moments[0][:, None, :] + delta_y * moments[1][:, None, :] + delta_z * moments[2][:, None, :]
    weighted = coef_five * along
    field_x = lax.optimization_barrier(jnp.sum(weighted * delta_x - coef_three * moments[0][:, None, :], axis=2))
    field_y = lax.optimization_barrier(jnp.sum(weighted * delta_y - coef_three * moments[1][:, None, :], axis=2))
    field_z = lax.optimization_barrier(jnp.sum(weighted * delta_z - coef_three * moments[2][:, None, :], axis=2))
    return jnp.stack([field_x, field_y, field_z])

def near_total(static_ext, dipole_ext, mask_rows, length_z, atom_count):
    reach = (mask_rows.shape[1] - 1) // 2
    width = reach * BLOCK
    blocks = atom_count // BLOCK
    target = static_ext[:, width:width + atom_count].reshape(5, blocks, BLOCK)
    total = jnp.zeros((3, blocks, BLOCK), static_ext.dtype)
    for offset in range(-reach, reach + 1):
        begin = (reach + offset) * BLOCK
        source = static_ext[:, begin:begin + atom_count].reshape(5, blocks, BLOCK)
        moments = dipole_ext[:, begin:begin + atom_count].reshape(3, blocks, BLOCK)
        keep_tile = mask_rows[:, reach + offset].astype(static_ext.dtype)
        total = total + near_tiles(target, source, moments, keep_tile, length_z)
    return total.reshape(3, atom_count)

def node_tables():
    count = ORDER
    roots = np.cos((2.0 * np.arange(count) + 1.0) * np.pi / (2.0 * count))
    degree = np.arange(count)
    coeff = 2.0 / count * np.cos(np.outer(2.0 * np.arange(count) + 1.0, degree) * np.pi / (2.0 * count))
    coeff = np.where(degree[None, :] == 0, 1.0 / count, coeff)
    index = np.arange(NODE_PAD)
    live = index < count ** 3
    safe = np.where(live, index, 0)
    first = safe // (count * count)
    second = safe // count % count
    third = safe % count
    levels = np.arange(count)[None, :]
    pick_a = (first[:, None] == levels) * live[:, None] * 1.0
    pick_b = (second[:, None] == levels) * 1.0
    pick_c = (third[:, None] == levels) * 1.0
    node_x = 16.0 * (1.0 + roots[first])
    node_y = 16.0 * (1.0 + roots[second])
    node_t = roots[third]
    tables = [coeff, pick_a, pick_b, pick_c, node_x, node_y, node_t]
    return [jnp.asarray(item, jnp.float32) for item in tables]

def interpolation(coords, box_ids, box_height):
    coeff, pick_a, pick_b, pick_c, node_x, node_y, node_t = node_tables()
    scaled_x = coords[0] / 16.0 - 1.0
    scaled_y = coords[1] / 16.0 - 1.0
    scaled_z = 2.0 * (coords[2] - box_ids.astype(coords.dtype)[:, None] * box_height) / box_height - 1.0

    def basis(values, picks):
        terms = [jnp.ones_like(values), values]
        for degree in range(2, ORDER):
            terms.append(2.0 * values * terms[-1] - terms[-2])
        stacked = jnp.stack(terms[:ORDER])
        smooth = jnp.einsum('kn,nba->kba', coeff, stacked, precision=highest)
        return jnp.einsum('pk,kba->pba', picks, smooth, precision=highest)
    return basis(scaled_x, pick_a) * basis(scaled_y, pick_b) * basis(scaled_z, pick_c)

def far_block(target_ids, source_ids, weights, slabs, box_height, length_z):
    coeff, pick_a, pick_b, pick_c, node_x, node_y, node_t = node_tables()
    height_t = target_ids.astype(weights.dtype)[:, None] * box_height + 0.5 * box_height * (1.0 + node_t)[None, :]
    height_s = source_ids.astype(weights.dtype)[:, None] * box_height + 0.5 * box_height * (1.0 + node_t)[None, :]
    delta_x = wrap_image(node_x[:, None] - node_x[None, :], side_length)[None, :, None, :]
    delta_y = wrap_image(node_y[:, None] - node_y[None, :], side_length)[None, :, None, :]
    delta_z = wrap_image(height_t[:, :, None, None] - height_s[None, None, :, :], length_z)
    apart = jnp.abs(target_ids[:, None] // BOXES_DEV - source_ids[None, :] // BOXES_DEV)
    apart = jnp.minimum(apart, slabs - apart)
    keep = (apart >= 1)[:, None, :, None]
    dist_sq = jnp.where(keep, delta_x * delta_x + delta_y * delta_y + delta_z * delta_z + box_height * box_height, 1.0)
    inv_three = lax.rsqrt(dist_sq) / dist_sq
    coef_five = jnp.where(keep, 3.0 * inv_three / dist_sq, 0.0)
    coef_three = jnp.where(keep, inv_three, 0.0)
    weight_x = weights[:, 0, :][None, None]
    weight_y = weights[:, 1, :][None, None]
    weight_z = weights[:, 2, :][None, None]
    weighted = coef_five * (delta_x * weight_x + delta_y * weight_y + delta_z * weight_z)
    field_x = lax.optimization_barrier(jnp.sum(weighted * delta_x - coef_three * weight_x, axis=(2, 3)))
    field_y = lax.optimization_barrier(jnp.sum(weighted * delta_y - coef_three * weight_y, axis=(2, 3)))
    field_z = lax.optimization_barrier(jnp.sum(weighted * delta_z - coef_three * weight_z, axis=(2, 3)))
    return jnp.stack([field_x, field_y, field_z], axis=1)

def reference(positions, polarizability, permanent_field, group_id, pair_mask):
    atom_count = positions.shape[1]
    slabs = atom_count // ATOM_DEV
    length_z = layer_gap * atom_count / 256.0
    box_height = length_z / BOXES
    per_box = atom_count // BOXES
    width = REACH * BLOCK
    rows_dev = ATOM_DEV // BLOCK
    static = jnp.concatenate([positions, polarizability[None, :], group_id.astype(positions.dtype)[None, :]], axis=0)
    static_ext = jnp.concatenate([static[:, atom_count - width:], static, static[:, :width]], axis=1)
    all_boxes = jnp.arange(BOXES, dtype=jnp.int32)
    interp = interpolation(positions.reshape(3, BOXES, per_box), all_boxes, box_height)
    surface = 4.0 * math.pi / 3.0 / (side_length * side_length * length_z)

    def induced(dipoles):
        dipole_ext = jnp.concatenate([dipoles[:, atom_count - width:], dipoles, dipoles[:, :width]], axis=1)

        def near_slab(index):
            begin = (index * ATOM_DEV).astype(jnp.int32)
            part_static = lax.dynamic_slice_in_dim(static_ext, begin, ATOM_DEV + 2 * width, 1)
            part_dipole = lax.dynamic_slice_in_dim(dipole_ext, begin, ATOM_DEV + 2 * width, 1)
            part_mask = lax.dynamic_slice_in_dim(pair_mask, (index * rows_dev).astype(jnp.int32), rows_dev, 0)
            return near_total(part_static, part_dipole, part_mask, length_z, ATOM_DEV)
        near = lax.map(near_slab, jnp.arange(slabs, dtype=jnp.int32))
        near = jnp.transpose(near, (1, 0, 2)).reshape(3, atom_count)
        weights = jnp.einsum('pba,cba->bcp', interp, dipoles.reshape(3, BOXES, per_box), precision=highest)

        def far_box(target):
            return far_block(target[None], all_boxes, weights, slabs, box_height, length_z)[0]
        node_field = lax.map(far_box, all_boxes)
        far = jnp.einsum('pba,bcp->cba', interp, node_field, precision=highest).reshape(3, atom_count)
        total = lax.optimization_barrier(jnp.sum(dipoles, axis=1))
        return near + far - surface * total[:, None]
    dipoles = polarizability[None, :] * permanent_field
    residual = induced(dipoles)
    precond = polarizability[None, :] * residual
    norm_now = jnp.sum(residual * precond)
    direction = precond
    for step in range(ITERS):
        image = direction / polarizability[None, :] - induced(direction)
        rate = norm_now / jnp.sum(direction * image)
        dipoles = dipoles + rate * direction
        residual = residual - rate * image
        if step + 1 < ITERS:
            precond = polarizability[None, :] * residual
            norm_next = jnp.sum(residual * precond)
            direction = precond + norm_next / norm_now * direction
            norm_now = norm_next
    return (dipoles, residual)
```

```python
import functools
import math

import jax
import jax.numpy as jnp
import numpy as np
from jax import lax
from jax.experimental import pallas as pl
from jax.experimental.pallas import tpu as pltpu
from jax.sharding import PartitionSpec as P

BOXES_DEV = 2
BLOCK = 128
ORDER = 5
NODE_PAD = 128
ITERS = 2
SUB = 8
CHUNK = 32

side_length = 32.0
layer_gap = 2.5
thole_damp = 0.39
highest = lax.Precision.HIGHEST
f32 = jnp.float32
RING = ("blk", "oct", "sub")

VM = pl.BlockSpec(memory_space=pltpu.VMEM)
SM = pl.BlockSpec(memory_space=pltpu.SMEM)
TABLE_LIMIT = 16 << 20


def call(body, outs, args, smem=0, scratch=(), limit=None, cost=None, pinned=()):
    shapes = [
        pltpu.VMEM(shape, f32) if at in pinned else jax.ShapeDtypeStruct(shape, f32)
        for at, shape in enumerate(outs)
    ]
    return list(pl.pallas_call(
        body,
        out_shape=shapes,
        in_specs=[SM] * smem + [VM] * (len(args) - smem),
        out_specs=[VM] * len(outs),
        scratch_shapes=[pltpu.VMEM(shape, f32) for shape in scratch],
        compiler_params=pltpu.CompilerParams(vmem_limit_bytes=limit or (6 << 20)),
        cost_estimate=cost,
    )(*args))


def node_tables():
    count = ORDER
    roots = np.cos((2.0 * np.arange(count) + 1.0) * np.pi / (2.0 * count))
    degree = np.arange(count)
    coeff = (
        2.0 / count * np.cos(np.outer(2.0 * np.arange(count) + 1.0, degree) * np.pi / (2.0 * count))
    )
    coeff = np.where(degree[None, :] == 0, 1.0 / count, coeff)
    index = np.arange(NODE_PAD)
    live = index < count**3
    safe = np.where(live, index, 0)
    levels = np.stack([safe // (count * count), safe // count % count, safe % count])
    picks = (levels[:, :, None] == np.arange(8)) * 1.0
    picks[0] *= live[:, None]
    nodes = np.zeros((8, NODE_PAD))
    nodes[0] = 0.5 * (1.0 + roots[levels[0]])
    nodes[1] = 0.5 * (1.0 + roots[levels[1]])
    nodes[2] = 0.5 * roots[levels[2]]
    return coeff.astype(np.float32), picks.astype(np.float32), nodes.astype(np.float32)


def wrap_unit(delta):
    return (delta - jnp.floor(delta + 0.5)) * side_length


def wrap_z(delta, length_z):
    return delta - length_z * jnp.floor(delta * (1.0 / length_z) + 0.5)


def tensor(five, three, dx, dy, dz):
    fx, fy, fz = five * dx, five * dy, five * dz
    return (fx * dx - three, fx * dy, fx * dz, fy * dy - three, fy * dz, fz * dz - three)


def columns(tile, count, put):
    turned = tile.T
    for k in range(count):
        put(k, jnp.broadcast_to(turned[:, k : k + 1], (BLOCK, BLOCK)))


def diagonal(step):
    row = lax.broadcasted_iota(jnp.int32, (SUB, BLOCK), 0)
    lane = lax.broadcasted_iota(jnp.int32, (SUB, BLOCK), 1)
    return lane - row == step * SUB


def spread(tile, k):
    return jnp.broadcast_to(tile[k : k + 1, :], (SUB, BLOCK))


def row_sum(x):
    return jnp.sum(x, axis=0, keepdims=True)


def build_pair(col, rows, put, length_z):
    def part(step, unused):
        at = pl.ds(pl.multiple_of(step * CHUNK, CHUNK), CHUNK)
        wide = [jnp.broadcast_to(r, (CHUNK, BLOCK)) for r in rows]
        dx = wrap_unit(col[0, at, :] - wide[0])
        dy = wrap_unit(col[1, at, :] - wide[1])
        dz = wrap_z(col[2, at, :] - wide[2], length_z)
        keep = col[4, at, :] != wide[4]
        dist = jnp.where(keep, dx * dx + dy * dy + dz * dz, 1.0)
        inv = lax.rsqrt(dist)
        inv_two = inv * inv
        inv_three = inv * inv_two
        s = dist * (dist * inv) * (col[3, at, :] * wide[3])
        decay = jnp.exp(-s)
        small = s * (1.0 - s * (0.5 - s * (1.0 / 6.0 - s * (1.0 / 24.0 - s * (1.0 / 120.0)))))
        three = jnp.where(s < 0.0625, small, 1.0 - decay)
        five = 3.0 * (three - s * decay) * (inv_three * inv_two)
        three = jnp.where(keep, three * inv_three, 0.0)
        five = jnp.where(keep, five, 0.0)
        for k, value in enumerate(tensor(five, three, dx, dy, dz)):
            put(k, at, value)
        return unused

    lax.fori_loop(0, BLOCK // CHUNK, part, 0)


def project(phi, v, tiles):
    out = []
    per = tiles // BOXES_DEV
    for box in range(BOXES_DEV):
        wide = [[spread(v[box * per + t], c) for c in range(3)] for t in range(per)]

        def part(step, acc):
            at = pl.ds(pl.multiple_of(step * SUB, SUB), SUB)
            sums = [None] * 3
            for t in range(per):
                value = phi[box * per + t, at, :]
                for c in range(3):
                    term = value * wide[t][c]
                    sums[c] = term if sums[c] is None else sums[c] + term
            mask = diagonal(step)
            return tuple(
                a + jnp.where(mask, jnp.sum(x, axis=1, keepdims=True), 0.0)
                for a, x in zip(acc, sums)
            )

        zero = jnp.zeros((SUB, BLOCK), f32)
        acc = lax.fori_loop(0, BLOCK // SUB, part, (zero, zero, zero))
        out += [row_sum(a) for a in acc]
    return out


def edges(meta, put_core, put_ring, tiles, reach):
    even = meta[0] % 2 == 0
    high, low = tiles - reach, 0
    put_core(jnp.where(even, high, low))
    put_ring(jnp.where(even, low, high))


def first_body(
    meta, pos, alpha, field, gid, picks, stat, x0, phi, weights, core, ring, *, coeff, box_height, tiles, reach
):
    total = tiles * BLOCK
    lane = lax.broadcasted_iota(jnp.int32, (1, total), 1)
    first = meta[0] * BOXES_DEV
    box = jnp.where(lane < total // BOXES_DEV, first, first + 1).astype(f32)
    p = pos[...]
    al = alpha[...]
    coords = [
        p[0:1] / 16.0 - 1.0,
        p[1:2] / 16.0 - 1.0,
        2.0 * (p[2:3] - box * box_height) / box_height - 1.0,
    ]
    levels = []
    for u in coords:
        terms = [None, u]
        for degree in range(2, ORDER):
            prev = terms[-2] if degree > 2 else 1.0
            terms.append(2.0 * u * terms[-1] - prev)
        rows = []
        for k in range(ORDER):
            value = float(coeff[k, 0]) + float(coeff[k, 1]) * terms[1]
            for n in range(2, ORDER):
                value = value + float(coeff[k, n]) * terms[n]
            rows.append(value)
        levels.append(jnp.concatenate(rows + [jnp.zeros((8 - ORDER, total), f32)], axis=0))
    wide = 4 * BLOCK
    for begin in range(0, total, wide):
        value = None
        for d in range(3):
            part = jnp.dot(
                picks[d], levels[d][:, begin : begin + wide], precision=highest, preferred_element_type=f32
            )
            value = part if value is None else value * part
        for t in range(4):
            phi[begin // BLOCK + t] = value[:, t * BLOCK : (t + 1) * BLOCK]
    start = al * field[...]
    scaled = jnp.concatenate(
        [
            p[0:2] * (1.0 / side_length),
            p[2:3],
            lax.rsqrt(al) * math.sqrt(thole_damp),
            gid[...].astype(f32),
            al,
            jnp.zeros((2, total), f32),
        ],
        axis=0,
    )
    vec = jnp.concatenate([start, jnp.zeros((5, total), f32)], axis=0)
    for t in range(tiles):
        stat[t] = scaled[:, t * BLOCK : (t + 1) * BLOCK]
        x0[t] = vec[:, t * BLOCK : (t + 1) * BLOCK]
    rows = project(phi, x0, tiles)
    weights[...] = jnp.concatenate(rows + [jnp.zeros((2, BLOCK), f32)], axis=0)

    def put(ref):
        def at(begin):
            for k in range(reach):
                ref[k] = stat[begin + k]
                ref[reach + k] = x0[begin + k]

        return at

    edges(meta, put(core), put(ring), tiles, reach)


def own_slot(b, begin, tiles, reach):
    k = jnp.maximum(b - (tiles - reach), 0)
    return (b - begin) * (reach + 1) - k * (k + 1) // 2


def own_slots(begin, end, tiles, reach):
    return sum(min(reach + 1, tiles - b) for b in range(begin, end))


def tensors_body(mask, stat, out, col, *, begin, end, tiles, reach, length_z):
    def visit(b, unused):
        def put(k, value):
            col[k] = value

        columns(stat[b], 5, put)
        slot = own_slot(b, begin, tiles, reach)
        for o in range(reach + 1):

            @pl.when((b + o < tiles) & (mask[b * (2 * reach + 1) + reach + o] != 0))
            def _():
                other = stat[b + o]
                rows = [other[k : k + 1, :] for k in range(5)]

                def store(k, at, value):
                    out[slot + o, k, at, :] = value

                build_pair(col, rows, store, length_z)

        return unused

    lax.fori_loop(begin, end, visit, 0)


def own_body(mask, v, *rest, ranges, tiles, reach):
    tabs = rest[: len(ranges)]
    out, acc_i, acc_j, col = rest[len(ranges) :]

    def clear(t, unused):
        for c in range(3):
            acc_j[t, c] = jnp.zeros((SUB, BLOCK), f32)
        return unused

    lax.fori_loop(0, tiles, clear, 0)
    for (begin, end), tab in zip(ranges, tabs):

        def visit(b, unused):
            def put(k, value):
                col[k] = value

            columns(v[b], 3, put)
            for c in range(3):
                acc_i[c] = jnp.zeros((BLOCK, BLOCK), f32)
            slot = own_slot(b, begin, tiles, reach)
            for o in range(reach + 1):

                @pl.when((b + o < tiles) & (mask[b * (2 * reach + 1) + reach + o] != 0))
                def _():
                    other = v[b + o]
                    wide = [spread(other, c) for c in range(3)]

                    def part(step, acc):
                        at = pl.ds(pl.multiple_of(step * SUB, SUB), SUB)
                        xx, xy, xz, yy, yz, zz = [tab[slot + o, k, at, :] for k in range(6)]
                        vx, vy, vz = wide
                        acc_i[0, at, :] += xx * vx + xy * vy + xz * vz
                        acc_i[1, at, :] += xy * vx + yy * vy + yz * vz
                        acc_i[2, at, :] += xz * vx + yz * vy + zz * vz
                        if o == 0:
                            return acc
                        ux, uy, uz = [col[c, at, :] for c in range(3)]
                        return (
                            acc[0] + (xx * ux + xy * uy + xz * uz),
                            acc[1] + (xy * ux + yy * uy + yz * uz),
                            acc[2] + (xz * ux + yz * uy + zz * uz),
                        )

                    zero = jnp.zeros((SUB, BLOCK), f32)
                    acc = lax.fori_loop(0, BLOCK // SUB, part, (zero, zero, zero), unroll=4)
                    if o > 0:
                        for c in range(3):
                            acc_j[b + o, c] += acc[c]

            for c in range(3):
                total = acc_j[b, c]
                for step in range(BLOCK // SUB):
                    value = jnp.sum(acc_i[c, step * SUB : (step + 1) * SUB, :], axis=1, keepdims=True)
                    total = total + jnp.where(diagonal(step), value, 0.0)
                acc_j[b, c] = total
            return unused

        lax.fori_loop(begin, end, visit, 0)

    def finish(t, unused):
        rows = [row_sum(acc_j[t, c]) for c in range(3)]
        out[t] = jnp.concatenate(rows + [jnp.zeros((5, BLOCK), f32)], axis=0)
        return unused

    lax.fori_loop(0, tiles, finish, 0)


def halo_pairs(tiles, reach):
    pairs = []
    for l in range(reach):
        for c in range(l + 1):
            pairs.append((l, c, l - c))
    for l in range(reach):
        for c in range(tiles - reach + l, tiles):
            pairs.append((reach + l, c, reach + tiles + l - c))
    return pairs


def halo_tiles(meta, core, ring, begin, reach, put):
    even = meta[0] % 2 == 0
    for k in range(reach):
        a, b = core[begin + k], ring[begin + k]
        put(k, jnp.where(even, b, a))
        put(reach + k, jnp.where(even, a, b))


def halo_tensors_body(meta, mask, stat, core, ring, out, held, col, *, tiles, reach, length_z):
    def keep(k, value):
        held[k] = value

    halo_tiles(meta, core, ring, 0, reach, keep)
    last = None
    for index, (h, c, m) in enumerate(halo_pairs(tiles, reach)):
        if h != last:

            def put(k, value):
                col[k] = value

            columns(held[h], 5, put)
            last = h

        @pl.when(mask[c * (2 * reach + 1) + m] != 0)
        def _():
            own = stat[c]
            rows = [own[k : k + 1, :] for k in range(5)]

            def store(k, at, value):
                out[index, k, at, :] = value

            build_pair(col, rows, store, length_z)


def far_geometry(nodes, geo, box_height):
    turned = nodes[...].T
    row = nodes[...]

    def delta(k):
        return jnp.broadcast_to(turned[:, k : k + 1], (BLOCK, BLOCK)) - jnp.broadcast_to(
            row[k : k + 1, :], (BLOCK, BLOCK)
        )

    dx, dy = wrap_unit(delta(0)), wrap_unit(delta(1))
    geo[0] = dx
    geo[1] = dy
    geo[2] = box_height * delta(2)
    geo[3] = dx * dx + dy * dy + box_height * box_height


def far_tensor(geo, apart, put, box_height, length_z):
    def part(step, unused):
        at = pl.ds(pl.multiple_of(step * CHUNK, CHUNK), CHUNK)
        dx, dy = geo[0, at, :], geo[1, at, :]
        dz = wrap_z(geo[2, at, :] - apart * box_height, length_z)
        inv = lax.rsqrt(geo[3, at, :] + dz * dz)
        inv_two = inv * inv
        three = inv * inv_two
        five = 3.0 * three * inv_two
        for k, value in enumerate(tensor(five, three, dx, dy, dz)):
            put(k, at, value)
        return unused

    lax.fori_loop(0, BLOCK // CHUNK, part, 0)


def far_tensors_body(nodes, out, geo, *, box_height, length_z):
    far_geometry(nodes, geo, box_height)

    def visit(d, unused):
        def put(k, at, value):
            out[d - 1, k, at, :] = value

        far_tensor(geo, d.astype(f32), put, box_height, length_z)
        return unused

    lax.fori_loop(1, out.shape[0] + 1, visit, 0)


def apply_tensor(t, v):
    xx, xy, xz, yy, yz, zz = t
    x, y, z = v
    return (
        xx * x + xy * y + xz * z,
        xy * x + yy * y + yz * z,
        xz * x + yz * y + zz * z,
    )


def far_nodes(table, geo, wide, fcol, boxes, box_height, length_z):
    if table is not None:
        def rows(step, unused):
            at = pl.ds(pl.multiple_of(step * SUB, SUB), SUB)

            def load(d):
                return [table[d - 1, k, at, :] for k in range(6)]

            def field(t, k):
                return apply_tensor(t, [wide[k, c] for c in range(3)])

            def visit(d, acc):
                t = load(d)
                new = field(t, d) + field(t, d + 1)
                return tuple(a + n for a, n in zip(acc, new))

            acc = field(load(boxes - 1), boxes - 1) + field(load(1), 2)
            acc = lax.fori_loop(2, boxes - 1, visit, acc, unroll=4)
            for box in range(BOXES_DEV):
                for c in range(3):
                    fcol[box, c, at, :] = jnp.broadcast_to(
                        jnp.sum(acc[box * 3 + c], axis=1, keepdims=True), (SUB, BLOCK)
                    )
            return unused

        lax.fori_loop(0, BLOCK // SUB, rows, 0)
        return
    for box in range(BOXES_DEV):
        for c in range(3):
            fcol[box, c] = jnp.zeros((BLOCK, BLOCK), f32)

    def visit(d, unused):
        def hold(k, at, value):
            geo[4 + k, at, :] = value

        far_tensor(geo, d.astype(f32), hold, box_height, length_z)
        for box in range(BOXES_DEV):

            @pl.when(d < boxes - 1 if box else d > 1)
            def _():
                v = [wide[d + box, c] for c in range(3)]

                def part(step, skip):
                    at = pl.ds(pl.multiple_of(step * SUB, SUB), SUB)
                    new = apply_tensor([geo[4 + k, at, :] for k in range(6)], v)
                    for c in range(3):
                        fcol[box, c, at, :] += new[c]
                    return skip

                lax.fori_loop(0, BLOCK // SUB, part, 0)

        return unused

    lax.fori_loop(1, boxes, visit, 0)
    for box in range(BOXES_DEV):
        for c in range(3):
            fcol[box, c] = jnp.broadcast_to(
                jnp.sum(fcol[box, c], axis=1, keepdims=True), (BLOCK, BLOCK)
            )


def field_body(meta, mask, nodes, stat, v, near, phi, gathered, core, ring, halo_tab, *rest,
               mode, tiles, reach, plane, slabs, box_height, length_z, surface, kept, offset):
    rest = list(rest)
    table = rest.pop(0) if kept else None
    extra = [rest.pop(0) for _ in range((0, 0, 4)[mode])]
    outs = [rest.pop(0) for _ in range((5, 6, 5)[mode])]
    acc, held, col, wide, fcol, geo = rest
    boxes = slabs * BOXES_DEV
    member = meta[0]
    own_row, own_col = member // plane, member % plane

    def expand(k, total):
        other = lax.rem(member + k, slabs)
        slot = lax.bitwise_xor(other // plane, own_row) * plane + lax.bitwise_xor(other % plane, own_col)
        tile = gathered[slot]
        for box in range(BOXES_DEV):
            for c in range(3):
                wide[k * BOXES_DEV + box, c] = spread(tile, box * 3 + c)
        return total + tile

    total = lax.fori_loop(0, slabs, expand, jnp.zeros((SUB, BLOCK), f32))
    sums = jnp.sum(total, axis=1, keepdims=True)
    moment = [surface * (sums[c : c + 1] + sums[3 + c : 4 + c]) for c in range(3)]

    def keep(k, value):
        held[k] = value

    halo_tiles(meta, core, ring, offset, reach, keep)

    def clear(t, unused):
        for c in range(3):
            acc[t, c] = jnp.zeros((SUB, BLOCK), f32)
        return unused

    lax.fori_loop(0, tiles, clear, 0)
    last = None
    for index, (h, c, m) in enumerate(halo_pairs(tiles, reach)):
        if h != last:

            def put(k, value):
                col[k] = value

            columns(held[h], 3, put)
            last = h

        @pl.when(mask[c * (2 * reach + 1) + m] != 0)
        def _():
            def part(step, sofar):
                at = pl.ds(pl.multiple_of(step * SUB, SUB), SUB)
                new = apply_tensor(
                    [halo_tab[index, k, at, :] for k in range(6)], [col[k, at, :] for k in range(3)]
                )
                return tuple(a + n for a, n in zip(sofar, new))

            zero = jnp.zeros((SUB, BLOCK), f32)
            new = lax.fori_loop(0, BLOCK // SUB, part, (zero, zero, zero), unroll=4)
            for k in range(3):
                acc[c, k] += new[k]

    if not kept:
        far_geometry(nodes, geo, box_height)
    far_nodes(table, geo, wide, fcol, boxes, box_height, length_z)

    per = tiles // BOXES_DEV
    zero = jnp.zeros((5, BLOCK), f32)
    fields = []
    for t in range(tiles):
        box = t // per
        sofar = [acc[t, c] for c in range(3)]
        for step in range(BLOCK // SUB):
            at = slice(step * SUB, (step + 1) * SUB)
            value = phi[t, at, :]
            sofar = [a + value * fcol[box, c, at, :] for c, a in enumerate(sofar)]
        rows = [row_sum(a) - m for a, m in zip(sofar, moment)]
        fields.append(near[t] + jnp.concatenate(rows + [zero], axis=0))

    def alpha(t):
        return spread(stat[t], 5)

    none = jnp.zeros((1, BLOCK), f32)

    def send(u, weights, core_out, ring_out, scalar):
        rows = project(phi, u, tiles)
        weights[...] = jnp.concatenate(rows + [scalar, none], axis=0)

        def at(ref):
            def store(begin):
                for k in range(reach):
                    ref[k] = u[begin + k]

            return store

        edges(meta, at(core_out), at(ring_out), tiles, reach)

    def fold(parts):
        out = parts[0]
        for x in parts[1:]:
            out = out + x
        return row_sum(out)

    if mode == 0:
        res, u, weights, core_out, ring_out = outs
        dots = []
        for t in range(tiles):
            scaled = alpha(t) * fields[t]
            res[t] = fields[t]
            u[t] = scaled
            dots.append(scaled * fields[t])
        send(u, weights, core_out, ring_out, fold(dots))
    elif mode == 1:
        image, u, weights, core_out, ring_out, norm = outs
        dots = []
        for t in range(tiles):
            w = v[t] / alpha(t) - fields[t]
            image[t] = w
            u[t] = alpha(t) * w
            dots.append(v[t] * w)
        norm[...] = jnp.broadcast_to(sums[6:7], (SUB, BLOCK))
        send(u, weights, core_out, ring_out, fold(dots))
    else:
        first, res, w0, norm = extra
        x1, r1, z1, q1, scal = outs
        rate = norm[...] / jnp.broadcast_to(sums[6:7], (SUB, BLOCK))
        one, two, three = [], [], []
        for t in range(tiles):
            y = v[t] / alpha(t) - fields[t]
            r = res[t] - rate * w0[t]
            z = alpha(t) * r
            q = w0[t] - rate * y
            x1[t] = first[t] + rate * (alpha(t) * res[t])
            r1[t] = r
            z1[t] = z
            q1[t] = q
            one.append(r * z)
            two.append(z * q)
            three.append(z * w0[t])
        scal[...] = jnp.concatenate(
            [fold(one), fold(two), fold(three), jnp.broadcast_to(sums[6:7], (1, BLOCK)), norm[0:1], none, none, none],
            axis=0,
        )


def last_body(gathered, scal, stat, res, w0, x1, r1, z1, q1, dip, out, *, tiles):
    total = gathered[0]
    for k in range(1, gathered.shape[0]):
        total = total + gathered[k]
    sums = jnp.sum(total, axis=1, keepdims=True)

    def value(x):
        return jnp.broadcast_to(x, (1, BLOCK))

    norm, curve, cross = value(sums[0:1]), value(sums[1:2]), value(sums[2:3])
    along, start = scal[3:4], scal[4:5]
    beta = norm / start
    rate = norm / (curve + 2.0 * beta * cross + beta * beta * along)
    for t in range(tiles):
        at = slice(t * BLOCK, (t + 1) * BLOCK)
        u0 = stat[t][5:6] * res[t][0:3]
        p = z1[t][0:3] + beta * u0
        w = q1[t][0:3] + beta * w0[t][0:3]
        dip[:, at] = x1[t][0:3] + rate * p
        out[:, at] = r1[t][0:3] - rate * w


def swap(x, axes, count):
    got = [x]
    for s in range(1, count):
        got.append(lax.ppermute(x, axes, [(i, i ^ s) for i in range(count)]))
    return got


def gather(x, plane, rows):
    near = jnp.stack(swap(x, ("oct", "sub"), plane))
    return jnp.concatenate(swap(near, "blk", rows), axis=0)


def halo(core, ring):
    count = lax.axis_size(RING)
    size = lax.axis_size("sub")
    got_core = lax.ppermute(core, "sub", [(i, i ^ 1) for i in range(size)])
    pairs = [(i, (i + 1) % count) for i in range(1, count, 2)]
    got_ring = lax.ppermute(ring, RING, pairs + [(b, a) for a, b in pairs])
    return got_core, got_ring


def on_device(positions, polarizability, permanent_field, group_id, pair_mask):
    slabs = lax.axis_size(RING)
    member = lax.axis_index(RING)
    plane = lax.axis_size(("oct", "sub"))
    rows = lax.axis_size("blk")
    atoms = positions.shape[1]
    tiles = atoms // BLOCK
    length_z = layer_gap * atoms * slabs / 256.0
    boxes = BOXES_DEV * slabs
    box_height = length_z / boxes
    reach = (pair_mask.shape[1] - 1) // 2
    surface = 4.0 * math.pi / 3.0 / (side_length * side_length * length_z)
    coeff, picks, nodes = node_tables()
    nodes = jnp.asarray(nodes)
    meta = jnp.reshape(member, (1,)).astype(jnp.int32)
    mask = pair_mask.reshape(-1)
    tile_shape = (tiles, 8, BLOCK)
    edge = (reach, 8, BLOCK)
    kept = (boxes - 1) * 6 * BLOCK * BLOCK * 4 <= TABLE_LIMIT

    stat, x0, phi, weights, core, ring = call(
        functools.partial(first_body, coeff=coeff, box_height=box_height, tiles=tiles, reach=reach),
        [tile_shape, tile_shape, (tiles, BLOCK, BLOCK), (8, BLOCK), (2 * reach, 8, BLOCK), (2 * reach, 8, BLOCK)],
        [meta, positions, polarizability[None], permanent_field, group_id[None], jnp.asarray(picks)],
        smem=1,
        limit=16 << 20,
    )
    got_core, got_ring = halo(core, ring)
    gathered = gather(weights, plane, rows)

    ranges = [(0, tiles // 2), (tiles // 2, tiles)]
    tabs = []
    for begin, end in ranges:
        count = own_slots(begin, end, tiles, reach)
        tabs += call(
            functools.partial(tensors_body, begin=begin, end=end, tiles=tiles, reach=reach, length_z=length_z),
            [(count, 6, BLOCK, BLOCK)],
            [mask, stat],
            smem=1,
            scratch=[(5, BLOCK, BLOCK)],
            cost=pl.CostEstimate(flops=count * BLOCK * BLOCK * 70, bytes_accessed=1 << 20, transcendentals=count * BLOCK * BLOCK * 2),
            pinned=(0,),
        )
    table = []
    if kept:
        table = call(
            functools.partial(far_tensors_body, box_height=box_height, length_z=length_z),
            [(boxes - 1, 6, BLOCK, BLOCK)],
            [nodes],
            scratch=[(4, BLOCK, BLOCK)],
            cost=pl.CostEstimate(flops=boxes * BLOCK * BLOCK * 28, bytes_accessed=1 << 20, transcendentals=boxes * BLOCK * BLOCK),
            pinned=(0,),
        )
    (halo_tab,) = call(
        functools.partial(halo_tensors_body, tiles=tiles, reach=reach, length_z=length_z),
        [(len(halo_pairs(tiles, reach)), 6, BLOCK, BLOCK)],
        [meta, mask, stat, got_core, got_ring],
        smem=2,
        scratch=[(2 * reach, 8, BLOCK), (5, BLOCK, BLOCK)],
        pinned=(0,),
    )

    def own_field(v):
        return call(
            functools.partial(own_body, ranges=ranges, tiles=tiles, reach=reach),
            [tile_shape],
            [mask, v] + tabs,
            smem=1,
            scratch=[(3, BLOCK, BLOCK), (tiles, 3, SUB, BLOCK), (3, BLOCK, BLOCK)],
            cost=pl.CostEstimate(flops=72 * 2 * BLOCK * BLOCK * 18, bytes_accessed=1 << 20, transcendentals=0),
        )[0]

    def field(mode, v, gathered, got_core, got_ring, extra):
        near = own_field(v)
        offset = reach if mode == 0 else 0
        outs = [
            [tile_shape, tile_shape, (8, BLOCK), edge, edge],
            [tile_shape, tile_shape, (8, BLOCK), edge, edge, (SUB, BLOCK)],
            [tile_shape] * 4 + [(8, BLOCK)],
        ][mode]
        return call(
            functools.partial(
                field_body, mode=mode, tiles=tiles, reach=reach, plane=plane, slabs=slabs, box_height=box_height,
                length_z=length_z, surface=surface, kept=kept, offset=offset,
            ),
            outs,
            [meta, mask, nodes, stat, v, near, phi, gathered, got_core, got_ring, halo_tab] + table + extra,
            smem=2,
            scratch=[
                (tiles, 3, SUB, BLOCK),
                (2 * reach, 8, BLOCK),
                (3, BLOCK, BLOCK),
                (boxes, 3, SUB, BLOCK),
                (BOXES_DEV, 3, BLOCK, BLOCK),
                (10, BLOCK, BLOCK) if not kept else (1, 8, BLOCK),
            ],
        )

    r0, u0, weights, core, ring = field(0, x0, gathered, got_core, got_ring, [])
    got_core, got_ring = halo(core, ring)
    gathered = gather(weights, plane, rows)
    w0, u1, weights, core, ring, norm = field(1, u0, gathered, got_core, got_ring, [])
    got_core, got_ring = halo(core, ring)
    gathered = gather(weights, plane, rows)
    x1, r1, z1, q1, scal = field(2, u1, gathered, got_core, got_ring, [x0, r0, w0, norm])
    gathered = gather(scal, plane, rows)
    return call(
        functools.partial(last_body, tiles=tiles),
        [(3, atoms), (3, atoms)],
        [gathered, scal, stat, r0, w0, x1, r1, z1, q1],
    )


def solution(mesh):
    split = P(("groups", "blk", "oct", "sub"))
    wide = P(None, ("groups", "blk", "oct", "sub"))
    return jax.shard_map(
        lambda *args: tuple(on_device(*args)),
        mesh=mesh,
        in_specs=(wide, split, wide, split, P(("groups", "blk", "oct", "sub"), None)),
        out_specs=(wide, wide),
        check_vma=False,
    )
```

```python
import functools
import math

import jax
import jax.numpy as jnp
import numpy as np
from jax import lax
from jax.experimental import pallas as pl
from jax.experimental.pallas import tpu as pltpu
from jax.sharding import PartitionSpec as P

BOXES_DEV = 2
BLOCK = 128
ORDER = 5
NODE_PAD = 128
ITERS = 2
SUB = 8
CHUNK = 32

side_length = 32.0
layer_gap = 2.5
thole_damp = 0.39
highest = lax.Precision.HIGHEST
f32 = jnp.float32
RING = ("blk", "oct", "sub")

VM = pl.BlockSpec(memory_space=pltpu.VMEM)
SM = pl.BlockSpec(memory_space=pltpu.SMEM)
TABLE_LIMIT = 16 << 20


def call(body, outs, args, smem=0, scratch=(), limit=None, cost=None, pinned=(), far=False, more=()):
    shapes = [
        pltpu.VMEM(shape, f32) if at in pinned else jax.ShapeDtypeStruct(shape, f32)
        for at, shape in enumerate(outs)
    ]
    return list(pl.pallas_call(
        body,
        out_shape=shapes,
        in_specs=[SM] * smem + [pl.BlockSpec(memory_space=pltpu.HBM) if far else VM] * (len(args) - smem),
        out_specs=[VM] * len(outs),
        scratch_shapes=[pltpu.VMEM(shape, f32) for shape in scratch] + list(more),
        compiler_params=pltpu.CompilerParams(vmem_limit_bytes=limit or (12 << 20)),
        cost_estimate=cost,
    )(*args))


def node_tables():
    count = ORDER
    roots = np.cos((2.0 * np.arange(count) + 1.0) * np.pi / (2.0 * count))
    degree = np.arange(count)
    coeff = (
        2.0 / count * np.cos(np.outer(2.0 * np.arange(count) + 1.0, degree) * np.pi / (2.0 * count))
    )
    coeff = np.where(degree[None, :] == 0, 1.0 / count, coeff)
    index = np.arange(NODE_PAD)
    live = index < count**3
    safe = np.where(live, index, 0)
    levels = np.stack([safe // (count * count), safe // count % count, safe % count])
    picks = (levels[:, :, None] == np.arange(8)) * 1.0
    picks[0] *= live[:, None]
    nodes = np.zeros((8, NODE_PAD))
    nodes[0] = 0.5 * (1.0 + roots[levels[0]])
    nodes[1] = 0.5 * (1.0 + roots[levels[1]])
    nodes[2] = 0.5 * roots[levels[2]]
    return coeff.astype(np.float32), picks.astype(np.float32), nodes.astype(np.float32)


def wrap_unit(delta):
    return (delta - jnp.floor(delta + 0.5)) * side_length


def wrap_z(delta, length_z):
    return delta - length_z * jnp.floor(delta * (1.0 / length_z) + 0.5)


def tensor(five, three, dx, dy, dz):
    five = jnp.maximum(five, 1e-36)
    root = five * lax.rsqrt(five)
    return (root * dx, root * dy, root * dz, three)


def columns(tiles, count, out):
    for t, tile in enumerate(tiles):
        turned = tile.T
        for k in range(count):
            out[t, k] = jnp.broadcast_to(turned[:, k : k + 1], (BLOCK, BLOCK))


def diagonal(step):
    row = lax.broadcasted_iota(jnp.int32, (SUB, BLOCK), 0)
    lane = lax.broadcasted_iota(jnp.int32, (SUB, BLOCK), 1)
    return lane - row == step * SUB


def spread(tile, k):
    return jnp.broadcast_to(tile[k : k + 1, :], (SUB, BLOCK))


def row_sum(x):
    return jnp.sum(x, axis=0, keepdims=True)


def build_pair(col, rows, put, length_z):
    wide = [jnp.broadcast_to(r, (CHUNK, BLOCK)) for r in rows]
    for step in range(BLOCK // CHUNK):
        at = slice(step * CHUNK, (step + 1) * CHUNK)
        dx = wrap_unit(col(0, at) - wide[0])
        dy = wrap_unit(col(1, at) - wide[1])
        dz = wrap_z(col(2, at) - wide[2], length_z)
        keep = col(4, at) != wide[4]
        dist = jnp.where(keep, dx * dx + dy * dy + dz * dz, 1e24)
        inv = lax.rsqrt(dist)
        inv_two = inv * inv
        inv_three = inv * inv_two
        s = dist * (dist * inv) * (col(3, at) * wide[3])
        decay = jnp.exp(-s)
        small = s * (1.0 - s * (0.5 - s * (1.0 / 6.0 - s * (1.0 / 24.0))))
        three = jnp.where(s < 0.015625, small, 1.0 - decay)
        five = (three - s * decay) * (3.0 * inv_two * inv_three)
        for k, value in enumerate(tensor(five, three * inv_three, dx, dy, dz)):
            put(k, at, value)


def lane_sums(parts):
    total = None
    for step, x in enumerate(parts):
        term = jnp.where(diagonal(step), jnp.sum(x, axis=1, keepdims=True), 0.0)
        total = term if total is None else total + term
    return total


def project(phi, v, tiles):
    out = []
    per = tiles // BOXES_DEV
    for box in range(BOXES_DEV):
        wide = [[spread(v[box * per + t], c) for c in range(3)] for t in range(per)]
        parts = [[], [], []]
        for step in range(BLOCK // SUB):
            at = slice(step * SUB, (step + 1) * SUB)
            sums = [None] * 3
            for t in range(per):
                value = phi[box * per + t, at, :]
                for c in range(3):
                    term = value * wide[t][c]
                    sums[c] = term if sums[c] is None else sums[c] + term
            for c in range(3):
                parts[c].append(sums[c])
        out += [row_sum(lane_sums(p)) for p in parts]
    return out


def edges(meta, put_core, put_ring, tiles, reach):
    even = meta[0] % 2 == 0
    high, low = tiles - reach, 0
    put_core(jnp.where(even, high, low))
    put_ring(jnp.where(even, low, high))


def first_body(
    meta, pos_in, alpha_in, field_in, gid_in, picks_in, stat, x0, phi, weights, core, ring,
    pos, alpha, field, gid, picks, sems, *, coeff, box_height, tiles, reach
):
    pairs = [(pos_in, pos), (alpha_in, alpha), (field_in, field), (gid_in, gid), (picks_in, picks)]
    copies = [pltpu.make_async_copy(a, b, sems.at[k]) for k, (a, b) in enumerate(pairs)]
    for copy in copies:
        copy.start()
    for copy in copies:
        copy.wait()
    total = tiles * BLOCK
    lane = lax.broadcasted_iota(jnp.int32, (1, total), 1)
    first = meta[0] * BOXES_DEV
    box = jnp.where(lane < total // BOXES_DEV, first, first + 1).astype(f32)
    p = pos[...]
    al = alpha[...]
    coords = [
        p[0:1] / 16.0 - 1.0,
        p[1:2] / 16.0 - 1.0,
        2.0 * (p[2:3] - box * box_height) / box_height - 1.0,
    ]
    levels = []
    for u in coords:
        terms = [None, u]
        for degree in range(2, ORDER):
            prev = terms[-2] if degree > 2 else 1.0
            terms.append(2.0 * u * terms[-1] - prev)
        rows = []
        for k in range(ORDER):
            value = float(coeff[k, 0]) + float(coeff[k, 1]) * terms[1]
            for n in range(2, ORDER):
                value = value + float(coeff[k, n]) * terms[n]
            rows.append(value)
        levels.append(jnp.concatenate(rows + [jnp.zeros((8 - ORDER, total), f32)], axis=0))
    wide = 4 * BLOCK
    for begin in range(0, total, wide):
        value = None
        for d in range(3):
            part = jnp.dot(
                picks[d], levels[d][:, begin : begin + wide], precision=highest, preferred_element_type=f32
            )
            value = part if value is None else value * part
        for t in range(4):
            phi[begin // BLOCK + t] = value[:, t * BLOCK : (t + 1) * BLOCK]
    start = al * field[...]
    scaled = jnp.concatenate(
        [
            p[0:2] * (1.0 / side_length),
            p[2:3],
            lax.rsqrt(al) * math.sqrt(thole_damp),
            gid[...].astype(f32),
            al,
            jnp.zeros((2, total), f32),
        ],
        axis=0,
    )
    vec = jnp.concatenate([start, jnp.zeros((5, total), f32)], axis=0)
    for t in range(tiles):
        stat[t] = scaled[:, t * BLOCK : (t + 1) * BLOCK]
        x0[t] = vec[:, t * BLOCK : (t + 1) * BLOCK]
    rows = project(phi, x0, tiles)
    weights[...] = jnp.concatenate(rows + [jnp.zeros((2, BLOCK), f32)], axis=0)

    def put(ref):
        def at(begin):
            for k in range(reach):
                ref[k] = stat[begin + k]
                ref[reach + k] = x0[begin + k]

        return at

    edges(meta, put(core), put(ring), tiles, reach)


def own_slot(b, begin, tiles, reach):
    k = jnp.maximum(b - (tiles - reach), 0)
    return (b - begin) * (reach + 1) - k * (k + 1) // 2


def own_slots(begin, end, tiles, reach):
    return sum(min(reach + 1, tiles - b) for b in range(begin, end))


def tensors_body(mask, stat, out, col, *, begin, end, tiles, reach, length_z):
    columns([stat[t] for t in range(begin, end)], 5, col)

    def visit(b, unused):
        slot = own_slot(b, begin, tiles, reach)
        for o in range(reach + 1):

            @pl.when((b + o < tiles) & (mask[b, reach + o] != 0) if o else b >= 0)
            def _():
                other = stat[b + o]
                rows = [other[k : k + 1, :] for k in range(5)]

                def store(k, at, value):
                    out[slot + o, k, at, :] = value

                build_pair(lambda k, at: col[b - begin, k, at, :], rows, store, length_z)

        return unused

    lax.fori_loop(begin, end, visit, 0)


def own_body(mask, v, *rest, ranges, tiles, reach):
    tabs = rest[: len(ranges)]
    out, acc_i, acc_j, col = rest[len(ranges) :]
    columns([v[t] for t in range(tiles)], 3, col)
    for t in range(tiles):
        for c in range(3):
            acc_j[t, c] = jnp.zeros((SUB, BLOCK), f32)
    for (begin, end), tab in zip(ranges, tabs):

        def visit(b, unused):
            slot = own_slot(b, begin, tiles, reach)
            for o in range(reach + 1):

                @pl.when((b + o < tiles) & (mask[b, reach + o] != 0) if o else b >= 0)
                def _():
                    other = v[b + o]
                    wide = [spread(other, c) for c in range(3)]
                    acc = [acc_j[b + o, c] for c in range(3)] if o else None
                    for step in range(BLOCK // SUB):
                        at = slice(step * SUB, (step + 1) * SUB)
                        t = [tab[slot + o, k, at, :] for k in range(4)]
                        new = apply_tensor(t, wide)
                        for c in range(3):
                            if o == 0:
                                acc_i[b, c, at, :] = new[c]
                            else:
                                acc_i[b, c, at, :] += new[c]
                        if o:
                            new = apply_tensor(t, [col[b, c, at, :] for c in range(3)])
                            acc = [a + n for a, n in zip(acc, new)]
                    if o:
                        for c in range(3):
                            acc_j[b + o, c] = acc[c]

            return unused

        lax.fori_loop(begin, end, visit, 0)
    for t in range(tiles):
        rows = []
        for c in range(3):
            parts = [acc_i[t, c, k * SUB : (k + 1) * SUB, :] for k in range(BLOCK // SUB)]
            rows.append(row_sum(acc_j[t, c] + lane_sums(parts)))
        out[t] = jnp.concatenate(rows + [jnp.zeros((5, BLOCK), f32)], axis=0)


def halo_pairs(tiles, reach):
    pairs = []
    for l in range(reach):
        for c in range(l + 1):
            pairs.append((l, c, l - c))
    for l in range(reach):
        for c in range(tiles - reach + l, tiles):
            pairs.append((reach + l, c, reach + tiles + l - c))
    return pairs


def halo_tiles(meta, core, ring, begin, reach):
    even = meta[0] % 2 == 0
    low, high = [], []
    for k in range(reach):
        a, b = core[begin + k], ring[begin + k]
        low.append(jnp.where(even, b, a))
        high.append(jnp.where(even, a, b))
    return low + high


def halo_tensors_body(meta, mask, stat, core, ring, out, col, *, tiles, reach, length_z):
    columns(halo_tiles(meta, core, ring, 0, reach), 5, col)
    for index, (h, c, m) in enumerate(halo_pairs(tiles, reach)):

        @pl.when(mask[c, m] != 0)
        def _():
            own = stat[c]
            rows = [own[k : k + 1, :] for k in range(5)]

            def store(k, at, value):
                out[index, k, at, :] = value

            build_pair(lambda k, at: col[h, k, at, :], rows, store, length_z)


def far_geometry(nodes, geo, box_height):
    turned = nodes[...].T
    row = nodes[...]

    def delta(k):
        return jnp.broadcast_to(turned[:, k : k + 1], (BLOCK, BLOCK)) - jnp.broadcast_to(
            row[k : k + 1, :], (BLOCK, BLOCK)
        )

    dx, dy = wrap_unit(delta(0)), wrap_unit(delta(1))
    geo[0] = dx
    geo[1] = dy
    geo[2] = box_height * delta(2)
    geo[3] = dx * dx + dy * dy + box_height * box_height


def far_tensor(geo, apart, put, box_height, length_z):
    for step in range(BLOCK // CHUNK):
        at = slice(step * CHUNK, (step + 1) * CHUNK)
        dx, dy = geo[0, at, :], geo[1, at, :]
        dz = wrap_z(geo[2, at, :] - apart * box_height, length_z)
        inv = lax.rsqrt(geo[3, at, :] + dz * dz)
        inv_two = inv * inv
        three = inv * inv_two
        five = 3.0 * three * inv_two
        for k, value in enumerate(tensor(five, three, dx, dy, dz)):
            put(k, at, value)


def far_tensors_body(nodes, out, geo, *, box_height, length_z):
    far_geometry(nodes, geo, box_height)

    def visit(d, unused):
        def put(k, at, value):
            out[d - 1, k, at, :] = value

        far_tensor(geo, d.astype(f32), put, box_height, length_z)
        return unused

    lax.fori_loop(1, out.shape[0] + 1, visit, 0)


def apply_tensor(t, v):
    ex, ey, ez, three = t
    x, y, z = v
    along = ex * x + ey * y + ez * z
    return (ex * along - three * x, ey * along - three * y, ez * along - three * z)


def far_nodes(table, geo, wide, fcol, boxes, box_height, length_z):
    if table is not None:
        def rows(step, unused):
            ats = [pl.ds(pl.multiple_of(step * 2 * SUB + k * SUB, SUB), SUB) for k in range(2)]

            def load(d):
                return [[table[d - 1, k, at, :] for k in range(4)] for at in ats]

            def field(ts, k):
                v = [wide[k, c] for c in range(3)]
                return sum([apply_tensor(t, v) for t in ts], ())

            acc = field(load(boxes - 1), boxes - 1) + field(load(1), 2)
            for d in range(2, boxes - 1):
                ts = load(d)
                new = field(ts, d) + field(ts, d + 1)
                acc = tuple(a + n for a, n in zip(acc, new))
            for box in range(BOXES_DEV):
                for half in range(2):
                    for c in range(3):
                        fcol[box, c, ats[half], :] = jnp.broadcast_to(
                            jnp.sum(acc[box * 6 + half * 3 + c], axis=1, keepdims=True), (SUB, BLOCK)
                        )
            return unused

        lax.fori_loop(0, BLOCK // (2 * SUB), rows, 0)
        return
    for box in range(BOXES_DEV):
        for c in range(3):
            fcol[box, c] = jnp.zeros((BLOCK, BLOCK), f32)

    def visit(d, unused):
        def hold(k, at, value):
            geo[4 + k, at, :] = value

        far_tensor(geo, d.astype(f32), hold, box_height, length_z)
        for box in range(BOXES_DEV):

            @pl.when(d < boxes - 1 if box else d > 1)
            def _():
                v = [wide[d + box, c] for c in range(3)]

                def part(step, skip):
                    at = pl.ds(pl.multiple_of(step * SUB, SUB), SUB)
                    new = apply_tensor([geo[4 + k, at, :] for k in range(4)], v)
                    for c in range(3):
                        fcol[box, c, at, :] += new[c]
                    return skip

                lax.fori_loop(0, BLOCK // SUB, part, 0)

        return unused

    lax.fori_loop(1, boxes, visit, 0)
    for box in range(BOXES_DEV):
        for c in range(3):
            fcol[box, c] = jnp.broadcast_to(
                jnp.sum(fcol[box, c], axis=1, keepdims=True), (BLOCK, BLOCK)
            )


def field_body(meta, mask, nodes, stat, v, near, phi, gathered, core, ring, halo_tab, *rest,
               mode, tiles, reach, plane, slabs, box_height, length_z, surface, kept, offset):
    rest = list(rest)
    table = rest.pop(0) if kept else None
    extra = [rest.pop(0) for _ in range((0, 0, 4)[mode])]
    outs = [rest.pop(0) for _ in range((5, 6, 5)[mode])]
    acc, col, wide, fcol, geo = rest
    boxes = slabs * BOXES_DEV
    member = meta[0]
    own_row, own_col = member // plane, member % plane

    def expand(k, total):
        other = lax.rem(member + k, slabs)
        slot = lax.bitwise_xor(other // plane, own_row) * plane + lax.bitwise_xor(other % plane, own_col)
        tile = gathered[slot]
        for box in range(BOXES_DEV):
            for c in range(3):
                wide[k * BOXES_DEV + box, c] = spread(tile, box * 3 + c)
        return total + tile

    total = lax.fori_loop(0, slabs, expand, jnp.zeros((SUB, BLOCK), f32))
    sums = jnp.sum(total, axis=1, keepdims=True)
    moment = [surface * (sums[c : c + 1] + sums[3 + c : 4 + c]) for c in range(3)]

    columns(halo_tiles(meta, core, ring, offset, reach), 3, col)
    for t in range(tiles):
        for c in range(3):
            acc[t, c] = jnp.zeros((SUB, BLOCK), f32)
    for index, (h, c, m) in enumerate(halo_pairs(tiles, reach)):

        @pl.when(mask[c, m] != 0)
        def _():
            sofar = [acc[c, k] for k in range(3)]
            for step in range(BLOCK // SUB):
                at = slice(step * SUB, (step + 1) * SUB)
                new = apply_tensor(
                    [halo_tab[index, k, at, :] for k in range(4)], [col[h, k, at, :] for k in range(3)]
                )
                sofar = [a + n for a, n in zip(sofar, new)]
            for k in range(3):
                acc[c, k] = sofar[k]

    if not kept:
        far_geometry(nodes, geo, box_height)
    far_nodes(table, geo, wide, fcol, boxes, box_height, length_z)

    per = tiles // BOXES_DEV
    zero = jnp.zeros((5, BLOCK), f32)
    fields = []
    for t in range(tiles):
        box = t // per
        sofar = [acc[t, c] for c in range(3)]
        for step in range(BLOCK // SUB):
            at = slice(step * SUB, (step + 1) * SUB)
            value = phi[t, at, :]
            sofar = [a + value * fcol[box, c, at, :] for c, a in enumerate(sofar)]
        rows = [row_sum(a) - m for a, m in zip(sofar, moment)]
        fields.append(near[t] + jnp.concatenate(rows + [zero], axis=0))

    def alpha(t):
        return spread(stat[t], 5)

    none = jnp.zeros((1, BLOCK), f32)

    def send(u, weights, core_out, ring_out, scalar):
        rows = project(phi, u, tiles)
        weights[...] = jnp.concatenate(rows + [scalar, none], axis=0)

        def at(ref):
            def store(begin):
                for k in range(reach):
                    ref[k] = u[begin + k]

            return store

        edges(meta, at(core_out), at(ring_out), tiles, reach)

    def fold(parts):
        out = parts[0]
        for x in parts[1:]:
            out = out + x
        return row_sum(out)

    if mode == 0:
        res, u, weights, core_out, ring_out = outs
        dots = []
        for t in range(tiles):
            scaled = alpha(t) * fields[t]
            res[t] = fields[t]
            u[t] = scaled
            dots.append(scaled * fields[t])
        send(u, weights, core_out, ring_out, fold(dots))
    elif mode == 1:
        image, u, weights, core_out, ring_out, norm = outs
        dots = []
        for t in range(tiles):
            w = v[t] / alpha(t) - fields[t]
            image[t] = w
            u[t] = alpha(t) * w
            dots.append(v[t] * w)
        norm[...] = jnp.broadcast_to(sums[6:7], (SUB, BLOCK))
        send(u, weights, core_out, ring_out, fold(dots))
    else:
        first, res, w0, norm = extra
        x1, r1, z1, q1, scal = outs
        rate = norm[...] / jnp.broadcast_to(sums[6:7], (SUB, BLOCK))
        one, two, three = [], [], []
        for t in range(tiles):
            y = v[t] / alpha(t) - fields[t]
            r = res[t] - rate * w0[t]
            z = alpha(t) * r
            q = w0[t] - rate * y
            x1[t] = first[t] + rate * (alpha(t) * res[t])
            r1[t] = r
            z1[t] = z
            q1[t] = q
            one.append(r * z)
            two.append(z * q)
            three.append(z * w0[t])
        scal[...] = jnp.concatenate(
            [fold(one), fold(two), fold(three), jnp.broadcast_to(sums[6:7], (1, BLOCK)), norm[0:1], none, none, none],
            axis=0,
        )


def last_body(gathered, scal, stat, res, w0, x1, r1, z1, q1, dip, out, *, tiles):
    total = gathered[0]
    for k in range(1, gathered.shape[0]):
        total = total + gathered[k]
    sums = jnp.sum(total, axis=1, keepdims=True)

    def value(x):
        return jnp.broadcast_to(x, (1, BLOCK))

    norm, curve, cross = value(sums[0:1]), value(sums[1:2]), value(sums[2:3])
    along, start = scal[3:4], scal[4:5]
    beta = norm / start
    rate = norm / (curve + 2.0 * beta * cross + beta * beta * along)
    for t in range(tiles):
        at = slice(t * BLOCK, (t + 1) * BLOCK)
        u0 = stat[t][5:6] * res[t][0:3]
        p = z1[t][0:3] + beta * u0
        w = q1[t][0:3] + beta * w0[t][0:3]
        dip[:, at] = x1[t][0:3] + rate * p
        out[:, at] = r1[t][0:3] - rate * w


def swap(x, axes, count):
    got = [x]
    for s in range(1, count):
        got.append(lax.ppermute(x, axes, [(i, i ^ s) for i in range(count)]))
    return got


def gather(x, plane, rows):
    near = jnp.stack(swap(x, ("oct", "sub"), plane))
    return jnp.concatenate(swap(near, "blk", rows), axis=0)


def halo(core, ring):
    count = lax.axis_size(RING)
    size = lax.axis_size("sub")
    got_core = lax.ppermute(core, "sub", [(i, i ^ 1) for i in range(size)])
    pairs = [(i, (i + 1) % count) for i in range(1, count, 2)]
    got_ring = lax.ppermute(ring, RING, pairs + [(b, a) for a, b in pairs])
    return got_core, got_ring


def on_device(positions, polarizability, permanent_field, group_id, pair_mask):
    slabs = lax.axis_size(RING)
    member = lax.axis_index(RING)
    plane = lax.axis_size(("oct", "sub"))
    rows = lax.axis_size("blk")
    atoms = positions.shape[1]
    tiles = atoms // BLOCK
    length_z = layer_gap * atoms * slabs / 256.0
    boxes = BOXES_DEV * slabs
    box_height = length_z / boxes
    reach = (pair_mask.shape[1] - 1) // 2
    surface = 4.0 * math.pi / 3.0 / (side_length * side_length * length_z)
    coeff, picks, nodes = node_tables()
    nodes = jnp.asarray(nodes)
    meta = jnp.reshape(member, (1,)).astype(jnp.int32)
    mask = pair_mask
    tile_shape = (tiles, 8, BLOCK)
    edge = (reach, 8, BLOCK)
    kept = (boxes - 1) * 4 * BLOCK * BLOCK * 4 <= TABLE_LIMIT

    stat, x0, phi, weights, core, ring = call(
        functools.partial(first_body, coeff=coeff, box_height=box_height, tiles=tiles, reach=reach),
        [tile_shape, tile_shape, (tiles, BLOCK, BLOCK), (8, BLOCK), (2 * reach, 8, BLOCK), (2 * reach, 8, BLOCK)],
        [meta, positions, polarizability[None], permanent_field, group_id[None], jnp.asarray(picks)],
        smem=1,
        limit=16 << 20,
        far=True,
        more=[
            pltpu.VMEM((3, atoms), f32),
            pltpu.VMEM((1, atoms), f32),
            pltpu.VMEM((3, atoms), f32),
            pltpu.VMEM((1, atoms), jnp.int32),
            pltpu.VMEM(picks.shape, f32),
            pltpu.SemaphoreType.DMA((5,)),
        ],
    )
    got_core, got_ring = halo(core, ring)
    gathered = gather(weights, plane, rows)

    ranges = [(0, tiles // 2), (tiles // 2, tiles)]
    tabs = []
    for begin, end in ranges:
        count = own_slots(begin, end, tiles, reach)
        tabs += call(
            functools.partial(tensors_body, begin=begin, end=end, tiles=tiles, reach=reach, length_z=length_z),
            [(count, 4, BLOCK, BLOCK)],
            [mask, stat],
            smem=1,
            scratch=[(end - begin, 5, BLOCK, BLOCK)],
            cost=pl.CostEstimate(flops=count * BLOCK * BLOCK * 70, bytes_accessed=1 << 20, transcendentals=count * BLOCK * BLOCK * 2),
            pinned=(0,),
        )
    table = []
    if kept:
        table = call(
            functools.partial(far_tensors_body, box_height=box_height, length_z=length_z),
            [(boxes - 1, 4, BLOCK, BLOCK)],
            [nodes],
            scratch=[(4, BLOCK, BLOCK)],
            cost=pl.CostEstimate(flops=boxes * BLOCK * BLOCK * 28, bytes_accessed=1 << 20, transcendentals=boxes * BLOCK * BLOCK),
            pinned=(0,),
        )
    (halo_tab,) = call(
        functools.partial(halo_tensors_body, tiles=tiles, reach=reach, length_z=length_z),
        [(len(halo_pairs(tiles, reach)), 4, BLOCK, BLOCK)],
        [meta, mask, stat, got_core, got_ring],
        smem=2,
        scratch=[(2 * reach, 5, BLOCK, BLOCK)],
        pinned=(0,),
    )

    def own_field(v):
        return call(
            functools.partial(own_body, ranges=ranges, tiles=tiles, reach=reach),
            [tile_shape],
            [mask, v] + tabs,
            smem=1,
            scratch=[(tiles, 3, BLOCK, BLOCK), (tiles, 3, SUB, BLOCK), (tiles, 3, BLOCK, BLOCK)],
            cost=pl.CostEstimate(flops=72 * 2 * BLOCK * BLOCK * 18, bytes_accessed=1 << 20, transcendentals=0),
        )[0]

    def field(mode, v, gathered, got_core, got_ring, extra):
        near = own_field(v)
        offset = reach if mode == 0 else 0
        outs = [
            [tile_shape, tile_shape, (8, BLOCK), edge, edge],
            [tile_shape, tile_shape, (8, BLOCK), edge, edge, (SUB, BLOCK)],
            [tile_shape] * 4 + [(8, BLOCK)],
        ][mode]
        return call(
            functools.partial(
                field_body, mode=mode, tiles=tiles, reach=reach, plane=plane, slabs=slabs, box_height=box_height,
                length_z=length_z, surface=surface, kept=kept, offset=offset,
            ),
            outs,
            [meta, mask, nodes, stat, v, near, phi, gathered, got_core, got_ring, halo_tab] + table + extra,
            smem=2,
            scratch=[
                (tiles, 3, SUB, BLOCK),
                (2 * reach, 3, BLOCK, BLOCK),
                (boxes, 3, SUB, BLOCK),
                (BOXES_DEV, 3, BLOCK, BLOCK),
                (8, BLOCK, BLOCK) if not kept else (1, 8, BLOCK),
            ],
        )

    r0, u0, weights, core, ring = field(0, x0, gathered, got_core, got_ring, [])
    got_core, got_ring = halo(core, ring)
    gathered = gather(weights, plane, rows)
    w0, u1, weights, core, ring, norm = field(1, u0, gathered, got_core, got_ring, [])
    got_core, got_ring = halo(core, ring)
    gathered = gather(weights, plane, rows)
    x1, r1, z1, q1, scal = field(2, u1, gathered, got_core, got_ring, [x0, r0, w0, norm])
    gathered = gather(scal, plane, rows)
    return call(
        functools.partial(last_body, tiles=tiles),
        [(3, atoms), (3, atoms)],
        [gathered, scal, stat, r0, w0, x1, r1, z1, q1],
    )


def solution(mesh):
    split = P(("groups", "blk", "oct", "sub"))
    wide = P(None, ("groups", "blk", "oct", "sub"))
    return jax.shard_map(
        lambda *args: tuple(on_device(*args)),
        mesh=mesh,
        in_specs=(wide, split, wide, split, P(("groups", "blk", "oct", "sub"), None)),
        out_specs=(wide, wide),
        check_vma=False,
    )
```

```python
import functools
import math

import jax
import jax.numpy as jnp
import numpy as np
from jax import lax
from jax.experimental import pallas as pl
from jax.experimental.pallas import tpu as pltpu
from jax.sharding import PartitionSpec as P

BOXES_DEV = 2
BLOCK = 128
ORDER = 5
NODE_PAD = 128
ITERS = 2
SUB = 8
CHUNK = 32

side_length = 32.0
layer_gap = 2.5
thole_damp = 0.39
highest = lax.Precision.HIGHEST
f32 = jnp.float32
RING = ("blk", "oct", "sub")

VM = pl.BlockSpec(memory_space=pltpu.VMEM)
SM = pl.BlockSpec(memory_space=pltpu.SMEM)
TABLE_LIMIT = 16 << 20


def call(body, outs, args, smem=0, scratch=(), limit=None, cost=None, pinned=(), far=False, more=(), lists=()):
    shapes = [
        pltpu.VMEM(shape, f32) if at in pinned else jax.ShapeDtypeStruct(shape, f32)
        for at, shape in enumerate(outs)
    ] + [jax.ShapeDtypeStruct((size,), jnp.int32) for size in lists]
    return list(pl.pallas_call(
        body,
        out_shape=shapes,
        in_specs=[SM] * smem + [pl.BlockSpec(memory_space=pltpu.HBM) if far else VM] * (len(args) - smem),
        out_specs=[VM] * len(outs) + [SM] * len(lists),
        scratch_shapes=[pltpu.VMEM(shape, f32) for shape in scratch] + list(more),
        compiler_params=pltpu.CompilerParams(vmem_limit_bytes=limit or (12 << 20)),
        cost_estimate=cost,
    )(*args))


def node_tables():
    count = ORDER
    roots = np.cos((2.0 * np.arange(count) + 1.0) * np.pi / (2.0 * count))
    degree = np.arange(count)
    coeff = (
        2.0 / count * np.cos(np.outer(2.0 * np.arange(count) + 1.0, degree) * np.pi / (2.0 * count))
    )
    coeff = np.where(degree[None, :] == 0, 1.0 / count, coeff)
    index = np.arange(NODE_PAD)
    live = index < count**3
    safe = np.where(live, index, 0)
    levels = np.stack([safe // (count * count), safe // count % count, safe % count])
    picks = (levels[:, :, None] == np.arange(8)) * 1.0
    picks[0] *= live[:, None]
    nodes = np.zeros((8, NODE_PAD))
    nodes[0] = 0.5 * (1.0 + roots[levels[0]])
    nodes[1] = 0.5 * (1.0 + roots[levels[1]])
    nodes[2] = 0.5 * roots[levels[2]]
    return coeff.astype(np.float32), picks.astype(np.float32), nodes.astype(np.float32)


def wrap_unit(delta):
    return (delta - jnp.floor(delta + 0.5)) * side_length


def wrap_z(delta, length_z):
    return delta - length_z * jnp.floor(delta * (1.0 / length_z) + 0.5)


def tensor(five, three, dx, dy, dz):
    five = jnp.maximum(five, 1e-36)
    root = five * lax.rsqrt(five)
    return (root * dx, root * dy, root * dz, three)


def columns(tiles, count, out):
    for t, tile in enumerate(tiles):
        if tile.shape[0] < 8:
            tile = jnp.concatenate([tile, jnp.zeros((8 - tile.shape[0], BLOCK), f32)], axis=0)
        turned = tile.T
        for k in range(count):
            out[t, k] = jnp.broadcast_to(turned[:, k : k + 1], (BLOCK, BLOCK))


def diagonal(step):
    row = lax.broadcasted_iota(jnp.int32, (SUB, BLOCK), 0)
    lane = lax.broadcasted_iota(jnp.int32, (SUB, BLOCK), 1)
    return lane - row == step * SUB


def spread(tile, k):
    return jnp.broadcast_to(tile[k : k + 1, :], (SUB, BLOCK))


def row_sum(x):
    return jnp.sum(x, axis=0, keepdims=True)


def build_pair(col, rows, put, length_z):
    wide = [jnp.broadcast_to(r, (CHUNK, BLOCK)) for r in rows]
    for step in range(BLOCK // CHUNK):
        at = slice(step * CHUNK, (step + 1) * CHUNK)
        dx = wrap_unit(col(0, at) - wide[0])
        dy = wrap_unit(col(1, at) - wide[1])
        dz = wrap_z(col(2, at) - wide[2], length_z)
        keep = col(4, at) != wide[4]
        dist = jnp.where(keep, dx * dx + dy * dy + dz * dz, 1e24)
        inv = lax.rsqrt(dist)
        inv_two = inv * inv
        inv_three = inv * inv_two
        s = dist * (dist * inv) * (col(3, at) * wide[3])
        decay = jnp.exp(-s)
        small = s * (1.0 - s * (0.5 - s * (1.0 / 6.0 - s * (1.0 / 24.0))))
        three = jnp.where(s < 0.015625, small, 1.0 - decay)
        five = (three - s * decay) * (3.0 * inv_two * inv_three)
        for k, value in enumerate(tensor(five, three * inv_three, dx, dy, dz)):
            put(k, at, value)


def lane_sums(parts):
    total = None
    for step, x in enumerate(parts):
        term = jnp.where(diagonal(step), jnp.sum(x, axis=1, keepdims=True), 0.0)
        total = term if total is None else total + term
    return total


def project(phi, v, tiles):
    out = []
    per = tiles // BOXES_DEV
    for box in range(BOXES_DEV):
        wide = [[spread(v[box * per + t], c) for c in range(3)] for t in range(per)]
        parts = [[], [], []]
        for step in range(BLOCK // SUB):
            at = slice(step * SUB, (step + 1) * SUB)
            sums = [None] * 3
            for t in range(per):
                value = phi[box * per + t, at, :]
                for c in range(3):
                    term = value * wide[t][c]
                    sums[c] = term if sums[c] is None else sums[c] + term
            for c in range(3):
                parts[c].append(sums[c])
        out += [row_sum(lane_sums(p)) for p in parts]
    return out


def pack(weights, tiles, reach, get, payload, both):
    payload[0] = weights
    for k in range(reach):
        low, high = get(k), get(tiles - reach + k)
        if both:
            rows = [low[0:3], high[0:3], jnp.zeros((2, BLOCK), f32)]
            payload[1 + k] = jnp.concatenate(rows, axis=0)
        else:
            payload[1 + k] = low
            payload[1 + reach + k] = high


def relay_body(meta, *rest, plane, reach):
    got, (out, held) = rest[:plane], rest[-2:]
    count = held.shape[1]
    for i in range(plane):
        out[i] = got[i][0]
        for k in range(count):
            held[i, k] = got[i][1 + k]
    own = meta[0] % plane
    last = lax.bitwise_xor(own, plane - 1)
    for k in range(count):
        low, high = held[own, k], held[last, k]
        if count == reach:
            out[plane + k] = jnp.concatenate([low[0:3], high[3:6], low[6:8]], axis=0)
        else:
            out[plane + k] = low if k < reach else high


def halo_tiles(meta, near, wide, held, plane, slabs, reach):
    count = held.shape[1]
    for i, ref in enumerate(near):
        for k in range(count):
            held[i, k] = ref[1 + k]
    for i, ref in enumerate(wide):
        for k in range(count):
            held[plane + i, k] = ref[plane + k]
    own_row, own_col = meta[0] // plane, meta[0] % plane
    rows = slabs // plane
    below = jnp.where(own_row == 0, rows - 1, own_row - 1)
    above = jnp.where(own_row == rows - 1, 0, own_row + 1)
    low = jnp.where(
        own_col > 0,
        lax.bitwise_xor(own_col, jnp.maximum(own_col - 1, 0)),
        plane + lax.bitwise_xor(own_row, below),
    )
    high = jnp.where(
        own_col < plane - 1,
        lax.bitwise_xor(own_col, jnp.minimum(own_col + 1, plane - 1)),
        plane + lax.bitwise_xor(own_row, above),
    )
    if count == reach:
        return [held[low, k][3:6] for k in range(reach)] + [held[high, k][0:3] for k in range(reach)]
    return [held[low, reach + k] for k in range(reach)] + [held[high, k] for k in range(reach)]


def first_body(
    meta, pos_in, alpha_in, field_in, gid_in, picks_in, stat, x0, phi, payload,
    pos, alpha, field, gid, picks, sems, *, coeff, box_height, tiles, reach
):
    pairs = [(pos_in, pos), (alpha_in, alpha), (field_in, field), (gid_in, gid), (picks_in, picks)]
    copies = [pltpu.make_async_copy(a, b, sems.at[k]) for k, (a, b) in enumerate(pairs)]
    for copy in copies:
        copy.start()
    for copy in copies:
        copy.wait()
    total = tiles * BLOCK
    lane = lax.broadcasted_iota(jnp.int32, (1, total), 1)
    first = meta[0] * BOXES_DEV
    box = jnp.where(lane < total // BOXES_DEV, first, first + 1).astype(f32)
    p = pos[...]
    al = alpha[...]
    coords = [
        p[0:1] / 16.0 - 1.0,
        p[1:2] / 16.0 - 1.0,
        2.0 * (p[2:3] - box * box_height) / box_height - 1.0,
    ]
    levels = []
    for u in coords:
        terms = [None, u]
        for degree in range(2, ORDER):
            prev = terms[-2] if degree > 2 else 1.0
            terms.append(2.0 * u * terms[-1] - prev)
        rows = []
        for k in range(ORDER):
            value = float(coeff[k, 0]) + float(coeff[k, 1]) * terms[1]
            for n in range(2, ORDER):
                value = value + float(coeff[k, n]) * terms[n]
            rows.append(value)
        levels.append(jnp.concatenate(rows + [jnp.zeros((8 - ORDER, total), f32)], axis=0))
    wide = 4 * BLOCK
    for begin in range(0, total, wide):
        value = None
        for d in range(3):
            part = jnp.dot(
                picks[d], levels[d][:, begin : begin + wide], precision=highest, preferred_element_type=f32
            )
            value = part if value is None else value * part
        for t in range(4):
            phi[begin // BLOCK + t] = value[:, t * BLOCK : (t + 1) * BLOCK]
    start = al * field[...]
    scaled = jnp.concatenate(
        [
            p[0:2] * (1.0 / side_length),
            p[2:3],
            lax.rsqrt(al) * math.sqrt(thole_damp),
            gid[...].astype(f32),
            al,
            jnp.zeros((2, total), f32),
        ],
        axis=0,
    )
    vec = jnp.concatenate([start, jnp.zeros((5, total), f32)], axis=0)
    for t in range(tiles):
        stat[t] = scaled[:, t * BLOCK : (t + 1) * BLOCK]
        x0[t] = vec[:, t * BLOCK : (t + 1) * BLOCK]
    rows = project(phi, x0, tiles)
    weights = jnp.concatenate(rows + [jnp.zeros((2, BLOCK), f32)], axis=0)

    def get(k):
        return jnp.concatenate([stat[k][0:5], x0[k][0:3]], axis=0)

    pack(weights, tiles, reach, get, payload, False)


def own_slot(b, begin, tiles, reach):
    k = jnp.maximum(b - (tiles - reach), 0)
    return (b - begin) * (reach + 1) - k * (k + 1) // 2


def own_slots(begin, end, tiles, reach):
    return sum(min(reach + 1, tiles - b) for b in range(begin, end))


def walk(codes, begin, end, visit):
    def step(at, code):
        later = codes[at + 1]
        visit(code)
        return later

    lax.fori_loop(begin, end, step, codes[begin])


def unpack(code):
    return code & 255, (code >> 8) & 255, code >> 16


def tensors_body(mask, stat, out, own_list, halo_list, col, *, half, tiles, reach, length_z):
    last = own_list.shape[0] - 2
    n = jnp.int32(0)
    for b in range(tiles):
        if b == half:
            own_list[last] = n
        k = max(b - (tiles - reach), 0)
        slot = b * (reach + 1) - k * (k + 1) // 2
        for o in range(1, min(reach + 1, tiles - b)):
            own_list[n] = jnp.int32(slot + o + (b << 8) + ((b + o) << 16))
            n = n + mask[b, reach + o]
    own_list[last + 1] = n
    m = jnp.int32(0)
    for index, (h, c, at) in enumerate(halo_pairs(tiles, reach)):
        halo_list[m] = jnp.int32(index + (h << 8) + (c << 16))
        m = m + mask[c, at]
    halo_list[halo_list.shape[0] - 1] = m
    columns([stat[t] for t in range(tiles)], 5, col)

    def visit(at, unused):
        slot, b, other = unpack(own_list[jnp.maximum(at - tiles, 0)])
        alone = at < tiles
        slot = jnp.where(alone, own_slot(at, 0, tiles, reach), slot)
        b = jnp.where(alone, at, b)
        tile = stat[jnp.where(alone, at, other)]
        rows = [tile[k : k + 1, :] for k in range(5)]

        def store(k, at, value):
            out[slot, k, at, :] = value

        build_pair(lambda k, at: col[b, k, at, :], rows, store, length_z)
        return unused

    lax.fori_loop(0, tiles + n, visit, 0)


def own_body(codes, v, tab, *rest, begin, end, tiles, reach):
    out, acc_i, acc_j, col, wide = rest[-5:]
    top = min(end + reach, tiles)
    columns([v[t] for t in range(begin, end)], 3, col)
    for t in range(top - begin):
        for c in range(3):
            acc_j[t, c] = jnp.zeros((SUB, BLOCK), f32)
            wide[t, c] = spread(v[begin + t], c)

    def pair(b, other, slot, both):
        at_b, at_o = b - begin, other - begin
        vec = [wide[at_o, c] for c in range(3)]
        acc = [acc_j[at_o, c] for c in range(3)] if both else None
        for step in range(BLOCK // SUB):
            at = slice(step * SUB, (step + 1) * SUB)
            t = [tab[slot, k, at, :] for k in range(4)]
            new = apply_tensor(t, vec)
            for c in range(3):
                if both:
                    acc_i[at_b, c, at, :] += new[c]
                else:
                    acc_i[at_b, c, at, :] = new[c]
            if both:
                new = apply_tensor(t, [col[at_b, c, at, :] for c in range(3)])
                acc = [a + n for a, n in zip(acc, new)]
        if both:
            for c in range(3):
                acc_j[at_o, c] = acc[c]

    def alone(b, unused):
        pair(b, b, own_slot(b, 0, tiles, reach), False)
        return unused

    lax.fori_loop(begin, end, alone, 0)
    last = codes.shape[0] - 2

    def visit(code):
        slot, b, other = unpack(code)
        pair(b, other, slot, True)

    walk(codes, codes[last] if begin else 0, codes[last + 1] if begin else codes[last], visit)
    for t in range(top - begin):
        rows = []
        for c in range(3):
            total = acc_j[t, c]
            if t < end - begin:
                parts = [acc_i[t, c, k * SUB : (k + 1) * SUB, :] for k in range(BLOCK // SUB)]
                total = total + lane_sums(parts)
            rows.append(row_sum(total))
        out[t] = jnp.concatenate(rows + [jnp.zeros((5, BLOCK), f32)], axis=0)


def halo_pairs(tiles, reach):
    pairs = []
    for l in range(reach):
        for c in range(l + 1):
            pairs.append((l, c, l - c))
    for l in range(reach):
        for c in range(tiles - reach + l, tiles):
            pairs.append((reach + l, c, reach + tiles + l - c))
    return pairs


def halo_tensors_body(meta, codes, stat, *rest, tiles, plane, slabs, reach, length_z):
    rows = slabs // plane
    near, wide = rest[:plane], rest[plane : plane + rows]
    out, first, col, held = rest[plane + rows :]
    halo = halo_tiles(meta, near, wide, held, plane, slabs, reach)
    for k, tile in enumerate(halo):
        first[k] = tile
    columns(halo, 5, col)
    def visit(code):
        index, h, c = unpack(code)
        own = stat[c]
        own_rows = [own[k : k + 1, :] for k in range(5)]

        def store(k, at, value):
            out[index, k, at, :] = value

        build_pair(lambda k, at: col[h, k, at, :], own_rows, store, length_z)

    walk(codes, 0, codes[codes.shape[0] - 1], visit)


def far_geometry(nodes, geo, box_height):
    turned = nodes[...].T
    row = nodes[...]

    def delta(k):
        return jnp.broadcast_to(turned[:, k : k + 1], (BLOCK, BLOCK)) - jnp.broadcast_to(
            row[k : k + 1, :], (BLOCK, BLOCK)
        )

    dx, dy = wrap_unit(delta(0)), wrap_unit(delta(1))
    geo[0] = dx
    geo[1] = dy
    geo[2] = box_height * delta(2)
    geo[3] = dx * dx + dy * dy + box_height * box_height


def far_tensor(geo, apart, put, box_height, length_z):
    for step in range(BLOCK // CHUNK):
        at = slice(step * CHUNK, (step + 1) * CHUNK)
        dx, dy = geo[0, at, :], geo[1, at, :]
        dz = wrap_z(geo[2, at, :] - apart * box_height, length_z)
        inv = lax.rsqrt(geo[3, at, :] + dz * dz)
        inv_two = inv * inv
        three = inv * inv_two
        five = 3.0 * three * inv_two
        for k, value in enumerate(tensor(five, three, dx, dy, dz)):
            put(k, at, value)


def far_tensors_body(nodes, out, geo, *, box_height, length_z):
    far_geometry(nodes, geo, box_height)

    def visit(d, unused):
        def put(k, at, value):
            out[d - 1, k, at, :] = value

        far_tensor(geo, d.astype(f32), put, box_height, length_z)
        return unused

    lax.fori_loop(1, out.shape[0] + 1, visit, 0)


def apply_tensor(t, v):
    ex, ey, ez, three = t
    x, y, z = v
    along = ex * x + ey * y + ez * z
    return (ex * along - three * x, ey * along - three * y, ez * along - three * z)


def far_nodes(table, geo, wide, fcol, boxes, box_height, length_z):
    if table is not None:
        def rows(step, unused):
            ats = [pl.ds(pl.multiple_of(step * 2 * SUB + k * SUB, SUB), SUB) for k in range(2)]

            def load(d):
                return [[table[d - 1, k, at, :] for k in range(4)] for at in ats]

            def field(ts, k):
                v = [wide[k, c] for c in range(3)]
                return sum([apply_tensor(t, v) for t in ts], ())

            acc = field(load(boxes - 1), boxes - 1) + field(load(1), 2)
            for d in range(2, boxes - 1):
                ts = load(d)
                new = field(ts, d) + field(ts, d + 1)
                acc = tuple(a + n for a, n in zip(acc, new))
            for box in range(BOXES_DEV):
                for half in range(2):
                    for c in range(3):
                        fcol[box, c, ats[half], :] = jnp.broadcast_to(
                            jnp.sum(acc[box * 6 + half * 3 + c], axis=1, keepdims=True), (SUB, BLOCK)
                        )
            return unused

        lax.fori_loop(0, BLOCK // (2 * SUB), rows, 0)
        return
    for box in range(BOXES_DEV):
        for c in range(3):
            fcol[box, c] = jnp.zeros((BLOCK, BLOCK), f32)

    def visit(d, unused):
        def hold(k, at, value):
            geo[4 + k, at, :] = value

        far_tensor(geo, d.astype(f32), hold, box_height, length_z)
        for box in range(BOXES_DEV):

            @pl.when(d < boxes - 1 if box else d > 1)
            def _():
                v = [wide[d + box, c] for c in range(3)]

                def part(step, skip):
                    at = pl.ds(pl.multiple_of(step * SUB, SUB), SUB)
                    new = apply_tensor([geo[4 + k, at, :] for k in range(4)], v)
                    for c in range(3):
                        fcol[box, c, at, :] += new[c]
                    return skip

                lax.fori_loop(0, BLOCK // SUB, part, 0)

        return unused

    lax.fori_loop(1, boxes, visit, 0)
    for box in range(BOXES_DEV):
        for c in range(3):
            fcol[box, c] = jnp.broadcast_to(
                jnp.sum(fcol[box, c], axis=1, keepdims=True), (BLOCK, BLOCK)
            )


def field_body(meta, codes, nodes, stat, v, phi, halo_tab, *rest,
               mode, tiles, reach, plane, slabs, box_height, length_z, surface, kept, half):
    rest = list(rest)

    def take(count):
        return [rest.pop(0) for _ in range(count)]

    rows = slabs // plane
    parts = take(2)
    near = take(plane) if mode else []
    bundles = take(rows)
    first = None if mode else take(1)[0]
    table = take(1)[0] if kept else None
    extra = take((0, 0, 4)[mode])
    outs = take((3, 4, 5)[mode])
    acc, col, wide, fcol, geo, held = rest
    boxes = slabs * BOXES_DEV
    member = meta[0]
    own_row, own_col = member // plane, member % plane

    total = jnp.zeros((SUB, BLOCK), f32)
    for i in range(rows):
        for j in range(plane):
            tile = bundles[i][j]
            total = total + tile
            other = lax.bitwise_xor(own_row, i) * plane + lax.bitwise_xor(own_col, j) - member
            k = jnp.where(other < 0, other + slabs, other) * BOXES_DEV
            for box in range(BOXES_DEV):
                for c in range(3):
                    wide[k + box, c] = spread(tile, box * 3 + c)
    sums = jnp.sum(total, axis=1, keepdims=True)
    moment = [surface * (sums[c : c + 1] + sums[3 + c : 4 + c]) for c in range(3)]

    if mode:
        halo = halo_tiles(meta, near, bundles, held, plane, slabs, reach)
    else:
        halo = [first[k][5:8] for k in range(2 * reach)]
    columns(halo, 3, col)
    for t in range(tiles):
        for c in range(3):
            acc[t, c] = jnp.zeros((SUB, BLOCK), f32)
    def visit(code):
        index, h, c = unpack(code)
        sofar = [acc[c, k] for k in range(3)]
        for step in range(BLOCK // SUB):
            at = slice(step * SUB, (step + 1) * SUB)
            new = apply_tensor(
                [halo_tab[index, k, at, :] for k in range(4)], [col[h, k, at, :] for k in range(3)]
            )
            sofar = [a + n for a, n in zip(sofar, new)]
        for k in range(3):
            acc[c, k] = sofar[k]

    walk(codes, 0, codes[codes.shape[0] - 1], visit)

    if not kept:
        far_geometry(nodes, geo, box_height)
    far_nodes(table, geo, wide, fcol, boxes, box_height, length_z)

    per = tiles // BOXES_DEV
    zero = jnp.zeros((5, BLOCK), f32)
    fields = []
    for t in range(tiles):
        box = t // per
        sofar = [acc[t, c] for c in range(3)]
        for step in range(BLOCK // SUB):
            at = slice(step * SUB, (step + 1) * SUB)
            value = phi[t, at, :]
            sofar = [a + value * fcol[box, c, at, :] for c, a in enumerate(sofar)]
        rows = [row_sum(a) - m for a, m in zip(sofar, moment)]
        value = jnp.concatenate(rows + [zero], axis=0)
        if t < parts[0].shape[0]:
            value = value + parts[0][t]
        if t >= half:
            value = value + parts[1][t - half]
        fields.append(value)

    def alpha(t):
        return spread(stat[t], 5)

    none = jnp.zeros((1, BLOCK), f32)

    def send(u, payload, scalar):
        weights = jnp.concatenate(project(phi, u, tiles) + [scalar, none], axis=0)
        pack(weights, tiles, reach, lambda k: u[k], payload, True)

    def fold(terms):
        out = terms[0]
        for x in terms[1:]:
            out = out + x
        return row_sum(out)

    if mode == 0:
        res, u, payload = outs
        dots = []
        for t in range(tiles):
            scaled = alpha(t) * fields[t]
            res[t] = fields[t]
            u[t] = scaled
            dots.append(scaled * fields[t])
        send(u, payload, fold(dots))
    elif mode == 1:
        image, u, payload, norm = outs
        dots = []
        for t in range(tiles):
            w = v[t] / alpha(t) - fields[t]
            image[t] = w
            u[t] = alpha(t) * w
            dots.append(v[t] * w)
        norm[...] = jnp.broadcast_to(sums[6:7], (SUB, BLOCK))
        send(u, payload, fold(dots))
    else:
        first, res, w0, norm = extra
        x1, r1, z1, q1, scal = outs
        rate = norm[...] / jnp.broadcast_to(sums[6:7], (SUB, BLOCK))
        one, two, three = [], [], []
        for t in range(tiles):
            y = v[t] / alpha(t) - fields[t]
            r = res[t] - rate * w0[t]
            z = alpha(t) * r
            q = w0[t] - rate * y
            x1[t] = first[t] + rate * (alpha(t) * res[t])
            r1[t] = r
            z1[t] = z
            q1[t] = q
            one.append(r * z)
            two.append(z * q)
            three.append(z * w0[t])
        scal[...] = jnp.concatenate(
            [fold(one), fold(two), fold(three), jnp.broadcast_to(sums[6:7], (1, BLOCK)), norm[0:1], none, none, none],
            axis=0,
        )


def last_body(scal, stat, res, w0, x1, r1, z1, q1, *rest, tiles):
    gathered, (dip, out) = rest[:-2], rest[-2:]
    total = gathered[0][...]
    for ref in gathered[1:]:
        total = total + ref[...]
    sums = jnp.sum(total, axis=1, keepdims=True)

    def value(x):
        return jnp.broadcast_to(x, (1, BLOCK))

    norm, curve, cross = value(sums[0:1]), value(sums[1:2]), value(sums[2:3])
    along, start = scal[3:4], scal[4:5]
    beta = norm / start
    rate = norm / (curve + 2.0 * beta * cross + beta * beta * along)
    for t in range(tiles):
        at = slice(t * BLOCK, (t + 1) * BLOCK)
        u0 = stat[t][5:6] * res[t][0:3]
        p = z1[t][0:3] + beta * u0
        w = q1[t][0:3] + beta * w0[t][0:3]
        dip[:, at] = x1[t][0:3] + rate * p
        out[:, at] = r1[t][0:3] - rate * w


def swap(x, axes, count):
    got = [x]
    for s in range(1, count):
        got.append(lax.ppermute(x, axes, [(i, i ^ s) for i in range(count)]))
    return got


def on_device(positions, polarizability, permanent_field, group_id, pair_mask):
    slabs = lax.axis_size(RING)
    member = lax.axis_index(RING)
    plane = lax.axis_size(("oct", "sub"))
    rows = lax.axis_size("blk")
    atoms = positions.shape[1]
    tiles = atoms // BLOCK
    length_z = layer_gap * atoms * slabs / 256.0
    boxes = BOXES_DEV * slabs
    box_height = length_z / boxes
    reach = (pair_mask.shape[1] - 1) // 2
    surface = 4.0 * math.pi / 3.0 / (side_length * side_length * length_z)
    coeff, picks, nodes = node_tables()
    nodes = jnp.asarray(nodes)
    meta = jnp.reshape(member, (1,)).astype(jnp.int32)
    mask = pair_mask
    tile_shape = (tiles, 8, BLOCK)
    kept = (boxes - 1) * 4 * BLOCK * BLOCK * 4 <= TABLE_LIMIT

    half = tiles // 2

    def far_memory(x):
        return pltpu.with_memory_space_constraint(x, pltpu.HBM)

    stat, x0, phi, payload = call(
        functools.partial(first_body, coeff=coeff, box_height=box_height, tiles=tiles, reach=reach),
        [tile_shape, tile_shape, (tiles, BLOCK, BLOCK), (1 + 2 * reach, 8, BLOCK)],
        [meta] + [far_memory(x) for x in (positions, polarizability[None], permanent_field, group_id[None], jnp.asarray(picks))],
        smem=1,
        limit=16 << 20,
        far=True,
        more=[
            pltpu.VMEM((3, atoms), f32),
            pltpu.VMEM((1, atoms), f32),
            pltpu.VMEM((3, atoms), f32),
            pltpu.VMEM((1, atoms), jnp.int32),
            pltpu.VMEM(picks.shape, f32),
            pltpu.SemaphoreType.DMA((5,)),
        ],
    )
    count = own_slots(0, tiles, tiles, reach)
    tab, own_list, halo_list = call(
        functools.partial(tensors_body, half=half, tiles=tiles, reach=reach, length_z=length_z),
        [(count, 4, BLOCK, BLOCK)],
        [mask, stat],
        smem=1,
        scratch=[(tiles, 5, BLOCK, BLOCK)],
        cost=pl.CostEstimate(flops=count * BLOCK * BLOCK * 70, bytes_accessed=1 << 20, transcendentals=count * BLOCK * BLOCK * 2),
        pinned=(0,),
        lists=(count - tiles + 2, len(halo_pairs(tiles, reach)) + 1),
    )
    table = []
    if kept:
        table = call(
            functools.partial(far_tensors_body, box_height=box_height, length_z=length_z),
            [(boxes - 1, 4, BLOCK, BLOCK)],
            [nodes],
            scratch=[(4, BLOCK, BLOCK)],
            cost=pl.CostEstimate(flops=boxes * BLOCK * BLOCK * 28, bytes_accessed=1 << 20, transcendentals=boxes * BLOCK * BLOCK),
            pinned=(0,),
        )

    def own_field(v, begin, end, after):
        top = min(end + reach, tiles) - begin
        return call(
            functools.partial(own_body, begin=begin, end=end, tiles=tiles, reach=reach),
            [(top, 8, BLOCK)],
            [own_list, v, tab] + after,
            smem=1,
            scratch=[
                (end - begin, 3, BLOCK, BLOCK),
                (top, 3, SUB, BLOCK),
                (end - begin, 3, BLOCK, BLOCK),
                (top, 3, SUB, BLOCK),
            ],
            cost=pl.CostEstimate(flops=72 * BLOCK * BLOCK * 18, bytes_accessed=1 << 20, transcendentals=0),
        )[0]

    def exchange(payload, v):
        near = swap(payload, ("oct", "sub"), plane)
        first = own_field(v, 0, half, [])
        bundle = call(
            functools.partial(relay_body, plane=plane, reach=reach),
            [(plane + payload.shape[0] - 1, 8, BLOCK)],
            [meta] + near + [first],
            smem=1,
            scratch=[(plane, payload.shape[0] - 1, 8, BLOCK)],
        )[0]
        bundles = swap(bundle, "blk", rows)
        second = own_field(v, half, tiles, [bundle])
        return [first, second], near, bundles

    def field(mode, v, parts, near, bundles, extra):
        outs = [
            [tile_shape, tile_shape, (1 + reach, 8, BLOCK)],
            [tile_shape, tile_shape, (1 + reach, 8, BLOCK), (SUB, BLOCK)],
            [tile_shape] * 4 + [(8, BLOCK)],
        ][mode]
        return call(
            functools.partial(
                field_body, mode=mode, tiles=tiles, reach=reach, plane=plane, slabs=slabs, box_height=box_height,
                length_z=length_z, surface=surface, kept=kept, half=half,
            ),
            outs,
            [meta, halo_list, nodes, stat, v, phi, halo_tab] + parts + (near if mode else []) + bundles
            + ([] if mode else [edge]) + table + extra,
            smem=2,
            scratch=[
                (tiles, 3, SUB, BLOCK),
                (2 * reach, 3, BLOCK, BLOCK),
                (boxes, 3, SUB, BLOCK),
                (BOXES_DEV, 3, BLOCK, BLOCK),
                (8, BLOCK, BLOCK) if not kept else (1, 8, BLOCK),
                (plane + rows, reach, 8, BLOCK),
            ],
        )

    parts, near, bundles = exchange(payload, x0)
    halo_tab, edge = call(
        functools.partial(
            halo_tensors_body, tiles=tiles, plane=plane, slabs=slabs, reach=reach, length_z=length_z
        ),
        [(len(halo_pairs(tiles, reach)), 4, BLOCK, BLOCK), (2 * reach, 8, BLOCK)],
        [meta, halo_list, stat] + near + bundles,
        smem=2,
        scratch=[(2 * reach, 5, BLOCK, BLOCK), (plane + rows, 2 * reach, 8, BLOCK)],
        pinned=(0,),
    )
    r0, u0, payload = field(0, x0, parts, near, bundles, [])
    parts, near, bundles = exchange(payload, u0)
    w0, u1, payload, norm = field(1, u0, parts, near, bundles, [])
    parts, near, bundles = exchange(payload, u1)
    x1, r1, z1, q1, scal = field(2, u1, parts, near, bundles, [x0, r0, w0, norm])
    sums = swap(scal, ("oct", "sub"), plane)
    sums = swap(functools.reduce(jnp.add, sums), "blk", rows)
    return call(
        functools.partial(last_body, tiles=tiles),
        [(3, atoms), (3, atoms)],
        [scal, stat, r0, w0, x1, r1, z1, q1] + sums,
    )


def solution(mesh):
    split = P(("groups", "blk", "oct", "sub"))
    wide = P(None, ("groups", "blk", "oct", "sub"))
    return jax.shard_map(
        lambda *args: tuple(on_device(*args)),
        mesh=mesh,
        in_specs=(wide, split, wide, split, P(("groups", "blk", "oct", "sub"), None)),
        out_specs=(wide, wide),
        check_vma=False,
    )
```

```python
import functools
import math

import jax
import jax.numpy as jnp
import numpy as np
from jax import lax
from jax.experimental import pallas as pl
from jax.experimental.pallas import tpu as pltpu
from jax.sharding import PartitionSpec as P

BOXES_DEV = 2
BLOCK = 128
ORDER = 5
NODE_PAD = 128
ITERS = 2
SUB = 8
CHUNK = 8

side_length = 32.0
layer_gap = 2.5
thole_damp = 0.39
highest = lax.Precision.HIGHEST
f32 = jnp.float32
RING = ("blk", "oct", "sub")

VM = pl.BlockSpec(memory_space=pltpu.VMEM)
SM = pl.BlockSpec(memory_space=pltpu.SMEM)
FAR = pl.BlockSpec(memory_space=pltpu.HBM)
TABLE_LIMIT = 16 << 20


def call(body, outs, args, smem=0, scratch=(), limit=None, cost=None, pinned=(), far=0, more=(), lists=()):
    shapes = [
        pltpu.VMEM(shape, f32) if at in pinned else jax.ShapeDtypeStruct(shape, f32)
        for at, shape in enumerate(outs)
    ] + [jax.ShapeDtypeStruct((size,), jnp.int32) for size in lists]
    return list(pl.pallas_call(
        body,
        out_shape=shapes,
        in_specs=[SM] * smem + [FAR] * far + [VM] * (len(args) - smem - far),
        out_specs=[VM] * len(outs) + [SM] * len(lists),
        scratch_shapes=[pltpu.VMEM(shape, f32) for shape in scratch] + list(more),
        compiler_params=pltpu.CompilerParams(vmem_limit_bytes=limit or (12 << 20)),
        cost_estimate=cost,
    )(*args))


def node_tables():
    count = ORDER
    roots = np.cos((2.0 * np.arange(count) + 1.0) * np.pi / (2.0 * count))
    degree = np.arange(count)
    coeff = (
        2.0 / count * np.cos(np.outer(2.0 * np.arange(count) + 1.0, degree) * np.pi / (2.0 * count))
    )
    coeff = np.where(degree[None, :] == 0, 1.0 / count, coeff)
    index = np.arange(NODE_PAD)
    live = index < count**3
    safe = np.where(live, index, 0)
    levels = np.stack([safe // (count * count), safe // count % count, safe % count])
    picks = np.zeros((3, NODE_PAD, count, 8))
    for d in range(3):
        picks[d, index, levels[d], d] = 1.0
    picks[0] *= live[:, None, None]
    picks = picks.reshape(3 * NODE_PAD, count * 8)
    nodes = np.zeros((8, NODE_PAD))
    nodes[0] = 0.5 * (1.0 + roots[levels[0]])
    nodes[1] = 0.5 * (1.0 + roots[levels[1]])
    nodes[2] = 0.5 * roots[levels[2]]
    return coeff.astype(np.float32), picks.astype(np.float32), nodes.astype(np.float32)


def wrap_unit(delta):
    return (delta - jnp.floor(delta + 0.5)) * side_length


def wrap_z(delta, length_z):
    return delta - length_z * jnp.floor(delta * (1.0 / length_z) + 0.5)


def tensor(five, three, dx, dy, dz):
    five = jnp.maximum(five, 1e-36)
    root = five * lax.rsqrt(five)
    return (root * dx, root * dy, root * dz, three)


def columns(tiles, count, out):
    for t, tile in enumerate(tiles):
        for k in range(count):
            out[t, k] = jnp.broadcast_to(tile[k : k + 1, :], (BLOCK, BLOCK)).T


def diagonal(step):
    row = lax.broadcasted_iota(jnp.int32, (SUB, BLOCK), 0)
    lane = lax.broadcasted_iota(jnp.int32, (SUB, BLOCK), 1)
    return lane - row == step * SUB


def spread(tile, k):
    return jnp.broadcast_to(tile[k : k + 1, :], (SUB, BLOCK))


def row_sum(x):
    return jnp.sum(x, axis=0, keepdims=True)


def build_pair(col, rows, put, length_z):
    wide = [jnp.broadcast_to(r, (CHUNK, BLOCK)) for r in rows]
    for step in range(BLOCK // CHUNK):
        at = slice(step * CHUNK, (step + 1) * CHUNK)
        dx = wrap_unit(col(0, at) - wide[0])
        dy = wrap_unit(col(1, at) - wide[1])
        dz = wrap_z(col(2, at) - wide[2], length_z)
        keep = col(4, at) != wide[4]
        dist = jnp.where(keep, dx * dx + dy * dy + dz * dz, 1e24)
        inv = lax.rsqrt(dist)
        inv_two = inv * inv
        inv_three = inv * inv_two
        s = dist * (dist * inv) * (col(3, at) * wide[3])
        decay = jnp.exp(-s)
        small = s * (1.0 - s * (0.5 - s * (1.0 / 6.0 - s * (1.0 / 24.0))))
        three = jnp.where(s < 0.015625, small, 1.0 - decay)
        five = (three - s * decay) * (3.0 * inv_two * inv_three)
        for k, value in enumerate(tensor(five, three * inv_three, dx, dy, dz)):
            put(k, at, value)


def lane_sums(parts):
    total = None
    for step, x in enumerate(parts):
        term = jnp.where(diagonal(step), jnp.sum(x, axis=1, keepdims=True), 0.0)
        total = term if total is None else total + term
    return total


def project(phi, v, tiles):
    out = []
    per = tiles // BOXES_DEV
    for box in range(BOXES_DEV):
        wide = [[spread(v[box * per + t], c) for c in range(3)] for t in range(per)]
        parts = [[], [], []]
        for step in range(BLOCK // SUB):
            at = slice(step * SUB, (step + 1) * SUB)
            sums = [None] * 3
            for t in range(per):
                value = phi[box * per + t, at, :]
                for c in range(3):
                    term = value * wide[t][c]
                    sums[c] = term if sums[c] is None else sums[c] + term
            for c in range(3):
                parts[c].append(sums[c])
        out += [row_sum(lane_sums(p)) for p in parts]
    return out


def pack(weights, tiles, reach, get, payload, both):
    payload[0] = weights
    for k in range(reach):
        low, high = get(k), get(tiles - reach + k)
        if both:
            rows = [low[0:3], high[0:3], jnp.zeros((2, BLOCK), f32)]
            payload[1 + k] = jnp.concatenate(rows, axis=0)
        else:
            payload[1 + k] = low
            payload[1 + reach + k] = high


def relay_body(meta, *rest, plane, reach):
    got, (out, held) = rest[:plane], rest[-2:]
    count = held.shape[1]
    for i in range(plane):
        out[i] = got[i][0]
        for k in range(count):
            held[i, k] = got[i][1 + k]
    own = meta[0] % plane
    last = lax.bitwise_xor(own, plane - 1)
    for k in range(count):
        low, high = held[own, k], held[last, k]
        if count == reach:
            out[plane + k] = jnp.concatenate([low[0:3], high[3:6], low[6:8]], axis=0)
        else:
            out[plane + k] = low if k < reach else high


def halo_tiles(meta, near, wide, held, plane, slabs, reach):
    count = held.shape[1]
    for i, ref in enumerate(near):
        for k in range(count):
            held[i, k] = ref[1 + k]
    for i, ref in enumerate(wide):
        for k in range(count):
            held[plane + i, k] = ref[plane + k]
    own_row, own_col = meta[0] // plane, meta[0] % plane
    rows = slabs // plane
    below = jnp.where(own_row == 0, rows - 1, own_row - 1)
    above = jnp.where(own_row == rows - 1, 0, own_row + 1)
    low = jnp.where(
        own_col > 0,
        lax.bitwise_xor(own_col, jnp.maximum(own_col - 1, 0)),
        plane + lax.bitwise_xor(own_row, below),
    )
    high = jnp.where(
        own_col < plane - 1,
        lax.bitwise_xor(own_col, jnp.minimum(own_col + 1, plane - 1)),
        plane + lax.bitwise_xor(own_row, above),
    )
    if count == reach:
        return [held[low, k][3:6] for k in range(reach)] + [held[high, k][0:3] for k in range(reach)]
    return [held[low, reach + k] for k in range(reach)] + [held[high, k] for k in range(reach)]


def first_body(
    meta, pos_in, alpha_in, field_in, gid_in, picks_in, stat, x0, phi, payload,
    pos, alpha, field, gid, picks, sems, *, coeff, box_height, tiles, reach
):
    pairs = [(pos_in, pos), (alpha_in, alpha), (field_in, field), (gid_in, gid), (picks_in, picks)]
    copies = [pltpu.make_async_copy(a, b, sems.at[k]) for k, (a, b) in enumerate(pairs)]
    for copy in copies:
        copy.start()
    for copy in copies:
        copy.wait()
    total = tiles * BLOCK
    lane = lax.broadcasted_iota(jnp.int32, (1, total), 1)
    first = meta[0] * BOXES_DEV
    box = jnp.where(lane < total // BOXES_DEV, first, first + 1).astype(f32)
    p = pos[...]
    al = alpha[...]
    side = jnp.concatenate([p, jnp.zeros((5, total), f32)], axis=0)
    tall = lax.broadcasted_iota(jnp.int32, (8, total), 0) == 2
    u = jnp.where(tall, 2.0 * (side - box * box_height) / box_height - 1.0, side / 16.0 - 1.0)
    terms = [None, u]
    for degree in range(2, ORDER):
        prev = terms[-2] if degree > 2 else 1.0
        terms.append(2.0 * u * terms[-1] - prev)
    levels = []
    for k in range(ORDER):
        value = float(coeff[k, 0]) + float(coeff[k, 1]) * terms[1]
        for n in range(2, ORDER):
            value = value + float(coeff[k, n]) * terms[n]
        levels.append(value)
    levels = jnp.concatenate(levels, axis=0)
    wide = 4 * BLOCK
    for begin in range(0, total, wide):
        value = jnp.dot(
            picks[...], levels[:, begin : begin + wide], precision=highest, preferred_element_type=f32
        )
        value = value[:BLOCK] * value[BLOCK : 2 * BLOCK] * value[2 * BLOCK :]
        for t in range(4):
            phi[begin // BLOCK + t] = value[:, t * BLOCK : (t + 1) * BLOCK]
    start = al * field[...]
    scaled = jnp.concatenate(
        [
            p[0:2] * (1.0 / side_length),
            p[2:3],
            lax.rsqrt(al) * math.sqrt(thole_damp),
            gid[...].astype(f32),
            al,
            jnp.zeros((2, total), f32),
        ],
        axis=0,
    )
    vec = jnp.concatenate([start, jnp.zeros((5, total), f32)], axis=0)
    for t in range(tiles):
        stat[t] = scaled[:, t * BLOCK : (t + 1) * BLOCK]
        x0[t] = vec[:, t * BLOCK : (t + 1) * BLOCK]
    rows = project(phi, x0, tiles)
    weights = jnp.concatenate(rows + [jnp.zeros((2, BLOCK), f32)], axis=0)

    def get(k):
        return jnp.concatenate([stat[k][0:5], x0[k][0:3]], axis=0)

    pack(weights, tiles, reach, get, payload, False)


def own_slot(b, begin, tiles, reach):
    k = jnp.maximum(b - (tiles - reach), 0)
    return (b - begin) * (reach + 1) - k * (k + 1) // 2


def own_slots(begin, end, tiles, reach):
    return sum(min(reach + 1, tiles - b) for b in range(begin, end))


def walk(codes, begin, end, visit):
    def step(at, code):
        later = codes[at + 1]
        visit(code)
        return later

    lax.fori_loop(begin, end, step, codes[begin])


def unpack(code):
    return code & 255, (code >> 8) & 255, code >> 16


def tensors_body(mask_in, stat, out, own_list, halo_list, col, mask, sem, *, half, tiles, reach, length_z):
    copy = pltpu.make_async_copy(mask_in, mask, sem)
    copy.start()
    columns([stat[t] for t in range(tiles)], 5, col)
    copy.wait()
    last = own_list.shape[0] - 2
    n = jnp.int32(0)
    for b in range(tiles):
        if b == half:
            own_list[last] = n
        k = max(b - (tiles - reach), 0)
        slot = b * (reach + 1) - k * (k + 1) // 2
        for o in range(1, min(reach + 1, tiles - b)):
            own_list[n] = jnp.int32(slot + o + (b << 8) + ((b + o) << 16))
            n = n + mask[b, reach + o]
    own_list[last + 1] = n
    m = jnp.int32(0)
    for index, (h, c, at) in enumerate(halo_pairs(tiles, reach)):
        halo_list[m] = jnp.int32(index + (h << 8) + (c << 16))
        m = m + mask[c, at]
    halo_list[halo_list.shape[0] - 1] = m

    def visit(at, unused):
        slot, b, other = unpack(own_list[jnp.maximum(at - tiles, 0)])
        alone = at < tiles
        slot = jnp.where(alone, own_slot(at, 0, tiles, reach), slot)
        b = jnp.where(alone, at, b)
        tile = stat[jnp.where(alone, at, other)]
        rows = [tile[k : k + 1, :] for k in range(5)]

        def store(k, at, value):
            out[slot, k, at, :] = value

        build_pair(lambda k, at: col[b, k, at, :], rows, store, length_z)
        return unused

    lax.fori_loop(0, tiles + n, visit, 0)


def own_body(codes, v, tab, *rest, begin, end, tiles, reach):
    out, acc_i, acc_j, col, wide = rest[-5:]
    top = min(end + reach, tiles)
    columns([v[t] for t in range(begin, end)], 3, col)
    for t in range(top - begin):
        for c in range(3):
            acc_j[t, c] = jnp.zeros((SUB, BLOCK), f32)
            wide[t, c] = spread(v[begin + t], c)

    def pair(b, other, slot, both):
        at_b, at_o = b - begin, other - begin
        vec = [wide[at_o, c] for c in range(3)]
        acc = [acc_j[at_o, c] for c in range(3)] if both else None
        for step in range(BLOCK // SUB):
            at = slice(step * SUB, (step + 1) * SUB)
            t = [tab[slot, k, at, :] for k in range(4)]
            new = apply_tensor(t, vec)
            for c in range(3):
                if both:
                    acc_i[at_b, c, at, :] += new[c]
                else:
                    acc_i[at_b, c, at, :] = new[c]
            if both:
                new = apply_tensor(t, [col[at_b, c, at, :] for c in range(3)])
                acc = [a + n for a, n in zip(acc, new)]
        if both:
            for c in range(3):
                acc_j[at_o, c] = acc[c]

    def alone(b, unused):
        pair(b, b, own_slot(b, 0, tiles, reach), False)
        return unused

    lax.fori_loop(begin, end, alone, 0)
    last = codes.shape[0] - 2

    def visit(code):
        slot, b, other = unpack(code)
        pair(b, other, slot, True)

    walk(codes, codes[last] if begin else 0, codes[last + 1] if begin else codes[last], visit)
    for t in range(top - begin):
        rows = []
        for c in range(3):
            total = acc_j[t, c]
            if t < end - begin:
                parts = [acc_i[t, c, k * SUB : (k + 1) * SUB, :] for k in range(BLOCK // SUB)]
                total = total + lane_sums(parts)
            rows.append(row_sum(total))
        out[t] = jnp.concatenate(rows + [jnp.zeros((5, BLOCK), f32)], axis=0)


def halo_pairs(tiles, reach):
    pairs = []
    for l in range(reach):
        for c in range(l + 1):
            pairs.append((l, c, l - c))
    for l in range(reach):
        for c in range(tiles - reach + l, tiles):
            pairs.append((reach + l, c, reach + tiles + l - c))
    return pairs


def halo_tensors_body(meta, codes, stat, *rest, tiles, plane, slabs, reach, length_z):
    rows = slabs // plane
    near, wide = rest[:plane], rest[plane : plane + rows]
    out, first, col, held = rest[plane + rows :]
    halo = halo_tiles(meta, near, wide, held, plane, slabs, reach)
    for k, tile in enumerate(halo):
        first[k] = tile
    columns(halo, 5, col)
    def visit(code):
        index, h, c = unpack(code)
        own = stat[c]
        own_rows = [own[k : k + 1, :] for k in range(5)]

        def store(k, at, value):
            out[index, k, at, :] = value

        build_pair(lambda k, at: col[h, k, at, :], own_rows, store, length_z)

    walk(codes, 0, codes[codes.shape[0] - 1], visit)


def far_geometry(nodes, geo, box_height):
    turned = nodes[...].T
    row = nodes[...]

    def delta(k):
        return jnp.broadcast_to(turned[:, k : k + 1], (BLOCK, BLOCK)) - jnp.broadcast_to(
            row[k : k + 1, :], (BLOCK, BLOCK)
        )

    dx, dy = wrap_unit(delta(0)), wrap_unit(delta(1))
    geo[0] = dx
    geo[1] = dy
    geo[2] = box_height * delta(2)
    geo[3] = dx * dx + dy * dy + box_height * box_height


def far_tensor(geo, apart, put, box_height, length_z):
    for step in range(BLOCK // CHUNK):
        at = slice(step * CHUNK, (step + 1) * CHUNK)
        dx, dy = geo[0, at, :], geo[1, at, :]
        dz = wrap_z(geo[2, at, :] - apart * box_height, length_z)
        inv = lax.rsqrt(geo[3, at, :] + dz * dz)
        inv_two = inv * inv
        three = inv * inv_two
        five = 3.0 * three * inv_two
        for k, value in enumerate(tensor(five, three, dx, dy, dz)):
            put(k, at, value)


def far_tensors_body(nodes, out, geo, *, box_height, length_z):
    far_geometry(nodes, geo, box_height)

    def visit(d, unused):
        def put(k, at, value):
            out[at.start // SUB, d - 1, k] = value

        far_tensor(geo, d.astype(f32), put, box_height, length_z)
        return unused

    lax.fori_loop(1, out.shape[1] + 1, visit, 0)


def apply_tensor(t, v):
    ex, ey, ez, three = t
    x, y, z = v
    along = ex * x + ey * y + ez * z
    return (ex * along - three * x, ey * along - three * y, ez * along - three * z)


def far_nodes(table, geo, wide, fcol, boxes, box_height, length_z):
    if table is not None:
        def rows(step, unused):
            ats = [pl.ds(pl.multiple_of(step * SUB, SUB), SUB)]

            def load(d):
                return [[table[step, d - 1, k] for k in range(4)]]

            def field(ts, k):
                v = [wide[k, c] for c in range(3)]
                return sum([apply_tensor(t, v) for t in ts], ())

            acc = field(load(boxes - 1), boxes - 1) + field(load(1), 2)
            def visit(d, acc):
                ts = load(d)
                new = field(ts, d) + field(ts, d + 1)
                return tuple(a + n for a, n in zip(acc, new))

            acc = visit(2, acc)
            acc = lax.fori_loop(3, boxes - 1, visit, acc, unroll=7)
            for box in range(BOXES_DEV):
                for half in range(1):
                    for c in range(3):
                        fcol[box, c, ats[half], :] = jnp.broadcast_to(
                            jnp.sum(acc[box * 3 + half * 3 + c], axis=1, keepdims=True), (SUB, BLOCK)
                        )
            return unused

        lax.fori_loop(0, BLOCK // SUB, rows, 0)
        return
    for box in range(BOXES_DEV):
        for c in range(3):
            fcol[box, c] = jnp.zeros((BLOCK, BLOCK), f32)

    def visit(d, unused):
        def hold(k, at, value):
            geo[4 + k, at, :] = value

        far_tensor(geo, d.astype(f32), hold, box_height, length_z)
        for box in range(BOXES_DEV):

            @pl.when(d < boxes - 1 if box else d > 1)
            def _():
                v = [wide[d + box, c] for c in range(3)]

                def part(step, skip):
                    at = pl.ds(pl.multiple_of(step * SUB, SUB), SUB)
                    new = apply_tensor([geo[4 + k, at, :] for k in range(4)], v)
                    for c in range(3):
                        fcol[box, c, at, :] += new[c]
                    return skip

                lax.fori_loop(0, BLOCK // SUB, part, 0)

        return unused

    lax.fori_loop(1, boxes, visit, 0)
    for box in range(BOXES_DEV):
        for c in range(3):
            fcol[box, c] = jnp.broadcast_to(
                jnp.sum(fcol[box, c], axis=1, keepdims=True), (BLOCK, BLOCK)
            )


def field_body(meta, codes, nodes, stat, v, phi, halo_tab, *rest,
               mode, tiles, reach, plane, slabs, box_height, length_z, surface, kept, half):
    rest = list(rest)

    def take(count):
        return [rest.pop(0) for _ in range(count)]

    rows = slabs // plane
    parts = take(2)
    near = take(plane) if mode else []
    bundles = take(rows)
    first = None if mode else take(1)[0]
    table = take(1)[0] if kept else None
    extra = take((0, 0, 4)[mode])
    outs = take((3, 4, 5)[mode])
    acc, col, wide, fcol, geo, held = rest
    boxes = slabs * BOXES_DEV
    member = meta[0]
    own_row, own_col = member // plane, member % plane

    total = jnp.zeros((SUB, BLOCK), f32)
    for i in range(rows):
        for j in range(plane):
            tile = bundles[i][j]
            total = total + tile
            other = lax.bitwise_xor(own_row, i) * plane + lax.bitwise_xor(own_col, j) - member
            k = jnp.where(other < 0, other + slabs, other) * BOXES_DEV
            for box in range(BOXES_DEV):
                for c in range(3):
                    wide[k + box, c] = spread(tile, box * 3 + c)
    sums = jnp.sum(total, axis=1, keepdims=True)
    moment = [surface * (sums[c : c + 1] + sums[3 + c : 4 + c]) for c in range(3)]

    if mode:
        halo = halo_tiles(meta, near, bundles, held, plane, slabs, reach)
    else:
        halo = [first[k][5:8] for k in range(2 * reach)]
    columns(halo, 3, col)
    for t in range(tiles):
        for c in range(3):
            acc[t, c] = jnp.zeros((SUB, BLOCK), f32)
    def visit(code):
        index, h, c = unpack(code)
        sofar = [acc[c, k] for k in range(3)]
        for step in range(BLOCK // SUB):
            at = slice(step * SUB, (step + 1) * SUB)
            new = apply_tensor(
                [halo_tab[index, k, at, :] for k in range(4)], [col[h, k, at, :] for k in range(3)]
            )
            sofar = [a + n for a, n in zip(sofar, new)]
        for k in range(3):
            acc[c, k] = sofar[k]

    walk(codes, 0, codes[codes.shape[0] - 1], visit)

    if not kept:
        far_geometry(nodes, geo, box_height)
    far_nodes(table, geo, wide, fcol, boxes, box_height, length_z)

    per = tiles // BOXES_DEV
    zero = jnp.zeros((5, BLOCK), f32)
    fields = []
    for t in range(tiles):
        box = t // per
        sofar = [acc[t, c] for c in range(3)]
        for step in range(BLOCK // SUB):
            at = slice(step * SUB, (step + 1) * SUB)
            value = phi[t, at, :]
            sofar = [a + value * fcol[box, c, at, :] for c, a in enumerate(sofar)]
        rows = [row_sum(a) - m for a, m in zip(sofar, moment)]
        value = jnp.concatenate(rows + [zero], axis=0)
        if t < parts[0].shape[0]:
            value = value + parts[0][t]
        if t >= half:
            value = value + parts[1][t - half]
        fields.append(value)

    def alpha(t):
        return spread(stat[t], 5)

    none = jnp.zeros((1, BLOCK), f32)

    def send(u, payload, scalar):
        weights = jnp.concatenate(project(phi, u, tiles) + [scalar, none], axis=0)
        pack(weights, tiles, reach, lambda k: u[k], payload, True)

    def fold(terms):
        out = terms[0]
        for x in terms[1:]:
            out = out + x
        return row_sum(out)

    if mode == 0:
        res, u, payload = outs
        dots = []
        for t in range(tiles):
            scaled = alpha(t) * fields[t]
            res[t] = fields[t]
            u[t] = scaled
            dots.append(scaled * fields[t])
        send(u, payload, fold(dots))
    elif mode == 1:
        image, u, payload, norm = outs
        dots = []
        for t in range(tiles):
            w = v[t] / alpha(t) - fields[t]
            image[t] = w
            u[t] = alpha(t) * w
            dots.append(v[t] * w)
        norm[...] = jnp.broadcast_to(sums[6:7], (SUB, BLOCK))
        send(u, payload, fold(dots))
    else:
        first, res, w0, norm = extra
        x1, r1, z1, q1, scal = outs
        rate = norm[...] / jnp.broadcast_to(sums[6:7], (SUB, BLOCK))
        one, two, three = [], [], []
        for t in range(tiles):
            y = v[t] / alpha(t) - fields[t]
            r = res[t] - rate * w0[t]
            z = alpha(t) * r
            q = w0[t] - rate * y
            x1[t] = first[t] + rate * (alpha(t) * res[t])
            r1[t] = r
            z1[t] = z
            q1[t] = q
            one.append(r * z)
            two.append(z * q)
            three.append(z * w0[t])
        scal[...] = jnp.concatenate(
            [fold(one), fold(two), fold(three), jnp.broadcast_to(sums[6:7], (1, BLOCK)), norm[0:1], none, none, none],
            axis=0,
        )


def last_body(scal, stat, res, w0, x1, r1, z1, q1, *rest, tiles):
    gathered, (dip, out) = rest[:-2], rest[-2:]
    total = gathered[0][...]
    for ref in gathered[1:]:
        total = total + ref[...]
    sums = jnp.sum(total, axis=1, keepdims=True)

    def value(x):
        return jnp.broadcast_to(x, (1, BLOCK))

    norm, curve, cross = value(sums[0:1]), value(sums[1:2]), value(sums[2:3])
    along, start = scal[3:4], scal[4:5]
    beta = norm / start
    rate = norm / (curve + 2.0 * beta * cross + beta * beta * along)
    for t in range(tiles):
        at = slice(t * BLOCK, (t + 1) * BLOCK)
        u0 = stat[t][5:6] * res[t][0:3]
        p = z1[t][0:3] + beta * u0
        w = q1[t][0:3] + beta * w0[t][0:3]
        dip[:, at] = x1[t][0:3] + rate * p
        out[:, at] = r1[t][0:3] - rate * w


def swap(x, axes, count):
    got = [x]
    for s in range(1, count):
        got.append(lax.ppermute(x, axes, [(i, i ^ s) for i in range(count)]))
    return got


def on_device(positions, polarizability, permanent_field, group_id, pair_mask):
    slabs = lax.axis_size(RING)
    member = lax.axis_index(RING)
    plane = lax.axis_size(("oct", "sub"))
    rows = lax.axis_size("blk")
    atoms = positions.shape[1]
    tiles = atoms // BLOCK
    length_z = layer_gap * atoms * slabs / 256.0
    boxes = BOXES_DEV * slabs
    box_height = length_z / boxes
    reach = (pair_mask.shape[1] - 1) // 2
    surface = 4.0 * math.pi / 3.0 / (side_length * side_length * length_z)
    coeff, picks, nodes = node_tables()
    nodes = jnp.asarray(nodes)
    meta = jnp.reshape(member, (1,)).astype(jnp.int32)
    mask = pair_mask
    tile_shape = (tiles, 8, BLOCK)
    kept = (boxes - 1) * 4 * BLOCK * BLOCK * 4 <= TABLE_LIMIT

    half = tiles // 2

    def far_memory(x):
        return pltpu.with_memory_space_constraint(x, pltpu.HBM)

    stat, x0, phi, payload = call(
        functools.partial(first_body, coeff=coeff, box_height=box_height, tiles=tiles, reach=reach),
        [tile_shape, tile_shape, (tiles, BLOCK, BLOCK), (1 + 2 * reach, 8, BLOCK)],
        [meta] + [far_memory(x) for x in (positions, polarizability[None], permanent_field, group_id[None], jnp.asarray(picks))],
        smem=1,
        limit=16 << 20,
        far=5,
        more=[
            pltpu.VMEM((3, atoms), f32),
            pltpu.VMEM((1, atoms), f32),
            pltpu.VMEM((3, atoms), f32),
            pltpu.VMEM((1, atoms), jnp.int32),
            pltpu.VMEM(picks.shape, f32),
            pltpu.SemaphoreType.DMA((5,)),
        ],
    )
    count = own_slots(0, tiles, tiles, reach)
    tab, own_list, halo_list = call(
        functools.partial(tensors_body, half=half, tiles=tiles, reach=reach, length_z=length_z),
        [(count, 4, BLOCK, BLOCK)],
        [far_memory(mask), stat],
        far=1,
        scratch=[(tiles, 5, BLOCK, BLOCK)],
        more=[pltpu.SMEM(mask.shape, jnp.int32), pltpu.SemaphoreType.DMA],
        cost=pl.CostEstimate(flops=count * BLOCK * BLOCK * 70, bytes_accessed=1 << 20, transcendentals=count * BLOCK * BLOCK * 2),
        pinned=(0,),
        lists=(count - tiles + 2, len(halo_pairs(tiles, reach)) + 1),
    )
    table = []
    if kept:
        table = call(
            functools.partial(far_tensors_body, box_height=box_height, length_z=length_z),
            [(BLOCK // SUB, boxes - 1, 4, SUB, BLOCK)],
            [nodes],
            scratch=[(4, BLOCK, BLOCK)],
            cost=pl.CostEstimate(flops=boxes * BLOCK * BLOCK * 28, bytes_accessed=1 << 20, transcendentals=boxes * BLOCK * BLOCK),
            pinned=(0,),
        )

    def own_field(v, begin, end, after):
        top = min(end + reach, tiles) - begin
        return call(
            functools.partial(own_body, begin=begin, end=end, tiles=tiles, reach=reach),
            [(top, 8, BLOCK)],
            [own_list, v, tab] + after,
            smem=1,
            scratch=[
                (end - begin, 3, BLOCK, BLOCK),
                (top, 3, SUB, BLOCK),
                (end - begin, 3, BLOCK, BLOCK),
                (top, 3, SUB, BLOCK),
            ],
            cost=pl.CostEstimate(flops=72 * BLOCK * BLOCK * 18, bytes_accessed=1 << 20, transcendentals=0),
        )[0]

    def exchange(payload, v):
        near = swap(payload, ("oct", "sub"), plane)
        first = own_field(v, 0, half, [])
        bundle = call(
            functools.partial(relay_body, plane=plane, reach=reach),
            [(plane + payload.shape[0] - 1, 8, BLOCK)],
            [meta] + near + [first],
            smem=1,
            scratch=[(plane, payload.shape[0] - 1, 8, BLOCK)],
        )[0]
        bundles = swap(bundle, "blk", rows)
        second = own_field(v, half, tiles, [bundle])
        return [first, second], near, bundles

    def field(mode, v, parts, near, bundles, extra):
        outs = [
            [tile_shape, tile_shape, (1 + reach, 8, BLOCK)],
            [tile_shape, tile_shape, (1 + reach, 8, BLOCK), (SUB, BLOCK)],
            [tile_shape] * 4 + [(8, BLOCK)],
        ][mode]
        return call(
            functools.partial(
                field_body, mode=mode, tiles=tiles, reach=reach, plane=plane, slabs=slabs, box_height=box_height,
                length_z=length_z, surface=surface, kept=kept, half=half,
            ),
            outs,
            [meta, halo_list, nodes, stat, v, phi, halo_tab] + parts + (near if mode else []) + bundles
            + ([] if mode else [edge]) + table + extra,
            smem=2,
            scratch=[
                (tiles, 3, SUB, BLOCK),
                (2 * reach, 3, BLOCK, BLOCK),
                (boxes, 3, SUB, BLOCK),
                (BOXES_DEV, 3, BLOCK, BLOCK),
                (8, BLOCK, BLOCK) if not kept else (1, 8, BLOCK),
                (plane + rows, reach, 8, BLOCK),
            ],
        )

    parts, near, bundles = exchange(payload, x0)
    halo_tab, edge = call(
        functools.partial(
            halo_tensors_body, tiles=tiles, plane=plane, slabs=slabs, reach=reach, length_z=length_z
        ),
        [(len(halo_pairs(tiles, reach)), 4, BLOCK, BLOCK), (2 * reach, 8, BLOCK)],
        [meta, halo_list, stat] + near + bundles,
        smem=2,
        scratch=[(2 * reach, 5, BLOCK, BLOCK), (plane + rows, 2 * reach, 8, BLOCK)],
        pinned=(0,),
    )
    r0, u0, payload = field(0, x0, parts, near, bundles, [])
    parts, near, bundles = exchange(payload, u0)
    w0, u1, payload, norm = field(1, u0, parts, near, bundles, [])
    parts, near, bundles = exchange(payload, u1)
    x1, r1, z1, q1, scal = field(2, u1, parts, near, bundles, [x0, r0, w0, norm])
    sums = swap(scal, ("oct", "sub"), plane)
    sums = swap(functools.reduce(jnp.add, sums), "blk", rows)
    return call(
        functools.partial(last_body, tiles=tiles),
        [(3, atoms), (3, atoms)],
        [scal, stat, r0, w0, x1, r1, z1, q1] + sums,
    )


def solution(mesh):
    split = P(("groups", "blk", "oct", "sub"))
    wide = P(None, ("groups", "blk", "oct", "sub"))
    return jax.shard_map(
        lambda *args: tuple(on_device(*args)),
        mesh=mesh,
        in_specs=(wide, split, wide, split, P(("groups", "blk", "oct", "sub"), None)),
        out_specs=(wide, wide),
        check_vma=False,
    )
```

```python
import functools
import math

import jax
import jax.numpy as jnp
import numpy as np
from jax import lax
from jax.experimental import pallas as pl
from jax.experimental.pallas import tpu as pltpu
from jax.sharding import PartitionSpec as P

BOXES_DEV = 2
BLOCK = 128
ORDER = 5
NODE_PAD = 128
ITERS = 2
SUB = 8
CHUNK = 8

side_length = 32.0
layer_gap = 2.5
thole_damp = 0.39
highest = lax.Precision.HIGHEST
f32 = jnp.float32
RING = ("blk", "oct", "sub")

VM = pl.BlockSpec(memory_space=pltpu.VMEM)
SM = pl.BlockSpec(memory_space=pltpu.SMEM)
FAR = pl.BlockSpec(memory_space=pltpu.HBM)
TABLE_LIMIT = 16 << 20


def call(body, outs, args, smem=0, scratch=(), limit=None, cost=None, pinned=(), far=0, more=(), lists=()):
    shapes = [
        pltpu.VMEM(shape, f32) if at in pinned else jax.ShapeDtypeStruct(shape, f32)
        for at, shape in enumerate(outs)
    ] + [jax.ShapeDtypeStruct((size,), jnp.int32) for size in lists]
    return list(pl.pallas_call(
        body,
        out_shape=shapes,
        in_specs=[SM] * smem + [FAR] * far + [VM] * (len(args) - smem - far),
        out_specs=[VM] * len(outs) + [SM] * len(lists),
        scratch_shapes=[pltpu.VMEM(shape, f32) for shape in scratch] + list(more),
        compiler_params=pltpu.CompilerParams(vmem_limit_bytes=limit or (12 << 20)),
        cost_estimate=cost,
    )(*args))


def node_tables():
    count = ORDER
    roots = np.cos((2.0 * np.arange(count) + 1.0) * np.pi / (2.0 * count))
    degree = np.arange(count)
    coeff = (
        2.0 / count * np.cos(np.outer(2.0 * np.arange(count) + 1.0, degree) * np.pi / (2.0 * count))
    )
    coeff = np.where(degree[None, :] == 0, 1.0 / count, coeff)
    index = np.arange(NODE_PAD)
    live = index < count**3
    safe = np.where(live, index, 0)
    levels = np.stack([safe // (count * count), safe // count % count, safe % count])
    picks = np.zeros((3, NODE_PAD, 6, 8))
    for d in range(3):
        picks[d, index, levels[d], d] = 1.0
    picks[0] *= live[:, None, None]
    picks = np.tile(picks.reshape(3 * NODE_PAD, 48), (1, 3))
    nodes = np.zeros((8, NODE_PAD))
    nodes[0] = 0.5 * (1.0 + roots[levels[0]])
    nodes[1] = 0.5 * (1.0 + roots[levels[1]])
    nodes[2] = 0.5 * roots[levels[2]]
    return coeff.astype(np.float32), picks.astype(np.float32), nodes.astype(np.float32)


def wrap_unit(delta):
    return (delta - jnp.floor(delta + 0.5)) * side_length


def wrap_z(delta, length_z):
    return delta - length_z * jnp.floor(delta * (1.0 / length_z) + 0.5)


def tensor(five, three, dx, dy, dz):
    five = jnp.maximum(five, 1e-36)
    root = five * lax.rsqrt(five)
    return (root * dx, root * dy, root * dz, three)


def columns(tiles, count, out):
    for t, tile in enumerate(tiles):
        for k in range(count):
            out[t, k] = jnp.broadcast_to(tile[k : k + 1, :], (BLOCK, BLOCK)).T


def diagonal(step):
    row = lax.broadcasted_iota(jnp.int32, (SUB, BLOCK), 0)
    lane = lax.broadcasted_iota(jnp.int32, (SUB, BLOCK), 1)
    return lane - row == step * SUB


def spread(tile, k):
    return jnp.broadcast_to(tile[k : k + 1, :], (SUB, BLOCK))


def row_sum(x):
    return jnp.sum(x, axis=0, keepdims=True)


def build_pair(col, rows, put, length_z):
    wide = [jnp.broadcast_to(r, (CHUNK, BLOCK)) for r in rows]
    for step in range(BLOCK // CHUNK):
        at = slice(step * CHUNK, (step + 1) * CHUNK)
        dx = wrap_unit(col(0, at) - wide[0])
        dy = wrap_unit(col(1, at) - wide[1])
        dz = wrap_z(col(2, at) - wide[2], length_z)
        keep = col(4, at) != wide[4]
        dist = jnp.where(keep, dx * dx + dy * dy + dz * dz, 1e24)
        inv = lax.rsqrt(dist)
        inv_two = inv * inv
        inv_three = inv * inv_two
        s = dist * (dist * inv) * (col(3, at) * wide[3])
        decay = jnp.exp(-s)
        small = s * (1.0 - s * (0.5 - s * (1.0 / 6.0 - s * (1.0 / 24.0))))
        three = jnp.where(s < 0.015625, small, 1.0 - decay)
        five = ((three - s * decay) * inv_three) * (3.0 * inv_two)
        for k, value in enumerate(tensor(five, three * inv_three, dx, dy, dz)):
            put(k, at, value)


def lane_sums(parts):
    total = None
    for step, x in enumerate(parts):
        term = jnp.where(diagonal(step), jnp.sum(x, axis=1, keepdims=True), 0.0)
        total = term if total is None else total + term
    return total


def project(phi, v, tiles):
    out = []
    per = tiles // BOXES_DEV
    for box in range(BOXES_DEV):
        wide = [[spread(v[box * per + t], c) for c in range(3)] for t in range(per)]
        parts = [[], [], []]
        for step in range(BLOCK // SUB):
            at = slice(step * SUB, (step + 1) * SUB)
            sums = [None] * 3
            for t in range(per):
                value = phi[box * per + t, at, :]
                for c in range(3):
                    term = value * wide[t][c]
                    sums[c] = term if sums[c] is None else sums[c] + term
            for c in range(3):
                parts[c].append(sums[c])
        out += [row_sum(lane_sums(p)) for p in parts]
    return out


def pack(weights, tiles, reach, get, payload, both):
    payload[0] = weights
    for k in range(reach):
        low, high = get(k), get(tiles - reach + k)
        if both:
            rows = [low[0:3], high[0:3], jnp.zeros((2, BLOCK), f32)]
            payload[1 + k] = jnp.concatenate(rows, axis=0)
        else:
            payload[1 + k] = low
            payload[1 + reach + k] = high


def relay_body(meta, *rest, plane, reach):
    got, (out, held) = rest[:plane], rest[-2:]
    count = held.shape[1]
    for i in range(plane):
        out[i] = got[i][0]
        for k in range(count):
            held[i, k] = got[i][1 + k]
    own = meta[0] % plane
    last = lax.bitwise_xor(own, plane - 1)
    for k in range(count):
        low, high = held[own, k], held[last, k]
        if count == reach:
            out[plane + k] = jnp.concatenate([low[0:3], high[3:6], low[6:8]], axis=0)
        else:
            out[plane + k] = low if k < reach else high


def halo_tiles(meta, near, wide, held, plane, slabs, reach):
    count = held.shape[1]
    for i, ref in enumerate(near):
        for k in range(count):
            held[i, k] = ref[1 + k]
    for i, ref in enumerate(wide):
        for k in range(count):
            held[plane + i, k] = ref[plane + k]
    own_row, own_col = meta[0] // plane, meta[0] % plane
    rows = slabs // plane
    below = jnp.where(own_row == 0, rows - 1, own_row - 1)
    above = jnp.where(own_row == rows - 1, 0, own_row + 1)
    low = jnp.where(
        own_col > 0,
        lax.bitwise_xor(own_col, jnp.maximum(own_col - 1, 0)),
        plane + lax.bitwise_xor(own_row, below),
    )
    high = jnp.where(
        own_col < plane - 1,
        lax.bitwise_xor(own_col, jnp.minimum(own_col + 1, plane - 1)),
        plane + lax.bitwise_xor(own_row, above),
    )
    if count == reach:
        return [held[low, k][3:6] for k in range(reach)] + [held[high, k][0:3] for k in range(reach)]
    return [held[low, reach + k] for k in range(reach)] + [held[high, k] for k in range(reach)]


def first_body(
    meta, pos_in, alpha_in, field_in, gid_in, picks_in, stat, x0, phi, payload,
    pos, alpha, field, gid, picks, sems, *, coeff, box_height, tiles, reach
):
    pairs = [(pos_in, pos), (alpha_in, alpha), (field_in, field), (gid_in, gid), (picks_in, picks)]
    copies = [pltpu.make_async_copy(a, b, sems.at[k]) for k, (a, b) in enumerate(pairs)]
    for copy in copies:
        copy.start()
    for copy in copies:
        copy.wait()
    total = tiles * BLOCK
    lane = lax.broadcasted_iota(jnp.int32, (1, total), 1)
    first = meta[0] * BOXES_DEV
    box = jnp.where(lane < total // BOXES_DEV, first, first + 1).astype(f32)
    p = pos[...]
    al = alpha[...]
    side = jnp.concatenate([p, jnp.zeros((5, total), f32)], axis=0)
    tall = lax.broadcasted_iota(jnp.int32, (8, total), 0) == 2
    u = jnp.where(tall, 2.0 * (side - box * box_height) / box_height - 1.0, side / 16.0 - 1.0)
    terms = [None, u]
    for degree in range(2, ORDER):
        prev = terms[-2] if degree > 2 else 1.0
        terms.append(2.0 * u * terms[-1] - prev)
    levels = []
    for k in range(ORDER):
        value = float(coeff[k, 0]) + float(coeff[k, 1]) * terms[1]
        for n in range(2, ORDER):
            value = value + float(coeff[k, n]) * terms[n]
        levels.append(value)
    levels = jnp.concatenate(levels + [jnp.zeros((8, total), f32)] * (6 - ORDER), axis=0)
    pieces = []
    for k in range(3):
        pieces.append(levels.astype(jnp.bfloat16))
        levels = levels - pieces[-1].astype(f32)
    levels = jnp.concatenate(pieces, axis=0)
    chosen = picks[...].astype(jnp.bfloat16)
    wide = 4 * BLOCK
    for begin in range(0, total, wide):
        value = jnp.dot(chosen, levels[:, begin : begin + wide], preferred_element_type=f32)
        value = value[:BLOCK] * value[BLOCK : 2 * BLOCK] * value[2 * BLOCK :]
        for t in range(4):
            phi[begin // BLOCK + t] = value[:, t * BLOCK : (t + 1) * BLOCK]
    start = al * field[...]
    scaled = jnp.concatenate(
        [
            p[0:2] * (1.0 / side_length),
            p[2:3],
            lax.rsqrt(al) * math.sqrt(thole_damp),
            gid[...].astype(f32),
            al,
            jnp.zeros((2, total), f32),
        ],
        axis=0,
    )
    vec = jnp.concatenate([start, jnp.zeros((5, total), f32)], axis=0)
    for t in range(tiles):
        stat[t] = scaled[:, t * BLOCK : (t + 1) * BLOCK]
        x0[t] = vec[:, t * BLOCK : (t + 1) * BLOCK]
    rows = project(phi, x0, tiles)
    weights = jnp.concatenate(rows + [jnp.zeros((2, BLOCK), f32)], axis=0)

    def get(k):
        return jnp.concatenate([stat[k][0:5], x0[k][0:3]], axis=0)

    pack(weights, tiles, reach, get, payload, False)


def own_slot(b, begin, tiles, reach):
    k = jnp.maximum(b - (tiles - reach), 0)
    return (b - begin) * (reach + 1) - k * (k + 1) // 2


def own_slots(begin, end, tiles, reach):
    return sum(min(reach + 1, tiles - b) for b in range(begin, end))


def walk(codes, begin, end, visit):
    def step(at, code):
        later = codes[at + 1]
        visit(code)
        return later

    lax.fori_loop(begin, end, step, codes[begin])


def unpack(code):
    return code & 255, (code >> 8) & 255, code >> 16


def tensors_body(mask_in, stat, out, own_list, halo_list, col, mask, sem, *, half, tiles, reach, length_z):
    copy = pltpu.make_async_copy(mask_in, mask, sem)
    copy.start()
    columns([stat[t] for t in range(tiles)], 5, col)
    copy.wait()
    last = own_list.shape[0] - 2
    n = jnp.int32(0)
    for b in range(tiles):
        if b == half:
            own_list[last] = n
        k = max(b - (tiles - reach), 0)
        slot = b * (reach + 1) - k * (k + 1) // 2
        for o in range(1, min(reach + 1, tiles - b)):
            own_list[n] = jnp.int32(slot + o + (b << 8) + ((b + o) << 16))
            n = n + mask[b, reach + o]
    own_list[last + 1] = n
    m = jnp.int32(0)
    for index, (h, c, at) in enumerate(halo_pairs(tiles, reach)):
        halo_list[m] = jnp.int32(index + (h << 8) + (c << 16))
        m = m + mask[c, at]
    halo_list[halo_list.shape[0] - 1] = m

    def visit(at, unused):
        slot, b, other = unpack(own_list[jnp.maximum(at - tiles, 0)])
        alone = at < tiles
        slot = jnp.where(alone, own_slot(at, 0, tiles, reach), slot)
        b = jnp.where(alone, at, b)
        tile = stat[jnp.where(alone, at, other)]
        rows = [tile[k : k + 1, :] for k in range(5)]

        def store(k, at, value):
            out[slot, k, at, :] = value

        build_pair(lambda k, at: col[b, k, at, :], rows, store, length_z)
        return unused

    lax.fori_loop(0, tiles + n, visit, 0)


def own_body(codes, v, tab, *rest, begin, end, tiles, reach):
    out, acc_i, acc_j, col, wide = rest[-5:]
    top = min(end + reach, tiles)
    columns([v[t] for t in range(begin, end)], 3, col)
    for t in range(top - begin):
        for c in range(3):
            acc_j[t, c] = jnp.zeros((SUB, BLOCK), f32)
            wide[t, c] = spread(v[begin + t], c)

    def pair(b, other, slot, both):
        at_b, at_o = b - begin, other - begin
        vec = [wide[at_o, c] for c in range(3)]
        acc = [acc_j[at_o, c] for c in range(3)] if both else None
        for step in range(BLOCK // SUB):
            at = slice(step * SUB, (step + 1) * SUB)
            t = [tab[slot, k, at, :] for k in range(4)]
            new = apply_tensor(t, vec)
            for c in range(3):
                if both:
                    acc_i[at_b, c, at, :] += new[c]
                else:
                    acc_i[at_b, c, at, :] = new[c]
            if both:
                new = apply_tensor(t, [col[at_b, c, at, :] for c in range(3)])
                acc = [a + n for a, n in zip(acc, new)]
        if both:
            for c in range(3):
                acc_j[at_o, c] = acc[c]

    def alone(b, unused):
        pair(b, b, own_slot(b, 0, tiles, reach), False)
        return unused

    lax.fori_loop(begin, end, alone, 0)
    last = codes.shape[0] - 2

    def visit(code):
        slot, b, other = unpack(code)
        pair(b, other, slot, True)

    walk(codes, codes[last] if begin else 0, codes[last + 1] if begin else codes[last], visit)
    for t in range(top - begin):
        rows = []
        for c in range(3):
            total = acc_j[t, c]
            if t < end - begin:
                parts = [acc_i[t, c, k * SUB : (k + 1) * SUB, :] for k in range(BLOCK // SUB)]
                total = total + lane_sums(parts)
            rows.append(row_sum(total))
        out[t] = jnp.concatenate(rows + [jnp.zeros((5, BLOCK), f32)], axis=0)


def halo_pairs(tiles, reach):
    pairs = []
    for l in range(reach):
        for c in range(l + 1):
            pairs.append((l, c, l - c))
    for l in range(reach):
        for c in range(tiles - reach + l, tiles):
            pairs.append((reach + l, c, reach + tiles + l - c))
    return pairs


def halo_tensors_body(meta, codes, stat, *rest, tiles, plane, slabs, reach, length_z):
    rows = slabs // plane
    near, wide = rest[:plane], rest[plane : plane + rows]
    out, first, col, held = rest[plane + rows :]
    halo = halo_tiles(meta, near, wide, held, plane, slabs, reach)
    for k, tile in enumerate(halo):
        first[k] = tile
    columns(halo, 5, col)
    def visit(code):
        index, h, c = unpack(code)
        own = stat[c]
        own_rows = [own[k : k + 1, :] for k in range(5)]

        def store(k, at, value):
            out[index, k, at, :] = value

        build_pair(lambda k, at: col[h, k, at, :], own_rows, store, length_z)

    walk(codes, 0, codes[codes.shape[0] - 1], visit)


def far_geometry(nodes, geo, box_height):
    turned = nodes[...].T
    row = nodes[...]

    def delta(k):
        return jnp.broadcast_to(turned[:, k : k + 1], (BLOCK, BLOCK)) - jnp.broadcast_to(
            row[k : k + 1, :], (BLOCK, BLOCK)
        )

    dx, dy = wrap_unit(delta(0)), wrap_unit(delta(1))
    geo[0] = dx
    geo[1] = dy
    geo[2] = box_height * delta(2)
    geo[3] = dx * dx + dy * dy + box_height * box_height


def far_tensor(geo, apart, put, box_height, length_z):
    for step in range(BLOCK // CHUNK):
        at = slice(step * CHUNK, (step + 1) * CHUNK)
        dx, dy = geo[0, at, :], geo[1, at, :]
        dz = wrap_z(geo[2, at, :] - apart * box_height, length_z)
        inv = lax.rsqrt(geo[3, at, :] + dz * dz)
        inv_two = inv * inv
        three = inv * inv_two
        five = 3.0 * three * inv_two
        for k, value in enumerate(tensor(five, three, dx, dy, dz)):
            put(k, at, value)


def far_tensors_body(nodes, out, geo, *, box_height, length_z):
    far_geometry(nodes, geo, box_height)

    def visit(d, unused):
        def put(k, at, value):
            out[at.start // SUB, d - 1, k] = value

        far_tensor(geo, d.astype(f32), put, box_height, length_z)
        return unused

    lax.fori_loop(1, out.shape[1] + 1, visit, 0)


def apply_tensor(t, v):
    ex, ey, ez, three = t
    x, y, z = v
    along = ex * x + ey * y + ez * z
    return (ex * along - three * x, ey * along - three * y, ez * along - three * z)


def far_nodes(table, geo, wide, fcol, boxes, box_height, length_z):
    if table is not None:
        def rows(step, unused):
            ats = [pl.ds(pl.multiple_of(step * SUB, SUB), SUB)]

            def load(d):
                return [[table[step, d - 1, k] for k in range(4)]]

            def field(ts, k):
                v = [wide[k, c] for c in range(3)]
                return sum([apply_tensor(t, v) for t in ts], ())

            acc = field(load(boxes - 1), boxes - 1) + field(load(1), 2)
            def visit(d, acc):
                ts = load(d)
                new = field(ts, d) + field(ts, d + 1)
                return tuple(a + n for a, n in zip(acc, new))

            acc = visit(2, acc)
            acc = lax.fori_loop(3, boxes - 1, visit, acc, unroll=14)
            for box in range(BOXES_DEV):
                for c in range(3):
                    fcol[box, c, ats[0], :] = acc[box * 3 + c]
            return unused

        lax.fori_loop(0, BLOCK // SUB, rows, 0)
        for box in range(BOXES_DEV):
            for c in range(3):
                fcol[box, c] = jnp.broadcast_to(
                    jnp.sum(fcol[box, c], axis=1, keepdims=True), (BLOCK, BLOCK)
                )
        return
    for box in range(BOXES_DEV):
        for c in range(3):
            fcol[box, c] = jnp.zeros((BLOCK, BLOCK), f32)

    def visit(d, unused):
        def hold(k, at, value):
            geo[4 + k, at, :] = value

        far_tensor(geo, d.astype(f32), hold, box_height, length_z)
        for box in range(BOXES_DEV):

            @pl.when(d < boxes - 1 if box else d > 1)
            def _():
                v = [wide[d + box, c] for c in range(3)]

                def part(step, skip):
                    at = pl.ds(pl.multiple_of(step * SUB, SUB), SUB)
                    new = apply_tensor([geo[4 + k, at, :] for k in range(4)], v)
                    for c in range(3):
                        fcol[box, c, at, :] += new[c]
                    return skip

                lax.fori_loop(0, BLOCK // SUB, part, 0)

        return unused

    lax.fori_loop(1, boxes, visit, 0)
    for box in range(BOXES_DEV):
        for c in range(3):
            fcol[box, c] = jnp.broadcast_to(
                jnp.sum(fcol[box, c], axis=1, keepdims=True), (BLOCK, BLOCK)
            )


def field_body(meta, codes, nodes, stat, v, phi, halo_tab, *rest,
               mode, tiles, reach, plane, slabs, box_height, length_z, surface, kept, half):
    rest = list(rest)

    def take(count):
        return [rest.pop(0) for _ in range(count)]

    rows = slabs // plane
    parts = take(2)
    near = take(plane) if mode else []
    bundles = take(rows)
    first = None if mode else take(1)[0]
    table = take(1)[0] if kept else None
    extra = take((0, 0, 4)[mode])
    outs = take((3, 4, 5)[mode])
    acc, col, wide, fcol, geo, held = rest
    boxes = slabs * BOXES_DEV
    member = meta[0]
    own_row, own_col = member // plane, member % plane

    total = jnp.zeros((SUB, BLOCK), f32)
    for i in range(rows):
        for j in range(plane):
            tile = bundles[i][j]
            total = total + tile
            other = lax.bitwise_xor(own_row, i) * plane + lax.bitwise_xor(own_col, j) - member
            k = jnp.where(other < 0, other + slabs, other) * BOXES_DEV
            for box in range(BOXES_DEV):
                for c in range(3):
                    wide[k + box, c] = spread(tile, box * 3 + c)
    sums = jnp.sum(total, axis=1, keepdims=True)
    moment = [surface * (sums[c : c + 1] + sums[3 + c : 4 + c]) for c in range(3)]

    if mode:
        halo = halo_tiles(meta, near, bundles, held, plane, slabs, reach)
    else:
        halo = [first[k][5:8] for k in range(2 * reach)]
    columns(halo, 3, col)
    for t in range(tiles):
        for c in range(3):
            acc[t, c] = jnp.zeros((SUB, BLOCK), f32)
    def visit(code):
        index, h, c = unpack(code)
        sofar = [acc[c, k] for k in range(3)]
        for step in range(BLOCK // SUB):
            at = slice(step * SUB, (step + 1) * SUB)
            new = apply_tensor(
                [halo_tab[index, k, at, :] for k in range(4)], [col[h, k, at, :] for k in range(3)]
            )
            sofar = [a + n for a, n in zip(sofar, new)]
        for k in range(3):
            acc[c, k] = sofar[k]

    walk(codes, 0, codes[codes.shape[0] - 1], visit)

    if not kept:
        far_geometry(nodes, geo, box_height)
    far_nodes(table, geo, wide, fcol, boxes, box_height, length_z)

    per = tiles // BOXES_DEV
    zero = jnp.zeros((5, BLOCK), f32)
    fields = []
    for t in range(tiles):
        box = t // per
        sofar = [acc[t, c] for c in range(3)]
        for step in range(BLOCK // SUB):
            at = slice(step * SUB, (step + 1) * SUB)
            value = phi[t, at, :]
            sofar = [a + value * fcol[box, c, at, :] for c, a in enumerate(sofar)]
        rows = [row_sum(a) - m for a, m in zip(sofar, moment)]
        value = jnp.concatenate(rows + [zero], axis=0)
        if t < parts[0].shape[0]:
            value = value + parts[0][t]
        if t >= half:
            value = value + parts[1][t - half]
        fields.append(value)

    def alpha(t):
        return spread(stat[t], 5)

    none = jnp.zeros((1, BLOCK), f32)

    def send(u, payload, scalar):
        weights = jnp.concatenate(project(phi, u, tiles) + [scalar, none], axis=0)
        pack(weights, tiles, reach, lambda k: u[k], payload, True)

    def fold(terms):
        out = terms[0]
        for x in terms[1:]:
            out = out + x
        return row_sum(out)

    if mode == 0:
        res, u, payload = outs
        dots = []
        for t in range(tiles):
            scaled = alpha(t) * fields[t]
            res[t] = fields[t]
            u[t] = scaled
            dots.append(scaled * fields[t])
        send(u, payload, fold(dots))
    elif mode == 1:
        image, u, payload, norm = outs
        dots = []
        for t in range(tiles):
            w = v[t] / alpha(t) - fields[t]
            image[t] = w
            u[t] = alpha(t) * w
            dots.append(v[t] * w)
        norm[...] = jnp.broadcast_to(sums[6:7], (SUB, BLOCK))
        send(u, payload, fold(dots))
    else:
        first, res, w0, norm = extra
        x1, r1, z1, q1, scal = outs
        rate = norm[...] / jnp.broadcast_to(sums[6:7], (SUB, BLOCK))
        one, two, three = [], [], []
        for t in range(tiles):
            y = v[t] / alpha(t) - fields[t]
            r = res[t] - rate * w0[t]
            z = alpha(t) * r
            q = w0[t] - rate * y
            x1[t] = first[t] + rate * (alpha(t) * res[t])
            r1[t] = r
            z1[t] = z
            q1[t] = q
            one.append(r * z)
            two.append(z * q)
            three.append(z * w0[t])
        scal[...] = jnp.concatenate(
            [fold(one), fold(two), fold(three), jnp.broadcast_to(sums[6:7], (1, BLOCK)), norm[0:1], none, none, none],
            axis=0,
        )


def last_body(scal, stat, res, w0, x1, r1, z1, q1, *rest, tiles):
    gathered, (dip, out) = rest[:-2], rest[-2:]
    total = gathered[0][...]
    for ref in gathered[1:]:
        total = total + ref[...]
    sums = jnp.sum(total, axis=1, keepdims=True)

    def value(x):
        return jnp.broadcast_to(x, (1, BLOCK))

    norm, curve, cross = value(sums[0:1]), value(sums[1:2]), value(sums[2:3])
    along, start = scal[3:4], scal[4:5]
    beta = norm / start
    rate = norm / (curve + 2.0 * beta * cross + beta * beta * along)
    for t in range(tiles):
        at = slice(t * BLOCK, (t + 1) * BLOCK)
        u0 = stat[t][5:6] * res[t][0:3]
        p = z1[t][0:3] + beta * u0
        w = q1[t][0:3] + beta * w0[t][0:3]
        dip[:, at] = x1[t][0:3] + rate * p
        out[:, at] = r1[t][0:3] - rate * w


def swap(x, axes, count):
    got = [x]
    for s in range(1, count):
        got.append(lax.ppermute(x, axes, [(i, i ^ s) for i in range(count)]))
    return got


def on_device(positions, polarizability, permanent_field, group_id, pair_mask):
    slabs = lax.axis_size(RING)
    member = lax.axis_index(RING)
    plane = lax.axis_size(("oct", "sub"))
    rows = lax.axis_size("blk")
    atoms = positions.shape[1]
    tiles = atoms // BLOCK
    length_z = layer_gap * atoms * slabs / 256.0
    boxes = BOXES_DEV * slabs
    box_height = length_z / boxes
    reach = (pair_mask.shape[1] - 1) // 2
    surface = 4.0 * math.pi / 3.0 / (side_length * side_length * length_z)
    coeff, picks, nodes = node_tables()
    nodes = jnp.asarray(nodes)
    meta = jnp.reshape(member, (1,)).astype(jnp.int32)
    mask = pair_mask
    tile_shape = (tiles, 8, BLOCK)
    kept = (boxes - 1) * 4 * BLOCK * BLOCK * 4 <= TABLE_LIMIT

    half = tiles // 2

    def far_memory(x):
        return pltpu.with_memory_space_constraint(x, pltpu.HBM)

    stat, x0, phi, payload = call(
        functools.partial(first_body, coeff=coeff, box_height=box_height, tiles=tiles, reach=reach),
        [tile_shape, tile_shape, (tiles, BLOCK, BLOCK), (1 + 2 * reach, 8, BLOCK)],
        [meta] + [far_memory(x) for x in (positions, polarizability[None], permanent_field, group_id[None], jnp.asarray(picks))],
        smem=1,
        limit=16 << 20,
        far=5,
        more=[
            pltpu.VMEM((3, atoms), f32),
            pltpu.VMEM((1, atoms), f32),
            pltpu.VMEM((3, atoms), f32),
            pltpu.VMEM((1, atoms), jnp.int32),
            pltpu.VMEM(picks.shape, f32),
            pltpu.SemaphoreType.DMA((5,)),
        ],
    )
    count = own_slots(0, tiles, tiles, reach)
    tab, own_list, halo_list = call(
        functools.partial(tensors_body, half=half, tiles=tiles, reach=reach, length_z=length_z),
        [(count, 4, BLOCK, BLOCK)],
        [far_memory(mask), stat],
        far=1,
        scratch=[(tiles, 5, BLOCK, BLOCK)],
        more=[pltpu.SMEM(mask.shape, jnp.int32), pltpu.SemaphoreType.DMA],
        cost=pl.CostEstimate(flops=count * BLOCK * BLOCK * 70, bytes_accessed=1 << 20, transcendentals=count * BLOCK * BLOCK * 2),
        pinned=(0,),
        lists=(count - tiles + 2, len(halo_pairs(tiles, reach)) + 1),
    )
    table = []
    if kept:
        table = call(
            functools.partial(far_tensors_body, box_height=box_height, length_z=length_z),
            [(BLOCK // SUB, boxes - 1, 4, SUB, BLOCK)],
            [nodes],
            scratch=[(4, BLOCK, BLOCK)],
            cost=pl.CostEstimate(flops=boxes * BLOCK * BLOCK * 28, bytes_accessed=1 << 20, transcendentals=boxes * BLOCK * BLOCK),
            pinned=(0,),
        )

    def own_field(v, begin, end, after):
        top = min(end + reach, tiles) - begin
        return call(
            functools.partial(own_body, begin=begin, end=end, tiles=tiles, reach=reach),
            [(top, 8, BLOCK)],
            [own_list, v, tab] + after,
            smem=1,
            scratch=[
                (end - begin, 3, BLOCK, BLOCK),
                (top, 3, SUB, BLOCK),
                (end - begin, 3, BLOCK, BLOCK),
                (top, 3, SUB, BLOCK),
            ],
            cost=pl.CostEstimate(flops=72 * BLOCK * BLOCK * 18, bytes_accessed=1 << 20, transcendentals=0),
        )[0]

    def exchange(payload, v):
        near = swap(payload, ("oct", "sub"), plane)
        first = own_field(v, 0, half, [])
        bundle = call(
            functools.partial(relay_body, plane=plane, reach=reach),
            [(plane + payload.shape[0] - 1, 8, BLOCK)],
            [meta] + near + [first],
            smem=1,
            scratch=[(plane, payload.shape[0] - 1, 8, BLOCK)],
        )[0]
        bundles = swap(bundle, "blk", rows)
        second = own_field(v, half, tiles, [bundle])
        return [first, second], near, bundles

    def field(mode, v, parts, near, bundles, extra):
        outs = [
            [tile_shape, tile_shape, (1 + reach, 8, BLOCK)],
            [tile_shape, tile_shape, (1 + reach, 8, BLOCK), (SUB, BLOCK)],
            [tile_shape] * 4 + [(8, BLOCK)],
        ][mode]
        return call(
            functools.partial(
                field_body, mode=mode, tiles=tiles, reach=reach, plane=plane, slabs=slabs, box_height=box_height,
                length_z=length_z, surface=surface, kept=kept, half=half,
            ),
            outs,
            [meta, halo_list, nodes, stat, v, phi, halo_tab] + parts + (near if mode else []) + bundles
            + ([] if mode else [edge]) + table + extra,
            smem=2,
            scratch=[
                (tiles, 3, SUB, BLOCK),
                (2 * reach, 3, BLOCK, BLOCK),
                (boxes, 3, SUB, BLOCK),
                (BOXES_DEV, 3, BLOCK, BLOCK),
                (8, BLOCK, BLOCK) if not kept else (1, 8, BLOCK),
                (plane + rows, reach, 8, BLOCK),
            ],
        )

    parts, near, bundles = exchange(payload, x0)
    halo_tab, edge = call(
        functools.partial(
            halo_tensors_body, tiles=tiles, plane=plane, slabs=slabs, reach=reach, length_z=length_z
        ),
        [(len(halo_pairs(tiles, reach)), 4, BLOCK, BLOCK), (2 * reach, 8, BLOCK)],
        [meta, halo_list, stat] + near + bundles,
        smem=2,
        scratch=[(2 * reach, 5, BLOCK, BLOCK), (plane + rows, 2 * reach, 8, BLOCK)],
        pinned=(0,),
    )
    r0, u0, payload = field(0, x0, parts, near, bundles, [])
    parts, near, bundles = exchange(payload, u0)
    w0, u1, payload, norm = field(1, u0, parts, near, bundles, [])
    parts, near, bundles = exchange(payload, u1)
    x1, r1, z1, q1, scal = field(2, u1, parts, near, bundles, [x0, r0, w0, norm])
    sums = swap(scal, ("oct", "sub"), plane)
    sums = swap(functools.reduce(jnp.add, sums), "blk", rows)
    return call(
        functools.partial(last_body, tiles=tiles),
        [(3, atoms), (3, atoms)],
        [scal, stat, r0, w0, x1, r1, z1, q1] + sums,
    )


def solution(mesh):
    split = P(("groups", "blk", "oct", "sub"))
    wide = P(None, ("groups", "blk", "oct", "sub"))
    return jax.shard_map(
        lambda *args: tuple(on_device(*args)),
        mesh=mesh,
        in_specs=(wide, split, wide, split, P(("groups", "blk", "oct", "sub"), None)),
        out_specs=(wide, wide),
        check_vma=False,
    )
```

```python
import functools
import math

import jax
import jax.numpy as jnp
import numpy as np
from jax import lax
from jax.experimental import pallas as pl
from jax.experimental.pallas import tpu as pltpu
from jax.sharding import PartitionSpec as P

BOXES_DEV = 2
BLOCK = 128
ORDER = 5
NODE_PAD = 128
ITERS = 2
SUB = 8
CHUNK = 8

side_length = 32.0
layer_gap = 2.5
thole_damp = 0.39
highest = lax.Precision.HIGHEST
f32 = jnp.float32
RING = ("blk", "oct", "sub")

VM = pl.BlockSpec(memory_space=pltpu.VMEM)
SM = pl.BlockSpec(memory_space=pltpu.SMEM)
FAR = pl.BlockSpec(memory_space=pltpu.HBM)
TABLE_LIMIT = 16 << 20


def call(body, outs, args, smem=0, scratch=(), limit=None, cost=None, pinned=(), far=0, more=(), lists=()):
    shapes = [
        pltpu.VMEM(shape, f32) if at in pinned else jax.ShapeDtypeStruct(shape, f32)
        for at, shape in enumerate(outs)
    ] + [jax.ShapeDtypeStruct((size,), jnp.int32) for size in lists]
    return list(pl.pallas_call(
        body,
        out_shape=shapes,
        in_specs=[SM] * smem + [FAR] * far + [VM] * (len(args) - smem - far),
        out_specs=[VM] * len(outs) + [SM] * len(lists),
        scratch_shapes=[pltpu.VMEM(shape, f32) for shape in scratch] + list(more),
        compiler_params=pltpu.CompilerParams(vmem_limit_bytes=limit or (12 << 20)),
        cost_estimate=cost,
    )(*args))


def node_tables():
    count = ORDER
    roots = np.cos((2.0 * np.arange(count) + 1.0) * np.pi / (2.0 * count))
    degree = np.arange(count)
    coeff = (
        2.0 / count * np.cos(np.outer(2.0 * np.arange(count) + 1.0, degree) * np.pi / (2.0 * count))
    )
    coeff = np.where(degree[None, :] == 0, 1.0 / count, coeff)
    index = np.arange(NODE_PAD)
    live = index < count**3
    safe = np.where(live, index, 0)
    levels = np.stack([safe // (count * count), safe // count % count, safe % count])
    picks = np.zeros((3, NODE_PAD, 6, 8))
    for d in range(3):
        picks[d, index, levels[d], d] = 1.0
    picks[0] *= live[:, None, None]
    picks = np.tile(picks.reshape(3 * NODE_PAD, 48), (1, 3))
    nodes = np.zeros((8, NODE_PAD))
    nodes[0] = 0.5 * (1.0 + roots[levels[0]])
    nodes[1] = 0.5 * (1.0 + roots[levels[1]])
    nodes[2] = 0.5 * roots[levels[2]]
    return coeff.astype(np.float32), picks.astype(np.float32), nodes.astype(np.float32)


def wrap_unit(delta):
    return (delta - jnp.floor(delta + 0.5)) * side_length


def wrap_z(delta, length_z):
    return delta - length_z * jnp.floor(delta * (1.0 / length_z) + 0.5)


def tensor(five, three, dx, dy, dz):
    five = jnp.maximum(five, 1e-36)
    root = five * lax.rsqrt(five)
    return (root * dx, root * dy, root * dz, three)


def columns(tiles, count, out):
    for t, tile in enumerate(tiles):
        for k in range(count):
            out[t, k] = jnp.broadcast_to(tile[k : k + 1, :], (BLOCK, BLOCK)).T


def diagonal(step):
    row = lax.broadcasted_iota(jnp.int32, (SUB, BLOCK), 0)
    lane = lax.broadcasted_iota(jnp.int32, (SUB, BLOCK), 1)
    return lane - row == step * SUB


def spread(tile, k):
    return jnp.broadcast_to(tile[k : k + 1, :], (SUB, BLOCK))


def row_sum(x):
    return jnp.sum(x, axis=0, keepdims=True)


def build_pair(col, rows, put, length_z):
    wide = [jnp.broadcast_to(r, (CHUNK, BLOCK)) for r in rows]
    for step in range(BLOCK // CHUNK):
        at = slice(step * CHUNK, (step + 1) * CHUNK)
        dx = wrap_unit(col(0, at) - wide[0])
        dy = wrap_unit(col(1, at) - wide[1])
        dz = wrap_z(col(2, at) - wide[2], length_z)
        keep = col(4, at) != wide[4]
        dist = jnp.where(keep, dx * dx + dy * dy + dz * dz, 1e24)
        inv = lax.rsqrt(dist)
        inv_two = inv * inv
        inv_three = inv * inv_two
        s = dist * (dist * inv) * (col(3, at) * wide[3])
        decay = jnp.exp(-s)
        small = s * (1.0 - s * (0.5 - s * (1.0 / 6.0 - s * (1.0 / 24.0))))
        three = jnp.where(s < 0.015625, small, 1.0 - decay)
        five = ((three - s * decay) * inv_three) * (3.0 * inv_two)
        for k, value in enumerate(tensor(five, three * inv_three, dx, dy, dz)):
            put(k, at, value)


def lane_sums(parts):
    total = None
    for step, x in enumerate(parts):
        term = jnp.where(diagonal(step), jnp.sum(x, axis=1, keepdims=True), 0.0)
        total = term if total is None else total + term
    return total


def project(phi, v, tiles):
    out = []
    per = tiles // BOXES_DEV
    for box in range(BOXES_DEV):
        wide = [[spread(v[box * per + t], c) for c in range(3)] for t in range(per)]
        parts = [[], [], []]
        for step in range(BLOCK // SUB):
            at = slice(step * SUB, (step + 1) * SUB)
            sums = [None] * 3
            for t in range(per):
                value = phi[box * per + t, at, :]
                for c in range(3):
                    term = value * wide[t][c]
                    sums[c] = term if sums[c] is None else sums[c] + term
            for c in range(3):
                parts[c].append(sums[c])
        out += [row_sum(lane_sums(p)) for p in parts]
    return out


def pack(weights, tiles, reach, get, payload, both):
    payload[0] = weights
    for k in range(reach):
        low, high = get(k), get(tiles - reach + k)
        if both:
            rows = [low[0:3], high[0:3], jnp.zeros((2, BLOCK), f32)]
            payload[1 + k] = jnp.concatenate(rows, axis=0)
        else:
            payload[1 + k] = low
            payload[1 + reach + k] = high


def relay_body(meta, *rest, plane, reach):
    got, (out, held) = rest[:plane], rest[-2:]
    count = held.shape[1]
    for i in range(plane):
        out[i] = got[i][0]
        for k in range(count):
            held[i, k] = got[i][1 + k]
    own = meta[0] % plane
    last = lax.bitwise_xor(own, plane - 1)
    for k in range(count):
        low, high = held[own, k], held[last, k]
        if count == reach:
            out[plane + k] = jnp.concatenate([low[0:3], high[3:6], low[6:8]], axis=0)
        else:
            out[plane + k] = low if k < reach else high


def halo_tiles(meta, near, wide, held, plane, slabs, reach):
    count = held.shape[1]
    for i, ref in enumerate(near):
        for k in range(count):
            held[i, k] = ref[1 + k]
    for i, ref in enumerate(wide):
        for k in range(count):
            held[plane + i, k] = ref[plane + k]
    own_row, own_col = meta[0] // plane, meta[0] % plane
    rows = slabs // plane
    below = jnp.where(own_row == 0, rows - 1, own_row - 1)
    above = jnp.where(own_row == rows - 1, 0, own_row + 1)
    low = jnp.where(
        own_col > 0,
        lax.bitwise_xor(own_col, jnp.maximum(own_col - 1, 0)),
        plane + lax.bitwise_xor(own_row, below),
    )
    high = jnp.where(
        own_col < plane - 1,
        lax.bitwise_xor(own_col, jnp.minimum(own_col + 1, plane - 1)),
        plane + lax.bitwise_xor(own_row, above),
    )
    if count == reach:
        return [held[low, k][3:6] for k in range(reach)] + [held[high, k][0:3] for k in range(reach)]
    return [held[low, reach + k] for k in range(reach)] + [held[high, k] for k in range(reach)]


def first_body(
    meta, pos_in, alpha_in, field_in, gid_in, picks_in, stat, x0, phi, payload,
    pos, alpha, field, gid, picks, sems, *, coeff, box_height, tiles, reach
):
    pairs = [(pos_in, pos), (alpha_in, alpha), (field_in, field), (gid_in, gid), (picks_in, picks)]
    copies = [pltpu.make_async_copy(a, b, sems.at[k]) for k, (a, b) in enumerate(pairs)]
    for copy in copies:
        copy.start()
    for copy in copies:
        copy.wait()
    total = tiles * BLOCK
    lane = lax.broadcasted_iota(jnp.int32, (1, total), 1)
    first = meta[0] * BOXES_DEV
    box = jnp.where(lane < total // BOXES_DEV, first, first + 1).astype(f32)
    p = pos[...]
    al = alpha[...]
    side = jnp.concatenate([p, jnp.zeros((5, total), f32)], axis=0)
    tall = lax.broadcasted_iota(jnp.int32, (8, total), 0) == 2
    u = jnp.where(tall, 2.0 * (side - box * box_height) / box_height - 1.0, side / 16.0 - 1.0)
    terms = [None, u]
    for degree in range(2, ORDER):
        prev = terms[-2] if degree > 2 else 1.0
        terms.append(2.0 * u * terms[-1] - prev)
    levels = []
    for k in range(ORDER):
        value = float(coeff[k, 0]) + float(coeff[k, 1]) * terms[1]
        for n in range(2, ORDER):
            value = value + float(coeff[k, n]) * terms[n]
        levels.append(value)
    levels = jnp.concatenate(levels + [jnp.zeros((8, total), f32)] * (6 - ORDER), axis=0)
    pieces = []
    for k in range(3):
        pieces.append(levels.astype(jnp.bfloat16))
        levels = levels - pieces[-1].astype(f32)
    levels = jnp.concatenate(pieces, axis=0)
    chosen = picks[...].astype(jnp.bfloat16)
    wide = 4 * BLOCK
    for begin in range(0, total, wide):
        value = jnp.dot(chosen, levels[:, begin : begin + wide], preferred_element_type=f32)
        value = value[:BLOCK] * value[BLOCK : 2 * BLOCK] * value[2 * BLOCK :]
        for t in range(4):
            phi[begin // BLOCK + t] = value[:, t * BLOCK : (t + 1) * BLOCK]
    start = al * field[...]
    scaled = jnp.concatenate(
        [
            p[0:2] * (1.0 / side_length),
            p[2:3],
            lax.rsqrt(al) * math.sqrt(thole_damp),
            gid[...].astype(f32),
            al,
            jnp.zeros((2, total), f32),
        ],
        axis=0,
    )
    vec = jnp.concatenate([start, jnp.zeros((5, total), f32)], axis=0)
    for t in range(tiles):
        stat[t] = scaled[:, t * BLOCK : (t + 1) * BLOCK]
        x0[t] = vec[:, t * BLOCK : (t + 1) * BLOCK]
    rows = project(phi, x0, tiles)
    weights = jnp.concatenate(rows + [jnp.zeros((2, BLOCK), f32)], axis=0)

    def get(k):
        return jnp.concatenate([stat[k][0:5], x0[k][0:3]], axis=0)

    pack(weights, tiles, reach, get, payload, False)


def own_slot(b, begin, tiles, reach):
    k = jnp.maximum(b - (tiles - reach), 0)
    return (b - begin) * (reach + 1) - k * (k + 1) // 2


def own_slots(begin, end, tiles, reach):
    return sum(min(reach + 1, tiles - b) for b in range(begin, end))


def walk(codes, begin, end, visit):
    def step(at, code):
        later = codes[at + 1]
        visit(code)
        return later

    lax.fori_loop(begin, end, step, codes[begin])


def unpack(code):
    return code & 255, (code >> 8) & 255, code >> 16


def apply_pair(tab, slot, vec, col, acc_i, acc_j, both):
    acc = [acc_j(c)[...] for c in range(3)] if both else None
    for step in range(BLOCK // SUB):
        at = slice(step * SUB, (step + 1) * SUB)
        t = [tab[slot, k, at, :] for k in range(4)]
        new = apply_tensor(t, vec)
        for c in range(3):
            if both:
                acc_i(c)[at, :] += new[c]
            else:
                acc_i(c)[at, :] = new[c]
        if both:
            new = apply_tensor(t, [col(c, at) for c in range(3)])
            acc = [a + n for a, n in zip(acc, new)]
    if both:
        for c in range(3):
            acc_j(c)[...] = acc[c]


def gather_sums(out, acc_i, acc_j, tall, count):
    for t in range(tall):
        rows = []
        for c in range(3):
            total = acc_j[t, c]
            if t < count:
                parts = [acc_i[t, c, k * SUB : (k + 1) * SUB, :] for k in range(BLOCK // SUB)]
                total = total + lane_sums(parts)
            rows.append(row_sum(total))
        out[t] = jnp.concatenate(rows + [jnp.zeros((5, BLOCK), f32)], axis=0)


def tensors_body(
    mask_in, stat, v, out, near, own_list, halo_list, col, acc_i, acc_j, wide, mask, sem, *, half, tiles, reach, length_z
):
    copy = pltpu.make_async_copy(mask_in, mask, sem)
    copy.start()
    columns([jnp.concatenate([stat[t][0:5], v[t][0:3]], axis=0) for t in range(tiles)], 8, col)
    for t in range(tiles):
        for c in range(3):
            acc_j[t, c] = jnp.zeros((SUB, BLOCK), f32)
            wide[t, c] = spread(v[t], c)
    copy.wait()
    last = own_list.shape[0] - 2
    n = jnp.int32(0)
    for b in range(tiles):
        if b == half:
            own_list[last] = n
        k = max(b - (tiles - reach), 0)
        slot = b * (reach + 1) - k * (k + 1) // 2
        for o in range(1, min(reach + 1, tiles - b)):
            own_list[n] = jnp.int32(slot + o + (b << 8) + ((b + o) << 16))
            n = n + mask[b, reach + o]
    own_list[last + 1] = n
    m = jnp.int32(0)
    for index, (h, c, at) in enumerate(halo_pairs(tiles, reach)):
        halo_list[m] = jnp.int32(index + (h << 8) + (c << 16))
        m = m + mask[c, at]
    halo_list[halo_list.shape[0] - 1] = m

    def pair(slot, b, other, both):
        tile = stat[other]
        rows = [tile[k : k + 1, :] for k in range(5)]

        def store(k, at, value):
            out[slot, k, at, :] = value

        build_pair(lambda k, at: col[b, k, at, :], rows, store, length_z)
        apply_pair(
            out,
            slot,
            [wide[other, c] for c in range(3)],
            lambda c, at: col[b, 5 + c, at, :],
            lambda c: acc_i.at[b, c],
            lambda c: acc_j.at[other, c],
            both,
        )

    def alone(b, unused):
        pair(own_slot(b, 0, tiles, reach), b, b, False)
        return unused

    lax.fori_loop(0, tiles, alone, 0)
    walk(own_list, 0, n, lambda code: pair(*unpack(code), True))
    gather_sums(near, acc_i, acc_j, tiles, tiles)


def own_body(codes, v, tab, *rest, begin, end, tiles, reach):
    out, acc_i, acc_j, col, wide = rest[-5:]
    top = min(end + reach, tiles)
    columns([v[t] for t in range(begin, end)], 3, col)
    for t in range(top - begin):
        for c in range(3):
            acc_j[t, c] = jnp.zeros((SUB, BLOCK), f32)
            wide[t, c] = spread(v[begin + t], c)

    def pair(slot, b, other, both):
        at_b, at_o = b - begin, other - begin
        apply_pair(
            tab,
            slot,
            [wide[at_o, c] for c in range(3)],
            lambda c, at: col[at_b, c, at, :],
            lambda c: acc_i.at[at_b, c],
            lambda c: acc_j.at[at_o, c],
            both,
        )

    def alone(b, unused):
        pair(own_slot(b, 0, tiles, reach), b, b, False)
        return unused

    lax.fori_loop(begin, end, alone, 0)
    last = codes.shape[0] - 2
    walk(
        codes,
        codes[last] if begin else 0,
        codes[last + 1] if begin else codes[last],
        lambda code: pair(*unpack(code), True),
    )
    gather_sums(out, acc_i, acc_j, top - begin, end - begin)


def halo_pairs(tiles, reach):
    pairs = []
    for l in range(reach):
        for c in range(l + 1):
            pairs.append((l, c, l - c))
    for l in range(reach):
        for c in range(tiles - reach + l, tiles):
            pairs.append((reach + l, c, reach + tiles + l - c))
    return pairs


def far_geometry(nodes, geo, box_height):
    turned = nodes[...].T
    row = nodes[...]

    def delta(k):
        return jnp.broadcast_to(turned[:, k : k + 1], (BLOCK, BLOCK)) - jnp.broadcast_to(
            row[k : k + 1, :], (BLOCK, BLOCK)
        )

    dx, dy = wrap_unit(delta(0)), wrap_unit(delta(1))
    geo[0] = dx
    geo[1] = dy
    geo[2] = box_height * delta(2)
    geo[3] = dx * dx + dy * dy + box_height * box_height


def far_tensor(geo, shift, put, length_z, wrapped):
    for step in range(BLOCK // CHUNK):
        at = slice(step * CHUNK, (step + 1) * CHUNK)
        dx, dy = geo[0, at, :], geo[1, at, :]
        dz = geo[2, at, :] - shift
        if wrapped:
            dz = wrap_z(dz, length_z)
        inv = lax.rsqrt(geo[3, at, :] + dz * dz)
        inv_two = inv * inv
        root = (math.sqrt(3.0) * inv_two) * (inv * lax.rsqrt(inv))
        for k, value in enumerate((root * dx, root * dy, root * dz, inv * inv_two)):
            put(k, at, value)


def far_tensors_body(nodes, after, out, geo, *, boxes, box_height, length_z):
    far_geometry(nodes, geo, box_height)

    def visit(d, shift, wrapped):
        def put(k, at, value):
            out[at.start // SUB, d - 1, k] = value

        far_tensor(geo, shift.astype(f32) * box_height, put, length_z, wrapped)

    def below(d, unused):
        visit(d, d, False)
        return unused

    def above(d, unused):
        visit(d, d - boxes, False)
        return unused

    lax.fori_loop(1, boxes // 2, below, 0)
    visit(boxes // 2, jnp.int32(boxes // 2), True)
    lax.fori_loop(boxes // 2 + 1, boxes, above, 0)


def apply_tensor(t, v):
    ex, ey, ez, three = t
    x, y, z = v
    along = ex * x + ey * y + ez * z
    return (ex * along - three * x, ey * along - three * y, ez * along - three * z)


def far_nodes(table, geo, wide, fcol, boxes, box_height, length_z):
    if table is not None:
        def rows(step, unused):
            ats = [pl.ds(pl.multiple_of(step * SUB, SUB), SUB)]

            def load(d):
                return [[table[step, d - 1, k] for k in range(4)]]

            def field(ts, k):
                v = [wide[k, c] for c in range(3)]
                return sum([apply_tensor(t, v) for t in ts], ())

            acc = field(load(boxes - 1), boxes - 1) + field(load(1), 2)
            def visit(d, acc):
                ts = load(d)
                new = field(ts, d) + field(ts, d + 1)
                return tuple(a + n for a, n in zip(acc, new))

            acc = visit(2, acc)
            acc = lax.fori_loop(3, boxes - 1, visit, acc, unroll=14)
            for box in range(BOXES_DEV):
                for c in range(3):
                    fcol[box, c, ats[0], :] = acc[box * 3 + c]
            return unused

        lax.fori_loop(0, BLOCK // SUB, rows, 0)
        for box in range(BOXES_DEV):
            for c in range(3):
                fcol[box, c] = jnp.broadcast_to(
                    jnp.sum(fcol[box, c], axis=1, keepdims=True), (BLOCK, BLOCK)
                )
        return
    for box in range(BOXES_DEV):
        for c in range(3):
            fcol[box, c] = jnp.zeros((BLOCK, BLOCK), f32)

    def visit(d, unused):
        def hold(k, at, value):
            geo[4 + k, at, :] = value

        far_tensor(geo, d.astype(f32) * box_height, hold, length_z, True)
        for box in range(BOXES_DEV):

            @pl.when(d < boxes - 1 if box else d > 1)
            def _():
                v = [wide[d + box, c] for c in range(3)]

                def part(step, skip):
                    at = pl.ds(pl.multiple_of(step * SUB, SUB), SUB)
                    new = apply_tensor([geo[4 + k, at, :] for k in range(4)], v)
                    for c in range(3):
                        fcol[box, c, at, :] += new[c]
                    return skip

                lax.fori_loop(0, BLOCK // SUB, part, 0)

        return unused

    lax.fori_loop(1, boxes, visit, 0)
    for box in range(BOXES_DEV):
        for c in range(3):
            fcol[box, c] = jnp.broadcast_to(
                jnp.sum(fcol[box, c], axis=1, keepdims=True), (BLOCK, BLOCK)
            )


def field_body(meta, codes, nodes, stat, v, phi, *rest,
               mode, tiles, reach, plane, slabs, box_height, length_z, surface, kept, half):
    rest = list(rest)

    def take(count):
        return [rest.pop(0) for _ in range(count)]

    rows = slabs // plane
    parts = take(2 if mode else 1)
    halo_tab = take(1)[0] if mode else None
    near = take(plane)
    bundles = take(rows)
    table = take(1)[0] if kept else None
    extra = take((0, 0, 4)[mode])
    outs = take((3, 4, 5)[mode])
    if not mode:
        halo_tab = take(1)[0]
    acc, col, wide, fcol, geo, held = rest
    boxes = slabs * BOXES_DEV
    member = meta[0]
    own_row, own_col = member // plane, member % plane

    total = jnp.zeros((SUB, BLOCK), f32)
    for i in range(rows):
        for j in range(plane):
            tile = bundles[i][j]
            total = total + tile
            other = lax.bitwise_xor(own_row, i) * plane + lax.bitwise_xor(own_col, j) - member
            k = jnp.where(other < 0, other + slabs, other) * BOXES_DEV
            for box in range(BOXES_DEV):
                for c in range(3):
                    wide[k + box, c] = spread(tile, box * 3 + c)
    sums = jnp.sum(total, axis=1, keepdims=True)
    moment = [surface * (sums[c : c + 1] + sums[3 + c : 4 + c]) for c in range(3)]

    halo = halo_tiles(meta, near, bundles, held, plane, slabs, reach)
    lead = 0 if mode else 5
    columns(halo, lead + 3, col)
    for t in range(tiles):
        for c in range(3):
            acc[t, c] = jnp.zeros((SUB, BLOCK), f32)
    def visit(code):
        index, h, c = unpack(code)
        if not mode:
            own = stat[c]
            own_rows = [own[k : k + 1, :] for k in range(5)]

            def store(k, at, value):
                halo_tab[index, k, at, :] = value

            build_pair(lambda k, at: col[h, k, at, :], own_rows, store, length_z)
        sofar = [acc[c, k] for k in range(3)]
        for step in range(BLOCK // SUB):
            at = slice(step * SUB, (step + 1) * SUB)
            new = apply_tensor(
                [halo_tab[index, k, at, :] for k in range(4)], [col[h, lead + k, at, :] for k in range(3)]
            )
            sofar = [a + n for a, n in zip(sofar, new)]
        for k in range(3):
            acc[c, k] = sofar[k]

    walk(codes, 0, codes[codes.shape[0] - 1], visit)

    if not kept:
        far_geometry(nodes, geo, box_height)
    far_nodes(table, geo, wide, fcol, boxes, box_height, length_z)

    per = tiles // BOXES_DEV
    zero = jnp.zeros((5, BLOCK), f32)
    fields = []
    for t in range(tiles):
        box = t // per
        sofar = [acc[t, c] for c in range(3)]
        for step in range(BLOCK // SUB):
            at = slice(step * SUB, (step + 1) * SUB)
            value = phi[t, at, :]
            sofar = [a + value * fcol[box, c, at, :] for c, a in enumerate(sofar)]
        rows = [row_sum(a) - m for a, m in zip(sofar, moment)]
        value = jnp.concatenate(rows + [zero], axis=0)
        if t < parts[0].shape[0]:
            value = value + parts[0][t]
        if mode and t >= half:
            value = value + parts[1][t - half]
        fields.append(value)

    def alpha(t):
        return spread(stat[t], 5)

    none = jnp.zeros((1, BLOCK), f32)

    def send(u, payload, scalar):
        weights = jnp.concatenate(project(phi, u, tiles) + [scalar, none], axis=0)
        pack(weights, tiles, reach, lambda k: u[k], payload, True)

    def fold(terms):
        out = terms[0]
        for x in terms[1:]:
            out = out + x
        return row_sum(out)

    if mode == 0:
        res, u, payload = outs
        dots = []
        for t in range(tiles):
            scaled = alpha(t) * fields[t]
            res[t] = fields[t]
            u[t] = scaled
            dots.append(scaled * fields[t])
        send(u, payload, fold(dots))
    elif mode == 1:
        image, u, payload, norm = outs
        dots = []
        for t in range(tiles):
            w = v[t] / alpha(t) - fields[t]
            image[t] = w
            u[t] = alpha(t) * w
            dots.append(v[t] * w)
        norm[...] = jnp.broadcast_to(sums[6:7], (SUB, BLOCK))
        send(u, payload, fold(dots))
    else:
        first, res, w0, norm = extra
        x1, r1, z1, q1, scal = outs
        rate = norm[...] / jnp.broadcast_to(sums[6:7], (SUB, BLOCK))
        one, two, three = [], [], []
        for t in range(tiles):
            y = v[t] / alpha(t) - fields[t]
            r = res[t] - rate * w0[t]
            z = alpha(t) * r
            q = w0[t] - rate * y
            x1[t] = first[t] + rate * (alpha(t) * res[t])
            r1[t] = r
            z1[t] = z
            q1[t] = q
            one.append(r * z)
            two.append(z * q)
            three.append(z * w0[t])
        scal[...] = jnp.concatenate(
            [fold(one), fold(two), fold(three), jnp.broadcast_to(sums[6:7], (1, BLOCK)), norm[0:1], none, none, none],
            axis=0,
        )


def last_body(scal, stat, res, w0, x1, r1, z1, q1, *rest, tiles):
    gathered, (dip, out) = rest[:-2], rest[-2:]
    total = gathered[0][...]
    for ref in gathered[1:]:
        total = total + ref[...]
    sums = jnp.sum(total, axis=1, keepdims=True)

    def value(x):
        return jnp.broadcast_to(x, (1, BLOCK))

    norm, curve, cross = value(sums[0:1]), value(sums[1:2]), value(sums[2:3])
    along, start = scal[3:4], scal[4:5]
    beta = norm / start
    rate = norm / (curve + 2.0 * beta * cross + beta * beta * along)
    for t in range(tiles):
        at = slice(t * BLOCK, (t + 1) * BLOCK)
        u0 = stat[t][5:6] * res[t][0:3]
        p = z1[t][0:3] + beta * u0
        w = q1[t][0:3] + beta * w0[t][0:3]
        dip[:, at] = x1[t][0:3] + rate * p
        out[:, at] = r1[t][0:3] - rate * w


def swap(x, axes, count):
    got = [x]
    for s in range(1, count):
        got.append(lax.ppermute(x, axes, [(i, i ^ s) for i in range(count)]))
    return got


def on_device(positions, polarizability, permanent_field, group_id, pair_mask):
    slabs = lax.axis_size(RING)
    member = lax.axis_index(RING)
    plane = lax.axis_size(("oct", "sub"))
    rows = lax.axis_size("blk")
    atoms = positions.shape[1]
    tiles = atoms // BLOCK
    length_z = layer_gap * atoms * slabs / 256.0
    boxes = BOXES_DEV * slabs
    box_height = length_z / boxes
    reach = (pair_mask.shape[1] - 1) // 2
    surface = 4.0 * math.pi / 3.0 / (side_length * side_length * length_z)
    coeff, picks, nodes = node_tables()
    nodes = jnp.asarray(nodes)
    meta = jnp.reshape(member, (1,)).astype(jnp.int32)
    mask = pair_mask
    tile_shape = (tiles, 8, BLOCK)
    kept = (boxes - 1) * 4 * BLOCK * BLOCK * 4 <= TABLE_LIMIT

    half = tiles // 2

    def far_memory(x):
        return pltpu.with_memory_space_constraint(x, pltpu.HBM)

    stat, x0, phi, payload = call(
        functools.partial(first_body, coeff=coeff, box_height=box_height, tiles=tiles, reach=reach),
        [tile_shape, tile_shape, (tiles, BLOCK, BLOCK), (1 + 2 * reach, 8, BLOCK)],
        [meta] + [far_memory(x) for x in (positions, polarizability[None], permanent_field, group_id[None], jnp.asarray(picks))],
        smem=1,
        limit=16 << 20,
        far=5,
        more=[
            pltpu.VMEM((3, atoms), f32),
            pltpu.VMEM((1, atoms), f32),
            pltpu.VMEM((3, atoms), f32),
            pltpu.VMEM((1, atoms), jnp.int32),
            pltpu.VMEM(picks.shape, f32),
            pltpu.SemaphoreType.DMA((5,)),
        ],
    )
    count = own_slots(0, tiles, tiles, reach)
    tab, near_zero, own_list, halo_list = call(
        functools.partial(tensors_body, half=half, tiles=tiles, reach=reach, length_z=length_z),
        [(count, 4, BLOCK, BLOCK), tile_shape],
        [far_memory(mask), stat, x0],
        far=1,
        scratch=[
            (tiles, 8, BLOCK, BLOCK),
            (tiles, 3, BLOCK, BLOCK),
            (tiles, 3, SUB, BLOCK),
            (tiles, 3, SUB, BLOCK),
        ],
        more=[pltpu.SMEM(mask.shape, jnp.int32), pltpu.SemaphoreType.DMA],
        cost=pl.CostEstimate(flops=count * BLOCK * BLOCK * 70, bytes_accessed=1 << 20, transcendentals=count * BLOCK * BLOCK * 2),
        limit=18 << 20,
        pinned=(0,),
        lists=(count - tiles + 2, len(halo_pairs(tiles, reach)) + 1),
    )

    def far_tables(after):
        if not kept:
            return []
        return call(
            functools.partial(far_tensors_body, boxes=boxes, box_height=box_height, length_z=length_z),
            [(BLOCK // SUB, boxes - 1, 4, SUB, BLOCK)],
            [nodes, after],
            scratch=[(4, BLOCK, BLOCK)],
            cost=pl.CostEstimate(flops=boxes * BLOCK * BLOCK * 28, bytes_accessed=1 << 20, transcendentals=boxes * BLOCK * BLOCK),
            pinned=(0,),
        )

    def own_field(v, begin, end, after):
        top = min(end + reach, tiles) - begin
        return call(
            functools.partial(own_body, begin=begin, end=end, tiles=tiles, reach=reach),
            [(top, 8, BLOCK)],
            [own_list, v, tab] + after,
            smem=1,
            scratch=[
                (end - begin, 3, BLOCK, BLOCK),
                (top, 3, SUB, BLOCK),
                (end - begin, 3, BLOCK, BLOCK),
                (top, 3, SUB, BLOCK),
            ],
            cost=pl.CostEstimate(flops=72 * BLOCK * BLOCK * 18, bytes_accessed=1 << 20, transcendentals=0),
        )[0]

    def relay(near, after):
        size = near[0].shape[0] - 1
        return call(
            functools.partial(relay_body, plane=plane, reach=reach),
            [(plane + size, 8, BLOCK)],
            [meta] + near + [after],
            smem=1,
            scratch=[(plane, size, 8, BLOCK)],
        )[0]

    def exchange(payload, v):
        near = swap(payload, ("oct", "sub"), plane)
        first = own_field(v, 0, half, [])
        bundle = relay(near, first)
        bundles = swap(bundle, "blk", rows)
        second = own_field(v, half, tiles, [bundle])
        return [first, second], near, bundles

    def field(mode, v, parts, halo_tab, near, bundles, extra):
        outs = [
            [tile_shape, tile_shape, (1 + reach, 8, BLOCK), (len(halo_pairs(tiles, reach)), 4, BLOCK, BLOCK)],
            [tile_shape, tile_shape, (1 + reach, 8, BLOCK), (SUB, BLOCK)],
            [tile_shape] * 4 + [(8, BLOCK)],
        ][mode]
        return call(
            functools.partial(
                field_body, mode=mode, tiles=tiles, reach=reach, plane=plane, slabs=slabs, box_height=box_height,
                length_z=length_z, surface=surface, kept=kept, half=half,
            ),
            outs,
            [meta, halo_list, nodes, stat, v, phi] + parts + halo_tab + near + bundles + table + extra,
            smem=2,
            pinned=() if mode else (3,),
            scratch=[
                (tiles, 3, SUB, BLOCK),
                (2 * reach, 3 if mode else 8, BLOCK, BLOCK),
                (boxes, 3, SUB, BLOCK),
                (BOXES_DEV, 3, BLOCK, BLOCK),
                (8, BLOCK, BLOCK) if not kept else (1, 8, BLOCK),
                (plane + rows, reach if mode else 2 * reach, 8, BLOCK),
            ],
        )

    near = swap(payload, ("oct", "sub"), plane)
    bundle = relay(near, near_zero)
    bundles = swap(bundle, "blk", rows)
    table = far_tables(bundle)
    r0, u0, payload, halo_tab = field(0, x0, [near_zero], [], near, bundles, [])
    parts, near, bundles = exchange(payload, u0)
    w0, u1, payload, norm = field(1, u0, parts, [halo_tab], near, bundles, [])
    parts, near, bundles = exchange(payload, u1)
    x1, r1, z1, q1, scal = field(2, u1, parts, [halo_tab], near, bundles, [x0, r0, w0, norm])
    sums = swap(scal, ("oct", "sub"), plane)
    sums = swap(functools.reduce(jnp.add, sums), "blk", rows)
    return call(
        functools.partial(last_body, tiles=tiles),
        [(3, atoms), (3, atoms)],
        [scal, stat, r0, w0, x1, r1, z1, q1] + sums,
    )


def solution(mesh):
    split = P(("groups", "blk", "oct", "sub"))
    wide = P(None, ("groups", "blk", "oct", "sub"))
    return jax.shard_map(
        lambda *args: tuple(on_device(*args)),
        mesh=mesh,
        in_specs=(wide, split, wide, split, P(("groups", "blk", "oct", "sub"), None)),
        out_specs=(wide, wide),
        check_vma=False,
    )
```

```python
import functools
import math

import jax
import jax.numpy as jnp
import numpy as np
from jax import lax
from jax.experimental import pallas as pl
from jax.experimental.pallas import tpu as pltpu
from jax.sharding import PartitionSpec as P

BOXES_DEV = 2
BLOCK = 128
ORDER = 5
NODE_PAD = 128
ITERS = 2
SUB = 8
CHUNK = 8

side_length = 32.0
layer_gap = 2.5
thole_damp = 0.39
highest = lax.Precision.HIGHEST
f32 = jnp.float32
RING = ("blk", "oct", "sub")

VM = pl.BlockSpec(memory_space=pltpu.VMEM)
SM = pl.BlockSpec(memory_space=pltpu.SMEM)
FAR = pl.BlockSpec(memory_space=pltpu.HBM)
TABLE_LIMIT = 16 << 20


def call(body, outs, args, smem=0, scratch=(), limit=None, cost=None, pinned=(), far=0, more=(), lists=()):
    shapes = [
        pltpu.VMEM(shape, f32) if at in pinned else jax.ShapeDtypeStruct(shape, f32)
        for at, shape in enumerate(outs)
    ] + [jax.ShapeDtypeStruct((size,), jnp.int32) for size in lists]
    return list(pl.pallas_call(
        body,
        out_shape=shapes,
        in_specs=[SM] * smem + [FAR] * far + [VM] * (len(args) - smem - far),
        out_specs=[VM] * len(outs) + [SM] * len(lists),
        scratch_shapes=[pltpu.VMEM(shape, f32) for shape in scratch] + list(more),
        compiler_params=pltpu.CompilerParams(vmem_limit_bytes=limit or (12 << 20)),
        cost_estimate=cost,
    )(*args))


def node_tables():
    count = ORDER
    roots = np.cos((2.0 * np.arange(count) + 1.0) * np.pi / (2.0 * count))
    degree = np.arange(count)
    coeff = (
        2.0 / count * np.cos(np.outer(2.0 * np.arange(count) + 1.0, degree) * np.pi / (2.0 * count))
    )
    coeff = np.where(degree[None, :] == 0, 1.0 / count, coeff)
    index = np.arange(NODE_PAD)
    live = index < count**3
    safe = np.where(live, index, 0)
    levels = np.stack([safe // (count * count), safe // count % count, safe % count])
    picks = np.zeros((3, NODE_PAD, 6, 8))
    for d in range(3):
        picks[d, index, levels[d], d] = 1.0
    picks[0] *= live[:, None, None]
    picks = np.tile(picks.reshape(3 * NODE_PAD, 48), (1, 3))
    nodes = np.zeros((8, NODE_PAD))
    nodes[0] = 0.5 * (1.0 + roots[levels[0]])
    nodes[1] = 0.5 * (1.0 + roots[levels[1]])
    nodes[2] = 0.5 * roots[levels[2]]
    return coeff.astype(np.float32), picks.astype(np.float32), nodes.astype(np.float32)


def wrap_unit(delta):
    return (delta - jnp.floor(delta + 0.5)) * side_length


def wrap_z(delta, length_z):
    return delta - length_z * jnp.floor(delta * (1.0 / length_z) + 0.5)


def tensor(five, three, dx, dy, dz):
    five = jnp.maximum(five, 1e-36)
    root = five * lax.rsqrt(five)
    return (root * dx, root * dy, root * dz, three)


def columns(tiles, count, out):
    for t, tile in enumerate(tiles):
        for k in range(count):
            out[t, k] = jnp.broadcast_to(tile[k : k + 1, :], (BLOCK, BLOCK)).T


def diagonal(step):
    row = lax.broadcasted_iota(jnp.int32, (SUB, BLOCK), 0)
    lane = lax.broadcasted_iota(jnp.int32, (SUB, BLOCK), 1)
    return lane - row == step * SUB


def spread(tile, k):
    return jnp.broadcast_to(tile[k : k + 1, :], (SUB, BLOCK))


def row_sum(x):
    return jnp.sum(x, axis=0, keepdims=True)


def build_pair(col, rows, put, length_z, rows_target=False):
    wide = [jnp.broadcast_to(r, (CHUNK, BLOCK)) for r in rows]
    for step in range(BLOCK // CHUNK):
        at = slice(step * CHUNK, (step + 1) * CHUNK)
        gap = [wide[k] - col(k, at) if rows_target else col(k, at) - wide[k] for k in range(3)]
        dx, dy, dz = wrap_unit(gap[0]), wrap_unit(gap[1]), wrap_z(gap[2], length_z)
        keep = col(4, at) != wide[4]
        dist = jnp.where(keep, dx * dx + dy * dy + dz * dz, 1e24)
        inv = lax.rsqrt(dist)
        inv_two = inv * inv
        inv_three = inv * inv_two
        s = dist * (dist * inv) * (col(3, at) * wide[3])
        decay = jnp.exp(-s)
        small = s * (1.0 - s * (0.5 - s * (1.0 / 6.0 - s * (1.0 / 24.0))))
        three = jnp.where(s < 0.015625, small, 1.0 - decay)
        five = ((three - s * decay) * inv_three) * (3.0 * inv_two)
        for k, value in enumerate(tensor(five, three * inv_three, dx, dy, dz)):
            put(k, at, value)


def lane_sums(parts):
    total = None
    for step, x in enumerate(parts):
        term = jnp.where(diagonal(step), jnp.sum(x, axis=1, keepdims=True), 0.0)
        total = term if total is None else total + term
    return total


def project(phi, v, tiles):
    out = []
    per = tiles // BOXES_DEV
    for box in range(BOXES_DEV):
        wide = [[spread(v[box * per + t], c) for c in range(3)] for t in range(per)]
        parts = [[], [], []]
        for step in range(BLOCK // SUB):
            at = slice(step * SUB, (step + 1) * SUB)
            sums = [None] * 3
            for t in range(per):
                value = phi[box * per + t, at, :]
                for c in range(3):
                    term = value * wide[t][c]
                    sums[c] = term if sums[c] is None else sums[c] + term
            for c in range(3):
                parts[c].append(sums[c])
        out += [row_sum(lane_sums(p)) for p in parts]
    return out


def pack(weights, tiles, reach, get, payload, both):
    payload[0] = weights
    for k in range(reach):
        low, high = get(k), get(tiles - reach + k)
        if both:
            rows = [low[0:3], high[0:3], jnp.zeros((2, BLOCK), f32)]
            payload[1 + k] = jnp.concatenate(rows, axis=0)
        else:
            payload[1 + k] = low
            payload[1 + reach + k] = high


def relay_body(meta, *rest, plane, reach):
    got, (out, held) = rest[:plane], rest[-2:]
    count = held.shape[1]
    for i in range(plane):
        out[i] = got[i][0]
        for k in range(count):
            held[i, k] = got[i][1 + k]
    own = meta[0] % plane
    last = lax.bitwise_xor(own, plane - 1)
    for k in range(count):
        low, high = held[own, k], held[last, k]
        if count == reach:
            out[plane + k] = jnp.concatenate([low[0:3], high[3:6], low[6:8]], axis=0)
        else:
            out[plane + k] = low if k < reach else high


def halo_tiles(meta, near, wide, held, plane, slabs, reach):
    count = held.shape[1]
    for i, ref in enumerate(near):
        for k in range(count):
            held[i, k] = ref[1 + k]
    for i, ref in enumerate(wide):
        for k in range(count):
            held[plane + i, k] = ref[plane + k]
    own_row, own_col = meta[0] // plane, meta[0] % plane
    rows = slabs // plane
    below = jnp.where(own_row == 0, rows - 1, own_row - 1)
    above = jnp.where(own_row == rows - 1, 0, own_row + 1)
    low = jnp.where(
        own_col > 0,
        lax.bitwise_xor(own_col, jnp.maximum(own_col - 1, 0)),
        plane + lax.bitwise_xor(own_row, below),
    )
    high = jnp.where(
        own_col < plane - 1,
        lax.bitwise_xor(own_col, jnp.minimum(own_col + 1, plane - 1)),
        plane + lax.bitwise_xor(own_row, above),
    )
    if count == reach:
        return [held[low, k][3:6] for k in range(reach)] + [held[high, k][0:3] for k in range(reach)]
    return [held[low, reach + k] for k in range(reach)] + [held[high, k] for k in range(reach)]


def first_body(
    meta, pos_in, alpha_in, field_in, gid_in, picks_in, stat, x0, phi, payload,
    pos, alpha, field, gid, picks, sems, *, coeff, box_height, tiles, reach
):
    pairs = [(pos_in, pos), (alpha_in, alpha), (field_in, field), (gid_in, gid), (picks_in, picks)]
    copies = [pltpu.make_async_copy(a, b, sems.at[k]) for k, (a, b) in enumerate(pairs)]
    for copy in copies:
        copy.start()
    for copy in copies:
        copy.wait()
    total = tiles * BLOCK
    lane = lax.broadcasted_iota(jnp.int32, (1, total), 1)
    first = meta[0] * BOXES_DEV
    box = jnp.where(lane < total // BOXES_DEV, first, first + 1).astype(f32)
    p = pos[...]
    al = alpha[...]
    side = jnp.concatenate([p, jnp.zeros((5, total), f32)], axis=0)
    tall = lax.broadcasted_iota(jnp.int32, (8, total), 0) == 2
    u = jnp.where(tall, 2.0 * (side - box * box_height) / box_height - 1.0, side / 16.0 - 1.0)
    terms = [None, u]
    for degree in range(2, ORDER):
        prev = terms[-2] if degree > 2 else 1.0
        terms.append(2.0 * u * terms[-1] - prev)
    levels = []
    for k in range(ORDER):
        value = float(coeff[k, 0]) + float(coeff[k, 1]) * terms[1]
        for n in range(2, ORDER):
            value = value + float(coeff[k, n]) * terms[n]
        levels.append(value)
    levels = jnp.concatenate(levels + [jnp.zeros((8, total), f32)] * (6 - ORDER), axis=0)
    pieces = []
    for k in range(3):
        pieces.append(levels.astype(jnp.bfloat16))
        levels = levels - pieces[-1].astype(f32)
    levels = jnp.concatenate(pieces, axis=0)
    chosen = picks[...].astype(jnp.bfloat16)
    wide = 4 * BLOCK
    for begin in range(0, total, wide):
        value = jnp.dot(chosen, levels[:, begin : begin + wide], preferred_element_type=f32)
        value = value[:BLOCK] * value[BLOCK : 2 * BLOCK] * value[2 * BLOCK :]
        for t in range(4):
            phi[begin // BLOCK + t] = value[:, t * BLOCK : (t + 1) * BLOCK]
    start = al * field[...]
    scaled = jnp.concatenate(
        [
            p[0:2] * (1.0 / side_length),
            p[2:3],
            lax.rsqrt(al) * math.sqrt(thole_damp),
            gid[...].astype(f32),
            al,
            jnp.zeros((2, total), f32),
        ],
        axis=0,
    )
    vec = jnp.concatenate([start, jnp.zeros((5, total), f32)], axis=0)
    for t in range(tiles):
        stat[t] = scaled[:, t * BLOCK : (t + 1) * BLOCK]
        x0[t] = vec[:, t * BLOCK : (t + 1) * BLOCK]
    rows = project(phi, x0, tiles)
    weights = jnp.concatenate(rows + [jnp.zeros((2, BLOCK), f32)], axis=0)

    def get(k):
        return jnp.concatenate([stat[k][0:5], x0[k][0:3]], axis=0)

    pack(weights, tiles, reach, get, payload, False)


def own_slot(b, begin, tiles, reach):
    k = jnp.maximum(b - (tiles - reach), 0)
    return (b - begin) * (reach + 1) - k * (k + 1) // 2


def own_slots(begin, end, tiles, reach):
    return sum(min(reach + 1, tiles - b) for b in range(begin, end))


def walk(codes, begin, end, visit):
    def step(at, code):
        later = codes[at + 1]
        visit(code)
        return later

    lax.fori_loop(begin, end, step, codes[begin])


def unpack(code):
    return code & 255, (code >> 8) & 255, code >> 16


def apply_pair(tab, slot, vec, col, acc_i, acc_j, both):
    acc = [acc_j(c)[...] for c in range(3)] if both else None
    for step in range(BLOCK // SUB):
        at = slice(step * SUB, (step + 1) * SUB)
        t = [tab[slot, k, at, :] for k in range(4)]
        new = apply_tensor(t, vec)
        for c in range(3):
            if both:
                acc_i(c)[at, :] += new[c]
            else:
                acc_i(c)[at, :] = new[c]
        if both:
            new = apply_tensor(t, [col(c, at) for c in range(3)])
            acc = [a + n for a, n in zip(acc, new)]
    if both:
        for c in range(3):
            acc_j(c)[...] = acc[c]


def gather_sums(out, acc_i, acc_j, tall, count):
    for t in range(tall):
        rows = []
        for c in range(3):
            total = acc_j[t, c]
            if t < count:
                parts = [acc_i[t, c, k * SUB : (k + 1) * SUB, :] for k in range(BLOCK // SUB)]
                total = total + lane_sums(parts)
            rows.append(row_sum(total))
        out[t] = jnp.concatenate(rows + [jnp.zeros((5, BLOCK), f32)], axis=0)


def tensors_body(
    mask_in, stat, v, out, near, own_list, halo_list, col, acc_i, acc_j, wide, mask, sem, *, half, tiles, reach, length_z
):
    copy = pltpu.make_async_copy(mask_in, mask, sem)
    copy.start()
    columns([jnp.concatenate([stat[t][0:5], v[t][0:3]], axis=0) for t in range(tiles)], 8, col)
    for t in range(tiles):
        for c in range(3):
            acc_j[t, c] = jnp.zeros((SUB, BLOCK), f32)
            wide[t, c] = spread(v[t], c)
    copy.wait()
    last = own_list.shape[0] - 2
    n = jnp.int32(0)
    for b in range(tiles):
        if b == half:
            own_list[last] = n
        k = max(b - (tiles - reach), 0)
        slot = b * (reach + 1) - k * (k + 1) // 2
        for o in range(1, min(reach + 1, tiles - b)):
            own_list[n] = jnp.int32(slot + o + (b << 8) + ((b + o) << 16))
            n = n + mask[b, reach + o]
    own_list[last + 1] = n
    m = jnp.int32(0)
    for index, (h, c, at) in enumerate(halo_pairs(tiles, reach)):
        halo_list[m] = jnp.int32(index + (h << 8) + (c << 16))
        m = m + mask[c, at]
    halo_list[halo_list.shape[0] - 1] = m

    def pair(slot, b, other, both):
        tile = stat[other]
        rows = [tile[k : k + 1, :] for k in range(5)]

        def store(k, at, value):
            out[slot, k, at, :] = value

        build_pair(lambda k, at: col[b, k, at, :], rows, store, length_z)
        apply_pair(
            out,
            slot,
            [wide[other, c] for c in range(3)],
            lambda c, at: col[b, 5 + c, at, :],
            lambda c: acc_i.at[b, c],
            lambda c: acc_j.at[other, c],
            both,
        )

    def alone(b, unused):
        pair(own_slot(b, 0, tiles, reach), b, b, False)
        return unused

    lax.fori_loop(0, tiles, alone, 0)
    walk(own_list, 0, n, lambda code: pair(*unpack(code), True))
    gather_sums(near, acc_i, acc_j, tiles, tiles)


def own_body(codes, v, tab, *rest, begin, end, tiles, reach):
    out, acc_i, acc_j, col, wide = rest[-5:]
    top = min(end + reach, tiles)
    columns([v[t] for t in range(begin, end)], 3, col)
    for t in range(top - begin):
        for c in range(3):
            acc_j[t, c] = jnp.zeros((SUB, BLOCK), f32)
            wide[t, c] = spread(v[begin + t], c)

    def pair(slot, b, other, both):
        at_b, at_o = b - begin, other - begin
        apply_pair(
            tab,
            slot,
            [wide[at_o, c] for c in range(3)],
            lambda c, at: col[at_b, c, at, :],
            lambda c: acc_i.at[at_b, c],
            lambda c: acc_j.at[at_o, c],
            both,
        )

    def alone(b, unused):
        pair(own_slot(b, 0, tiles, reach), b, b, False)
        return unused

    lax.fori_loop(begin, end, alone, 0)
    last = codes.shape[0] - 2
    walk(
        codes,
        codes[last] if begin else 0,
        codes[last + 1] if begin else codes[last],
        lambda code: pair(*unpack(code), True),
    )
    gather_sums(out, acc_i, acc_j, top - begin, end - begin)


def halo_pairs(tiles, reach):
    pairs = []
    for l in range(reach):
        for c in range(l + 1):
            pairs.append((l, c, l - c))
    for l in range(reach):
        for c in range(tiles - reach + l, tiles):
            pairs.append((reach + l, c, reach + tiles + l - c))
    return pairs


def far_geometry(nodes, geo, box_height):
    turned = nodes[...].T
    row = nodes[...]

    def delta(k):
        return jnp.broadcast_to(turned[:, k : k + 1], (BLOCK, BLOCK)) - jnp.broadcast_to(
            row[k : k + 1, :], (BLOCK, BLOCK)
        )

    dx, dy = wrap_unit(delta(0)), wrap_unit(delta(1))
    geo[0] = dx
    geo[1] = dy
    geo[2] = box_height * delta(2)
    geo[3] = dx * dx + dy * dy + box_height * box_height


def far_tensor(geo, shift, put, length_z, wrapped):
    for step in range(BLOCK // CHUNK):
        at = slice(step * CHUNK, (step + 1) * CHUNK)
        dx, dy = geo[0, at, :], geo[1, at, :]
        dz = geo[2, at, :] - shift
        if wrapped:
            dz = wrap_z(dz, length_z)
        inv = lax.rsqrt(geo[3, at, :] + dz * dz)
        inv_two = inv * inv
        root = (math.sqrt(3.0) * inv_two) * (inv * lax.rsqrt(inv))
        for k, value in enumerate((root * dx, root * dy, root * dz, inv * inv_two)):
            put(k, at, value)


def far_tensors_body(nodes, after, out, geo, *, boxes, box_height, length_z):
    far_geometry(nodes, geo, box_height)

    def visit(d, shift, wrapped):
        def put(k, at, value):
            out[at.start // SUB, d - 1, k] = value

        far_tensor(geo, shift.astype(f32) * box_height, put, length_z, wrapped)

    def below(d, unused):
        visit(d, d, False)
        return unused

    def above(d, unused):
        visit(d, d - boxes, False)
        return unused

    lax.fori_loop(1, boxes // 2, below, 0)
    visit(boxes // 2, jnp.int32(boxes // 2), True)
    lax.fori_loop(boxes // 2 + 1, boxes, above, 0)


def apply_tensor(t, v):
    ex, ey, ez, three = t
    x, y, z = v
    along = ex * x + ey * y + ez * z
    return (ex * along - three * x, ey * along - three * y, ez * along - three * z)


def far_nodes(table, geo, wide, fcol, boxes, box_height, length_z):
    if table is not None:
        def rows(step, unused):
            ats = [pl.ds(pl.multiple_of(step * SUB, SUB), SUB)]

            def load(d):
                return [[table[step, d - 1, k] for k in range(4)]]

            def field(ts, k):
                v = [wide[k, c] for c in range(3)]
                return sum([apply_tensor(t, v) for t in ts], ())

            acc = field(load(boxes - 1), boxes - 1) + field(load(1), 2)
            def visit(d, acc):
                ts = load(d)
                new = field(ts, d) + field(ts, d + 1)
                return tuple(a + n for a, n in zip(acc, new))

            acc = visit(2, acc)
            acc = lax.fori_loop(3, boxes - 1, visit, acc, unroll=14)
            for box in range(BOXES_DEV):
                for c in range(3):
                    fcol[box, c, ats[0], :] = acc[box * 3 + c]
            return unused

        lax.fori_loop(0, BLOCK // SUB, rows, 0)
        for box in range(BOXES_DEV):
            for c in range(3):
                fcol[box, c] = jnp.broadcast_to(
                    jnp.sum(fcol[box, c], axis=1, keepdims=True), (BLOCK, BLOCK)
                )
        return
    for box in range(BOXES_DEV):
        for c in range(3):
            fcol[box, c] = jnp.zeros((BLOCK, BLOCK), f32)

    def visit(d, unused):
        def hold(k, at, value):
            geo[4 + k, at, :] = value

        far_tensor(geo, d.astype(f32) * box_height, hold, length_z, True)
        for box in range(BOXES_DEV):

            @pl.when(d < boxes - 1 if box else d > 1)
            def _():
                v = [wide[d + box, c] for c in range(3)]

                def part(step, skip):
                    at = pl.ds(pl.multiple_of(step * SUB, SUB), SUB)
                    new = apply_tensor([geo[4 + k, at, :] for k in range(4)], v)
                    for c in range(3):
                        fcol[box, c, at, :] += new[c]
                    return skip

                lax.fori_loop(0, BLOCK // SUB, part, 0)

        return unused

    lax.fori_loop(1, boxes, visit, 0)
    for box in range(BOXES_DEV):
        for c in range(3):
            fcol[box, c] = jnp.broadcast_to(
                jnp.sum(fcol[box, c], axis=1, keepdims=True), (BLOCK, BLOCK)
            )


def field_body(meta, codes, nodes, stat, v, phi, *rest,
               mode, tiles, reach, plane, slabs, box_height, length_z, surface, kept, half):
    rest = list(rest)

    def take(count):
        return [rest.pop(0) for _ in range(count)]

    rows = slabs // plane
    parts = take(2 if mode else 1)
    halo_tab = take(1)[0] if mode else None
    near = take(plane)
    bundles = take(rows)
    table = take(1)[0] if kept else None
    extra = take((0, 0, 4)[mode])
    outs = take((3, 4, 5)[mode])
    if not mode:
        halo_tab = take(1)[0]
    acc, col, wide, fcol, geo, held = rest
    boxes = slabs * BOXES_DEV
    member = meta[0]
    own_row, own_col = member // plane, member % plane

    total = jnp.zeros((SUB, BLOCK), f32)
    for i in range(rows):
        for j in range(plane):
            tile = bundles[i][j]
            total = total + tile
            other = lax.bitwise_xor(own_row, i) * plane + lax.bitwise_xor(own_col, j) - member
            k = jnp.where(other < 0, other + slabs, other) * BOXES_DEV
            for box in range(BOXES_DEV):
                for c in range(3):
                    wide[k + box, c] = spread(tile, box * 3 + c)
    sums = jnp.sum(total, axis=1, keepdims=True)
    moment = [surface * (sums[c : c + 1] + sums[3 + c : 4 + c]) for c in range(3)]

    halo = halo_tiles(meta, near, bundles, held, plane, slabs, reach)
    lead = 0 if mode else 5
    columns(halo, lead + 3, col)
    for t in range(tiles):
        for c in range(3):
            acc[t, c] = jnp.zeros((SUB, BLOCK), f32)
    def visit(code):
        index, h, c = unpack(code)
        if not mode:
            own = stat[c]
            own_rows = [own[k : k + 1, :] for k in range(5)]

            def store(k, at, value):
                halo_tab[index, k, at, :] = value

            build_pair(lambda k, at: col[h, k, at, :], own_rows, store, length_z, True)
        sofar = [acc[c, k] for k in range(3)]
        for step in range(BLOCK // SUB):
            at = slice(step * SUB, (step + 1) * SUB)
            new = apply_tensor(
                [halo_tab[index, k, at, :] for k in range(4)], [col[h, lead + k, at, :] for k in range(3)]
            )
            sofar = [a + n for a, n in zip(sofar, new)]
        for k in range(3):
            acc[c, k] = sofar[k]

    walk(codes, 0, codes[codes.shape[0] - 1], visit)

    if not kept:
        far_geometry(nodes, geo, box_height)
    far_nodes(table, geo, wide, fcol, boxes, box_height, length_z)

    per = tiles // BOXES_DEV
    zero = jnp.zeros((5, BLOCK), f32)
    fields = []
    for t in range(tiles):
        box = t // per
        sofar = [acc[t, c] for c in range(3)]
        for step in range(BLOCK // SUB):
            at = slice(step * SUB, (step + 1) * SUB)
            value = phi[t, at, :]
            sofar = [a + value * fcol[box, c, at, :] for c, a in enumerate(sofar)]
        rows = [row_sum(a) - m for a, m in zip(sofar, moment)]
        value = jnp.concatenate(rows + [zero], axis=0)
        if t < parts[0].shape[0]:
            value = value + parts[0][t]
        if mode and t >= half:
            value = value + parts[1][t - half]
        fields.append(value)

    def alpha(t):
        return spread(stat[t], 5)

    none = jnp.zeros((1, BLOCK), f32)

    def send(u, payload, scalar):
        weights = jnp.concatenate(project(phi, u, tiles) + [scalar, none], axis=0)
        pack(weights, tiles, reach, lambda k: u[k], payload, True)

    def fold(terms):
        out = terms[0]
        for x in terms[1:]:
            out = out + x
        return row_sum(out)

    if mode == 0:
        res, u, payload = outs
        dots = []
        for t in range(tiles):
            scaled = alpha(t) * fields[t]
            res[t] = fields[t]
            u[t] = scaled
            dots.append(scaled * fields[t])
        send(u, payload, fold(dots))
    elif mode == 1:
        image, u, payload, norm = outs
        dots = []
        for t in range(tiles):
            w = v[t] / alpha(t) - fields[t]
            image[t] = w
            u[t] = alpha(t) * w
            dots.append(v[t] * w)
        norm[...] = jnp.broadcast_to(sums[6:7], (SUB, BLOCK))
        send(u, payload, fold(dots))
    else:
        first, res, w0, norm = extra
        x1, r1, z1, q1, scal = outs
        rate = norm[...] / jnp.broadcast_to(sums[6:7], (SUB, BLOCK))
        one, two, three = [], [], []
        for t in range(tiles):
            y = v[t] / alpha(t) - fields[t]
            r = res[t] - rate * w0[t]
            z = alpha(t) * r
            q = w0[t] - rate * y
            x1[t] = first[t] + rate * (alpha(t) * res[t])
            r1[t] = r
            z1[t] = z
            q1[t] = q
            one.append(r * z)
            two.append(z * q)
            three.append(z * w0[t])
        scal[...] = jnp.concatenate(
            [fold(one), fold(two), fold(three), jnp.broadcast_to(sums[6:7], (1, BLOCK)), norm[0:1], none, none, none],
            axis=0,
        )


def last_body(scal, stat, res, w0, x1, r1, z1, q1, *rest, tiles):
    gathered, (dip, out) = rest[:-2], rest[-2:]
    total = gathered[0][...]
    for ref in gathered[1:]:
        total = total + ref[...]
    sums = jnp.sum(total, axis=1, keepdims=True)

    def value(x):
        return jnp.broadcast_to(x, (1, BLOCK))

    norm, curve, cross = value(sums[0:1]), value(sums[1:2]), value(sums[2:3])
    along, start = scal[3:4], scal[4:5]
    beta = norm / start
    rate = norm / (curve + 2.0 * beta * cross + beta * beta * along)
    for t in range(tiles):
        at = slice(t * BLOCK, (t + 1) * BLOCK)
        u0 = stat[t][5:6] * res[t][0:3]
        p = z1[t][0:3] + beta * u0
        w = q1[t][0:3] + beta * w0[t][0:3]
        dip[:, at] = x1[t][0:3] + rate * p
        out[:, at] = r1[t][0:3] - rate * w


def swap(x, axes, count):
    got = [x]
    for s in range(1, count):
        got.append(lax.ppermute(x, axes, [(i, i ^ s) for i in range(count)]))
    return got


def on_device(positions, polarizability, permanent_field, group_id, pair_mask):
    slabs = lax.axis_size(RING)
    member = lax.axis_index(RING)
    plane = lax.axis_size(("oct", "sub"))
    rows = lax.axis_size("blk")
    atoms = positions.shape[1]
    tiles = atoms // BLOCK
    length_z = layer_gap * atoms * slabs / 256.0
    boxes = BOXES_DEV * slabs
    box_height = length_z / boxes
    reach = (pair_mask.shape[1] - 1) // 2
    surface = 4.0 * math.pi / 3.0 / (side_length * side_length * length_z)
    coeff, picks, nodes = node_tables()
    nodes = jnp.asarray(nodes)
    meta = jnp.reshape(member, (1,)).astype(jnp.int32)
    mask = pair_mask
    tile_shape = (tiles, 8, BLOCK)
    kept = (boxes - 1) * 4 * BLOCK * BLOCK * 4 <= TABLE_LIMIT

    half = tiles // 2

    def far_memory(x):
        return pltpu.with_memory_space_constraint(x, pltpu.HBM)

    stat, x0, phi, payload = call(
        functools.partial(first_body, coeff=coeff, box_height=box_height, tiles=tiles, reach=reach),
        [tile_shape, tile_shape, (tiles, BLOCK, BLOCK), (1 + 2 * reach, 8, BLOCK)],
        [meta] + [far_memory(x) for x in (positions, polarizability[None], permanent_field, group_id[None], jnp.asarray(picks))],
        smem=1,
        limit=16 << 20,
        far=5,
        more=[
            pltpu.VMEM((3, atoms), f32),
            pltpu.VMEM((1, atoms), f32),
            pltpu.VMEM((3, atoms), f32),
            pltpu.VMEM((1, atoms), jnp.int32),
            pltpu.VMEM(picks.shape, f32),
            pltpu.SemaphoreType.DMA((5,)),
        ],
    )
    count = own_slots(0, tiles, tiles, reach)
    tab, near_zero, own_list, halo_list = call(
        functools.partial(tensors_body, half=half, tiles=tiles, reach=reach, length_z=length_z),
        [(count, 4, BLOCK, BLOCK), tile_shape],
        [far_memory(mask), stat, x0],
        far=1,
        scratch=[
            (tiles, 8, BLOCK, BLOCK),
            (tiles, 3, BLOCK, BLOCK),
            (tiles, 3, SUB, BLOCK),
            (tiles, 3, SUB, BLOCK),
        ],
        more=[pltpu.SMEM(mask.shape, jnp.int32), pltpu.SemaphoreType.DMA],
        cost=pl.CostEstimate(flops=count * BLOCK * BLOCK * 70, bytes_accessed=1 << 20, transcendentals=count * BLOCK * BLOCK * 2),
        limit=18 << 20,
        pinned=(0,),
        lists=(count - tiles + 2, len(halo_pairs(tiles, reach)) + 1),
    )

    def far_tables(after):
        if not kept:
            return []
        return call(
            functools.partial(far_tensors_body, boxes=boxes, box_height=box_height, length_z=length_z),
            [(BLOCK // SUB, boxes - 1, 4, SUB, BLOCK)],
            [nodes, after],
            scratch=[(4, BLOCK, BLOCK)],
            cost=pl.CostEstimate(flops=boxes * BLOCK * BLOCK * 28, bytes_accessed=1 << 20, transcendentals=boxes * BLOCK * BLOCK),
            pinned=(0,),
        )

    def own_field(v, begin, end, after):
        top = min(end + reach, tiles) - begin
        return call(
            functools.partial(own_body, begin=begin, end=end, tiles=tiles, reach=reach),
            [(top, 8, BLOCK)],
            [own_list, v, tab] + after,
            smem=1,
            scratch=[
                (end - begin, 3, BLOCK, BLOCK),
                (top, 3, SUB, BLOCK),
                (end - begin, 3, BLOCK, BLOCK),
                (top, 3, SUB, BLOCK),
            ],
            cost=pl.CostEstimate(flops=72 * BLOCK * BLOCK * 18, bytes_accessed=1 << 20, transcendentals=0),
        )[0]

    def relay(near, after):
        size = near[0].shape[0] - 1
        return call(
            functools.partial(relay_body, plane=plane, reach=reach),
            [(plane + size, 8, BLOCK)],
            [meta] + near + [after],
            smem=1,
            scratch=[(plane, size, 8, BLOCK)],
        )[0]

    def exchange(payload, v):
        near = swap(payload, ("oct", "sub"), plane)
        first = own_field(v, 0, half, [])
        bundle = relay(near, first)
        bundles = swap(bundle, "blk", rows)
        second = own_field(v, half, tiles, [bundle])
        return [first, second], near, bundles

    def field(mode, v, parts, halo_tab, near, bundles, extra):
        outs = [
            [tile_shape, tile_shape, (1 + reach, 8, BLOCK), (len(halo_pairs(tiles, reach)), 4, BLOCK, BLOCK)],
            [tile_shape, tile_shape, (1 + reach, 8, BLOCK), (SUB, BLOCK)],
            [tile_shape] * 4 + [(8, BLOCK)],
        ][mode]
        return call(
            functools.partial(
                field_body, mode=mode, tiles=tiles, reach=reach, plane=plane, slabs=slabs, box_height=box_height,
                length_z=length_z, surface=surface, kept=kept, half=half,
            ),
            outs,
            [meta, halo_list, nodes, stat, v, phi] + parts + halo_tab + near + bundles + table + extra,
            smem=2,
            pinned=() if mode else (3,),
            scratch=[
                (tiles, 3, SUB, BLOCK),
                (2 * reach, 3 if mode else 8, BLOCK, BLOCK),
                (boxes, 3, SUB, BLOCK),
                (BOXES_DEV, 3, BLOCK, BLOCK),
                (8, BLOCK, BLOCK) if not kept else (1, 8, BLOCK),
                (plane + rows, reach if mode else 2 * reach, 8, BLOCK),
            ],
        )

    near = swap(payload, ("oct", "sub"), plane)
    bundle = relay(near, near_zero)
    bundles = swap(bundle, "blk", rows)
    table = far_tables(bundle)
    r0, u0, payload, halo_tab = field(0, x0, [near_zero], [], near, bundles, [])
    parts, near, bundles = exchange(payload, u0)
    w0, u1, payload, norm = field(1, u0, parts, [halo_tab], near, bundles, [])
    parts, near, bundles = exchange(payload, u1)
    x1, r1, z1, q1, scal = field(2, u1, parts, [halo_tab], near, bundles, [x0, r0, w0, norm])
    sums = swap(scal, ("oct", "sub"), plane)
    sums = swap(functools.reduce(jnp.add, sums), "blk", rows)
    return call(
        functools.partial(last_body, tiles=tiles),
        [(3, atoms), (3, atoms)],
        [scal, stat, r0, w0, x1, r1, z1, q1] + sums,
    )


def solution(mesh):
    split = P(("groups", "blk", "oct", "sub"))
    wide = P(None, ("groups", "blk", "oct", "sub"))
    return jax.shard_map(
        lambda *args: tuple(on_device(*args)),
        mesh=mesh,
        in_specs=(wide, split, wide, split, P(("groups", "blk", "oct", "sub"), None)),
        out_specs=(wide, wide),
        check_vma=False,
    )
```
